256 devices in a mesh: rows: 64 (over z, x, core), cols: 4 (over y).
Axes of the slice: x: 4, y: 4, z: 8, core: 2. Of those that a mesh axis runs over, the one named last changes fastest.
Arguments:
- pass_rates: float32 [32, 1048576], P(None, 'rows'), may hold values from 0 to 1
- upper_blocks: bfloat16 [8192, 8, 128, 128], P('rows', 'cols'), may hold values from 9.9658966e-05 to 0.0099487305
- neighbours: int32 [8192, 8], P('rows', 'cols'), may hold values from 0 to 8191, as said below
Outputs:
- solution: float32 [32, 1048576], P('cols', 'rows')
- residual: float32 [32, 1048576], P('cols', 'rows')
The draws below stay inside these ranges and needn't reach their ends.
Inputs may be any that keep to these rules, and one draw needn't show every extreme that they name: `neighbours`: slot 0 of block-row b names b itself; every other slot of block-row b names a block from b to b + 256 that exists; in the last block-row of every shard of 128 block-rows, slot 1 names the farthest such block.
All inputs are finite; a program needn't handle non-finite values.
Results may differ from the reference program's by a relative error of at most 0.034.
Values may be sent and summed in bfloat16 or wider, within the bound.
A program may use at most 128 MiB of HBM per device.

```python
import math
import jax
import jax.numpy as jnp
from jax import lax

BLOCK = 128
NBR = 8
COLS = 32
REACH = 2
ITERS = 2
BR_DEV = 128
NB = 8192
TRACES = 1048576


def draw_pass_rates(key, part):
    block_key = jax.random.fold_in(key, 11)
    trace_key = jax.random.fold_in(key, 23)
    block_level = jax.random.uniform(block_key, (COLS, NB), jnp.float32)
    block_level = jnp.repeat(block_level, BLOCK, axis=1)
    trace_level = jax.random.uniform(trace_key, (COLS, TRACES), jnp.float32)
    position = jnp.arange(TRACES, dtype=jnp.float32) / max(TRACES - 1, 1)
    rising = (1.0 + 2.0 * position) / 3.0
    mixed = 0.8 * block_level + 0.2 * trace_level
    return mixed * rising[None, :]


def draw_neighbours(key, part):
    block_index = jnp.arange(NB, dtype=jnp.int32)[:, None]
    room_ahead = jnp.minimum(REACH * BR_DEV, NB - 1 - block_index)
    offsets = jax.random.randint(key, (NB, NBR), 0, room_ahead + 1, dtype=jnp.int32)
    slot_index = jnp.arange(NBR, dtype=jnp.int32)[None, :]
    last_row = block_index % BR_DEV == BR_DEV - 1
    offsets = jnp.where(slot_index == 0, 0, jnp.where((slot_index == 1) & last_row, room_ahead, offsets))
    return (block_index + offsets).astype(jnp.int32)


def block_scale(key, extent, shards, least, largest):
    gain = 1.0
    for axis_at, parts in shards:
        draws = jax.random.uniform(jax.random.fold_in(jax.random.fold_in(key, 6), axis_at), (parts,), jnp.float32, least / len(shards), largest / len(shards))
        gain = gain * jnp.repeat(jnp.exp(draws), extent[axis_at] // parts).reshape((-1,) + (1,) * (len(extent) - 1 - axis_at))
    return gain


def setup_inputs(seed: int = 0) -> dict:
    key_list = jax.random.split(jax.random.key(seed), 4)
    pass_rates = draw_pass_rates(jax.random.fold_in(key_list[3], 71), 0)
    upper_blocks = jnp.clip(jnp.exp(math.log(0.0099487305) - 4.603446 * jax.random.uniform(key_list[1], (NB, NBR, BLOCK, BLOCK), jnp.float32) ** block_scale(key_list[1], (NB, NBR, BLOCK, BLOCK), ((0, 64), (1, 4)), -0.2, 0.2)), 9.965896606445312e-05, 0.0099487305).astype(jnp.bfloat16)
    neighbours = draw_neighbours(jax.random.fold_in(key_list[3], 71), 0)
    return dict(pass_rates=pass_rates, upper_blocks=upper_blocks, neighbours=neighbours)


def laplacian(rounded, upper_blocks, neighbours):
    block_rows = upper_blocks.shape[0]
    block_width = upper_blocks.shape[2]
    columns = rounded.shape[0]
    blocked = rounded.reshape(columns, block_rows, block_width)

    def visit(returned, group):
        start = (group * BR_DEV).astype(jnp.int32)
        weights = lax.dynamic_slice_in_dim(upper_blocks, start, BR_DEV, 0).astype(jnp.float32)
        targets = lax.dynamic_slice_in_dim(neighbours, start, BR_DEV, 0)
        own_block = lax.dynamic_slice_in_dim(blocked, start, BR_DEV, 1)
        far_blocks = jnp.take(blocked, targets, axis=1)
        row_weight = jnp.sum(weights, axis=(1, 3))
        col_weight = jnp.sum(weights, axis=2)
        forward = own_block * row_weight[None] - jnp.einsum("gkij,cgkj->cgi", weights, far_blocks, precision=lax.Precision.HIGHEST)
        transposed = col_weight[None] * far_blocks - jnp.einsum("gkij,cgi->cgkj", weights, own_block, precision=lax.Precision.HIGHEST)
        return returned.at[:, targets].add(transposed), forward

    start_field = jnp.zeros((columns, block_rows, block_width), jnp.float32)
    returned, forward = lax.scan(visit, start_field, jnp.arange(block_rows // BR_DEV, dtype=jnp.int32))
    forward = jnp.transpose(forward, (1, 0, 2, 3)).reshape(columns, block_rows * block_width)
    return forward + returned.reshape(columns, block_rows * block_width)


def operator(direction, upper_blocks, neighbours):
    rounded = lax.optimization_barrier(direction.astype(jnp.bfloat16)).astype(jnp.float32)
    return direction + 0.5 * laplacian(rounded, upper_blocks, neighbours)


def reference(pass_rates, upper_blocks, neighbours):
    solution = jnp.zeros_like(pass_rates)
    residual = pass_rates
    direction = pass_rates
    norm_now = jnp.sum(residual * residual, axis=1)
    for iteration in range(ITERS):
        mapped = operator(direction, upper_blocks, neighbours)
        step_size = norm_now / jnp.sum(direction * mapped, axis=1)
        solution = solution + step_size[:, None] * direction
        residual = residual - step_size[:, None] * mapped
        norm_next = jnp.sum(residual * residual, axis=1)
        direction = residual + (norm_next / norm_now)[:, None] * direction
        norm_now = norm_next
    return solution, residual
```

```python
import functools

import jax
import jax.numpy as jnp
from jax import lax
from jax.experimental import pallas as pl
from jax.experimental.pallas import tpu as pltpu
from jax.sharding import PartitionSpec as P

MESH = pl.DeviceIdType.MESH
F32 = jnp.float32
BF16 = jnp.bfloat16
RING = 4
VMEM = pl.BlockSpec(memory_space=pltpu.VMEM)
LIMIT = 48 * 2**20
ONES = 16
STEP_ROWS = 8


def rem(value, count):
    return lax.rem(value, jnp.int32(count))


class Place:
    def __init__(self, shards):
        self.shards = shards
        self.s = lax.axis_index("rows")
        self.y = lax.axis_index("cols")
        self.odd = rem(self.s, 2)
        self.next_y = rem(self.y + 1, RING)
        self.last_y = rem(self.y + RING - 1, RING)
        self.far_y = rem(self.y + 2, RING)
        self.partner = (self.s + 1 - 2 * self.odd, self.y)
        self.ahead = (rem(self.s + 2, shards), self.y)
        self.behind = (rem(self.s + shards - 2, shards), self.y)
        self.right = (self.s, self.next_y)
        self.left = (self.s, self.last_y)

    def around(self, stride, size, step):
        at = rem(self.s // stride, size)
        return (self.s + (rem(at + step, size) - at) * stride, self.y)


def signal_all(devices):
    barrier = pltpu.get_barrier_semaphore()
    for device in devices:
        pl.semaphore_signal(barrier, inc=1, device_id=device, device_id_type=MESH)


def wait_all(devices):
    pl.semaphore_wait(pltpu.get_barrier_semaphore(), len(devices))


def remote(src, dst, send_sem, recv_sem, device):
    return pltpu.make_async_remote_copy(
        src_ref=src, dst_ref=dst, send_sem=send_sem, recv_sem=recv_sem, device_id=device, device_id_type=MESH
    )


class Spread:
    def __init__(self, at, plane, send, recv):
        half = plane.shape[1] // 2
        low, high = pl.ds(0, half), pl.ds(half, half)
        routes = (
            (at.y, low, at.right),
            (at.y, high, at.left),
            (at.y, high, at.right),
            (at.y, low, at.left),
            (at.last_y, low, at.right),
            (at.next_y, high, at.left),
        )
        self.copies = [
            remote(plane.at[chunk, part], plane.at[chunk, part], send.at[i], recv.at[i], device)
            for i, (chunk, part, device) in enumerate(routes)
        ]

    def start(self):
        for copy in self.copies[:4]:
            copy.start()

    def relay(self):
        for first, second in ((0, 4), (1, 5)):
            self.copies[first].wait_recv()
            self.copies[second].start()

    def near(self):
        for i in (2, 3):
            self.copies[i].wait_recv()

    def far(self):
        for i in (4, 5):
            self.copies[i].wait_recv()

    def drain(self):
        for copy in self.copies:
            copy.wait_send()


class Gather:
    def __init__(self, at, window, own, send, recv, x_send, x_recv, p_send, p_recv):
        self.at = at
        self.to_behind = remote(window.at[0, at.y], window.at[2, at.y], x_send, x_recv, at.behind)
        self.planes = [Spread(at, window.at[d], send.at[i], recv.at[i]) for i, d in enumerate((0, 2)) if own or d]
        source = 2 - 2 * at.odd
        self.across = [
            remote(window.at[source, chunk], window.at[1, chunk], p_send.at[i], p_recv.at[i], at.partner)
            for i, chunk in enumerate((at.y, at.last_y, at.next_y, at.far_y))
        ]

    def run(self):
        own, ahead = (self.planes[0] if len(self.planes) > 1 else None), self.planes[-1]
        if own is not None:
            own.start()
            own.relay()
        self.to_behind.wait_recv()
        ahead.start()
        self.across[0].start()
        ahead.relay()
        if own is not None:
            own.near()
        ahead.near()
        self.across[1].start()
        self.across[2].start()
        if own is not None:
            own.far()
        ahead.far()
        self.across[3].start()
        for plane in self.planes:
            plane.drain()
        for copy in self.across:
            copy.wait()
        self.to_behind.wait_send()


def halo_kernel(shards, p_ref, window, send, recv, x_send, x_recv, p_send, p_recv):
    at = Place(shards)
    partners = (at.partner, at.ahead, at.behind, at.right, at.left)
    signal_all(partners)
    blocks, columns, width = window.shape[2:]

    def cast(chunk):
        def one(i, carry):
            first = pl.multiple_of((chunk * blocks + i) * width, width)
            window[0, chunk, i] = p_ref[:, pl.ds(first, width)].astype(BF16)
            return carry

        lax.fori_loop(0, blocks, one, 0)

    gather = Gather(at, window, False, send, recv, x_send, x_recv, p_send, p_recv)
    cast(at.y)
    wait_all(partners)
    gather.to_behind.start()
    for chunk in (at.last_y, at.next_y, at.far_y):
        cast(chunk)
    gather.run()


GATHER_SEMS = [
    pltpu.SemaphoreType.DMA((2, 6)),
    pltpu.SemaphoreType.DMA((2, 6)),
    pltpu.SemaphoreType.DMA,
    pltpu.SemaphoreType.DMA,
    pltpu.SemaphoreType.DMA((4,)),
    pltpu.SemaphoreType.DMA((4,)),
]
REDUCE_SEMS = [
    pltpu.SemaphoreType.DMA((4,)),
    pltpu.SemaphoreType.DMA((4,)),
    pltpu.SemaphoreType.DMA((2, 6)),
    pltpu.SemaphoreType.DMA((2, 6)),
    pltpu.SemaphoreType.DMA,
    pltpu.SemaphoreType.DMA,
]


def reduce_scratch(blocks, sub, width):
    return [
        pltpu.VMEM((RING, blocks, sub, width), BF16),
        pltpu.VMEM((2, RING, blocks, sub, width), BF16),
        pltpu.VMEM((2, 6, blocks // 2, sub, width), BF16),
        pltpu.VMEM((blocks, sub, width), BF16),
        pltpu.VMEM((blocks, sub, width), BF16),
    ] + REDUCE_SEMS


class Reduce:
    def __init__(self, at, part, crossed, total, landed, outgoing, incoming, c_send, c_recv, send, recv, x_send, x_recv):
        self.at, self.part, self.crossed, self.total, self.landed = at, part, crossed, total, landed
        self.outgoing, self.incoming = outgoing, incoming
        self.half = crossed.shape[1] // 2
        half = self.half
        self.order = (at.far_y, at.next_y, at.last_y, at.y)
        self.across = [
            remote(part.at[1, chunk], crossed.at[chunk], c_send.at[i], c_recv.at[i], at.partner)
            for i, chunk in enumerate(self.order)
        ]
        low, high = pl.ds(0, half), pl.ds(half, half)
        routes = (
            (at.far_y, low, at.right),
            (at.far_y, high, at.left),
            (at.next_y, high, at.right),
            (at.last_y, low, at.left),
            (at.next_y, low, at.right),
            (at.last_y, high, at.left),
        )
        self.copies = [
            [
                remote(total.at[j, chunk, part_], landed.at[j, i], send.at[j, i], recv.at[j, i], device)
                for i, (chunk, part_, device) in enumerate(routes)
            ]
            for j in range(2)
        ]
        self.to_ahead = remote(outgoing, incoming, x_send, x_recv, at.ahead)

    def start(self):
        for copy in self.across:
            copy.start()

    def combine(self, index):
        at, chunk = self.at, self.order[index]
        joined = 1 - at.odd
        kept = at.odd
        self.across[index].wait_recv()

        def one(i, carry):
            term = self.part[2 * joined, chunk, i].astype(F32) + self.crossed[chunk, i].astype(F32)
            self.total[joined, chunk, i] = term.astype(BF16)
            self.total[kept, chunk, i] = self.part[2 * kept, chunk, i]
            return carry

        lax.fori_loop(0, 2 * self.half, one, 0)

    def add_landed(self, j, slot, chunk, first):
        def one(i, carry):
            term = self.total[j, chunk, first + i].astype(F32) + self.landed[j, slot, i].astype(F32)
            self.total[j, chunk, first + i] = term.astype(BF16)
            return carry

        lax.fori_loop(0, self.half, one, 0)

    def run(self, finish, fill=None):
        at, half = self.at, self.half
        self.combine(0)
        for j in (1, 0):
            self.copies[j][0].start()
            self.copies[j][1].start()
        self.combine(1)
        for j in (1, 0):
            self.copies[j][2].start()
        self.combine(2)
        for j in (1, 0):
            self.copies[j][3].start()
        self.combine(3)
        if fill is not None:
            fill()
        for j in (1, 0):
            self.copies[j][0].wait_recv()
            self.add_landed(j, 0, at.next_y, 0)
            self.copies[j][4].start()
            self.copies[j][1].wait_recv()
            self.add_landed(j, 1, at.last_y, half)
            self.copies[j][5].start()
        for j in (1, 0):
            for slot in (2, 3, 4, 5):
                self.copies[j][slot].wait_recv()
            if j == 0:
                self.to_ahead.wait_recv()
            for first, slots in ((0, (3, 4)), (half, (2, 5))):

                def one(i, carry, j=j, first=first, slots=slots):
                    value = self.total[j, at.y, first + i].astype(F32)
                    for slot in slots:
                        value += self.landed[j, slot, i].astype(F32)
                    if j == 1:
                        self.outgoing[first + i] = value.astype(BF16)
                    else:
                        value += self.incoming[first + i].astype(F32)
                        finish(first + i, 0.5 * value)
                    return carry

                lax.fori_loop(0, half, one, 0)
            if j == 1:
                self.to_ahead.start()

    def drain(self):
        for copy in self.across:
            copy.wait_send()
        for copies in self.copies:
            for copy in copies:
                copy.wait_send()
        self.to_ahead.wait_send()


def middle_kernel(shards, part, window, *scratch):
    at = Place(shards)
    partners = (at.partner, at.ahead, at.behind, at.right, at.left)
    signal_all(partners)
    wait_all(partners)
    count = 5 + len(REDUCE_SEMS)
    reduce = Reduce(at, part, *scratch[:count])
    reduce.start()

    def keep(i, value):
        window[0, at.y, i] = value.astype(BF16)

    reduce.run(keep)
    gather = Gather(at, window, True, *scratch[count:])
    gather.to_behind.start()
    gather.run()
    reduce.drain()


def last_kernel(shards, groups, part, p_ref, h_ref, x_ref, r_ref, q_ref, sums, *scratch):
    at = Place(shards)
    peers = [at.around(stride, size, step) for stride, size in groups for step in range(1, size)]
    partners = [at.partner, at.ahead, at.behind, at.right, at.left] + peers
    signal_all(partners)
    wait_all(partners)
    count = 5 + len(REDUCE_SEMS)
    reduce = Reduce(at, part, *scratch[:count])
    heard, g_send, g_recv = scratch[count:]
    reduce.start()
    blocks, sub, width = q_ref.shape
    zero = jnp.zeros((sub, width), F32)

    def p_of(i):
        return p_ref[pl.ds(pl.multiple_of(at.y * sub, sub), sub), pl.ds(pl.multiple_of(i * width, width), width)]

    def h_of(i):
        return h_ref[at.y, i].astype(F32)

    def fill():
        def one(i, carry):
            p, h = p_of(i), h_of(i)
            return carry[0] + p * p, carry[1] + p * h, carry[2] + h * h

        for k, value in enumerate(lax.fori_loop(0, blocks, one, (zero, zero, zero))):
            sums[k] = value

    def keep(i, value):
        q_ref[i] = value

    reduce.run(keep, fill)

    def dots(i, carry):
        q = q_ref[i]
        return carry[0] + p_of(i) * q, carry[1] + h_of(i) * q

    for k, value in enumerate(lax.fori_loop(0, blocks, dots, (zero, zero))):
        sums[3 + k] = value
    slot = 0
    sent = []
    for stride, size in groups:
        copies = []
        for step in range(1, size):
            copies.append(
                remote(sums, heard.at[slot], g_send.at[slot], g_recv.at[slot], at.around(stride, size, step))
            )
            slot += 1
        for copy in copies:
            copy.start()
        for copy in copies:
            copy.wait_recv()
        for copy in copies:
            copy.wait_send()
        for k in range(5):
            value = sums[k]
            for i in range(len(copies)):
                value += heard[slot - len(copies) + i, k]
            sums[k] = value
    pp, ph, hh, pq, hq = (
        jnp.broadcast_to(jnp.sum(sums[k], axis=1, keepdims=True), (sub, width)) for k in range(5)
    )
    first = pp / (pp + ph)
    rest = ph / (pp + ph)
    norm = rest * rest * pp - 2.0 * rest * first * ph + first * first * hh
    a = rest + norm / pp
    c = first
    curve = a * a * pp + a * (a - c) * ph - a * c * pq - c * a * ph - c * (a - c) * hh + c * c * hq
    second = norm / curve
    x_p, x_h = first + second * a, second * c
    r_p, r_h, r_q = rest - second * a, first + second * (a - c), second * c

    def out(i, carry):
        at_i = pl.ds(pl.multiple_of(i * width, width), width)
        p, h, q = p_of(i), h_of(i), q_ref[i]
        x_ref[:, at_i] = x_p * p - x_h * h
        r_ref[:, at_i] = r_p * p - r_h * h + r_q * q
        return carry

    lax.fori_loop(0, blocks, out, 0)
    reduce.drain()


def apply_kernel(first, rows, nbr_ref, u_ref, x_ref, *rest):
    if first:
        part, deg, back, along, deg_along = rest
    else:
        deg, part, h_out, back, along = rest
    step = pl.program_id(0)
    columns, width = x_ref.shape[1:]
    base = lax.axis_index("rows") * rows
    window = 3 * rows

    @pl.when(step == 0)
    def _():
        def clear(i, carry):
            back[i] = jnp.zeros((columns, width), F32)
            if first:
                deg[i] = jnp.zeros((8, width), F32)
            return carry

        lax.fori_loop(0, window, clear, 0, unroll=8)

    ones = jnp.ones((ONES, 2 * width), BF16)
    for r in range(u_ref.shape[0]):
        b = step * u_ref.shape[0] + r
        t0, t1 = nbr_ref[2 * b] - base, nbr_ref[2 * b + 1] - base
        pair = jnp.concatenate([u_ref[r, 0], u_ref[r, 1]], axis=1)
        own = x_ref[b]
        far = jnp.concatenate([x_ref[t0], x_ref[t1]], axis=1)
        if first:
            own = jnp.concatenate([own, ones[:, :width]], axis=0)
            far = jnp.concatenate([far, ones], axis=0)
        forward = lax.dot_general(far, pair, (((1,), (1,)), ((), ())), preferred_element_type=F32)
        returned = lax.dot_general(own, pair, (((1,), (0,)), ((), ())), preferred_element_type=F32)
        along[b] = forward[:columns]
        back[t0] += returned[:columns, :width]
        back[t1] += returned[:columns, width:]
        if first:
            deg_along[b] = forward[columns : columns + 8]
            deg[t0] += returned[columns : columns + 8, :width]
            deg[t1] += returned[columns : columns + 8, width:]

    @pl.when(step == pl.num_programs(0) - 1)
    def _():
        def term(i, own):
            weight = deg[i]
            minus = back[i]
            if own:
                minus += along[i]
                if first:
                    weight += deg_along[i]
                    deg[i] = weight
            x = x_ref[i].astype(F32)
            return x, jnp.concatenate([weight] * (columns // 8), axis=0) * x - minus

        for d in range(3):

            def one(i, carry, d=d):
                x, value = term(d * rows + i, d == 0)
                if first:
                    part[d * rows + i] = value.astype(BF16)
                else:
                    for g in range(RING):
                        at = slice(g * (columns // RING), (g + 1) * (columns // RING))
                        part[d, g, i] = value[at].astype(BF16)
                        if d == 0:
                            h_out[g, i] = x[at].astype(BF16)
                return carry

            lax.fori_loop(0, rows, one, 0, unroll=4)


def apply(first, nbr, upper, window, deg=None):
    rows, slots, width, _ = upper.shape
    columns = window.shape[-2]
    step_rows = min(STEP_ROWS, rows)
    whole = lambda shape: pl.BlockSpec(shape, lambda i, n: (0,) * len(shape))
    x = window.reshape(3 * rows, columns, width)
    in_specs = [pl.BlockSpec((step_rows, slots, width, width), lambda i, n: (i, 0, 0, 0)), whole(x.shape)]
    deg_shape = jax.ShapeDtypeStruct((3 * rows, 8, width), F32)
    scratch = [pltpu.VMEM(x.shape, F32), pltpu.VMEM((rows, columns, width), F32)]
    if first:
        out_shape = [jax.ShapeDtypeStruct(x.shape, BF16), deg_shape]
        scratch.append(pltpu.VMEM((rows, 8, width), F32))
        args = (nbr, upper, x)
    else:
        sub = columns // RING
        out_shape = [
            jax.ShapeDtypeStruct((3, RING, rows, sub, width), BF16),
            jax.ShapeDtypeStruct((RING, rows, sub, width), BF16),
        ]
        in_specs.append(whole(deg_shape.shape))
        args = (nbr, upper, x, deg)
    return pl.pallas_call(
        functools.partial(apply_kernel, first, rows),
        out_shape=out_shape,
        grid_spec=pltpu.PrefetchScalarGridSpec(
            num_scalar_prefetch=1,
            grid=(rows // step_rows,),
            in_specs=in_specs,
            out_specs=[whole(o.shape) for o in out_shape],
            scratch_shapes=scratch,
        ),
        compiler_params=pltpu.CompilerParams(dimension_semantics=("arbitrary",), vmem_limit_bytes=LIMIT),
        name="apply_first" if first else "apply_second",
    )(*args)


def talk(body, out_shape, scratch, collective_id, name, *args):
    return pl.pallas_call(
        body,
        out_shape=out_shape,
        in_specs=[VMEM] * len(args),
        out_specs=jax.tree.map(lambda _: VMEM, out_shape),
        scratch_shapes=scratch,
        compiler_params=pltpu.CompilerParams(
            collective_id=collective_id, has_side_effects=True, vmem_limit_bytes=LIMIT
        ),
        name=name,
    )(*args)


def per_device(pass_rates, upper_blocks, neighbours):
    rows, _, width, _ = upper_blocks.shape
    columns = pass_rates.shape[0]
    shards = lax.axis_size("rows")
    if lax.axis_size("cols") != RING or shards % 8:
        raise ValueError("mesh shape")
    quarter, sub = rows // RING, columns // RING
    groups = [(1, 2), (2, 4), (8, shards // 8)]
    messages = sum(size - 1 for _, size in groups)
    nbr = neighbours.reshape(-1)
    window_shape = jax.ShapeDtypeStruct((3, RING, quarter, columns, width), BF16)

    window = talk(
        functools.partial(halo_kernel, shards), window_shape, GATHER_SEMS, 0, "halo", pass_rates
    )
    part, deg = apply(True, nbr, upper_blocks, window)
    window = talk(
        functools.partial(middle_kernel, shards),
        window_shape,
        reduce_scratch(quarter, columns, width) + GATHER_SEMS,
        1,
        "middle",
        part.reshape(window_shape.shape),
    )
    part, h = apply(False, nbr, upper_blocks, window, deg)
    out_shape = jax.ShapeDtypeStruct((sub, rows * width), F32)
    return talk(
        functools.partial(last_kernel, shards, groups),
        (out_shape, out_shape),
        [pltpu.VMEM((rows, sub, width), F32), pltpu.VMEM((5, sub, width), F32)]
        + reduce_scratch(rows, sub, width)
        + [
            pltpu.VMEM((messages, 5, sub, width), F32),
            pltpu.SemaphoreType.DMA((messages,)),
            pltpu.SemaphoreType.DMA((messages,)),
        ],
        2,
        "last",
        part,
        pass_rates,
        h,
    )


def solution(mesh):
    in_specs = (P(None, "rows"), P("rows", "cols", None, None), P("rows", "cols"))
    out_specs = (P("cols", "rows"), P("cols", "rows"))
    return jax.shard_map(per_device, mesh=mesh, in_specs=in_specs, out_specs=out_specs, check_vma=False)
```

```python
import functools

import jax
import jax.numpy as jnp
from jax import lax
from jax.experimental import pallas as pl
from jax.experimental.pallas import tpu as pltpu
from jax.sharding import PartitionSpec as P

MESH = pl.DeviceIdType.MESH
F32 = jnp.float32
BF16 = jnp.bfloat16
RING = 4
VMEM = pl.BlockSpec(memory_space=pltpu.VMEM)
MIB = 2**20
ONES = 16
UNROLL = 8
TRAFFIC = {"halo": 60 * MIB, "middle": 150 * MIB, "last": 120 * MIB}
LIMITS = {"halo": 20 * MIB, "apply": 32 * MIB, "middle": 24 * MIB, "last": 24 * MIB}


def rem(value, count):
    return lax.rem(value, jnp.int32(count))


def loop(count, body, carry=0):
    return lax.fori_loop(0, count, body, carry, unroll=min(UNROLL, count))


class Place:
    def __init__(self, shards):
        self.shards = shards
        self.s = lax.axis_index("rows")
        self.y = lax.axis_index("cols")
        self.odd = rem(self.s, 2)
        self.next_y = rem(self.y + 1, RING)
        self.last_y = rem(self.y + RING - 1, RING)
        self.far_y = rem(self.y + 2, RING)
        self.partner = (self.s + 1 - 2 * self.odd, self.y)
        self.ahead = (rem(self.s + 2, shards), self.y)
        self.behind = (rem(self.s + shards - 2, shards), self.y)
        self.right = (self.s, self.next_y)
        self.left = (self.s, self.last_y)

    def around(self, stride, size, step):
        at = rem(self.s // stride, size)
        return (self.s + (rem(at + step, size) - at) * stride, self.y)


def signal_all(devices):
    barrier = pltpu.get_barrier_semaphore()
    for device in devices:
        pl.semaphore_signal(barrier, inc=1, device_id=device, device_id_type=MESH)


def wait_all(devices):
    pl.semaphore_wait(pltpu.get_barrier_semaphore(), len(devices))


def remote(src, dst, send_sem, recv_sem, device):
    return pltpu.make_async_remote_copy(
        src_ref=src, dst_ref=dst, send_sem=send_sem, recv_sem=recv_sem, device_id=device, device_id_type=MESH
    )


class Spread:
    def __init__(self, at, plane, send, recv):
        half = plane.shape[1] // 2
        low, high = pl.ds(0, half), pl.ds(half, half)
        routes = (
            (at.y, low, at.right),
            (at.y, high, at.left),
            (at.y, high, at.right),
            (at.y, low, at.left),
            (at.last_y, low, at.right),
            (at.next_y, high, at.left),
        )
        self.copies = [
            remote(plane.at[chunk, part], plane.at[chunk, part], send.at[i], recv.at[i], device)
            for i, (chunk, part, device) in enumerate(routes)
        ]

    def start(self):
        for copy in self.copies[:4]:
            copy.start()

    def relay(self):
        for first, second in ((0, 4), (1, 5)):
            self.copies[first].wait_recv()
            self.copies[second].start()

    def near(self):
        for i in (2, 3):
            self.copies[i].wait_recv()

    def far(self):
        for i in (4, 5):
            self.copies[i].wait_recv()

    def drain(self):
        for copy in self.copies:
            copy.wait_send()


class Gather:
    def __init__(self, at, window, own, send, recv, x_send, x_recv, p_send, p_recv):
        self.at = at
        self.to_behind = remote(window.at[0, at.y], window.at[2, at.y], x_send, x_recv, at.behind)
        self.planes = [Spread(at, window.at[d], send.at[i], recv.at[i]) for i, d in enumerate((0, 2)) if own or d]
        source = 2 - 2 * at.odd
        self.across = [
            remote(window.at[source, chunk], window.at[1, chunk], p_send.at[i], p_recv.at[i], at.partner)
            for i, chunk in enumerate((at.y, at.last_y, at.next_y, at.far_y))
        ]

    def run(self):
        own, ahead = (self.planes[0] if len(self.planes) > 1 else None), self.planes[-1]
        if own is not None:
            own.start()
            own.relay()
        self.to_behind.wait_recv()
        ahead.start()
        self.across[0].start()
        ahead.relay()
        if own is not None:
            own.near()
        ahead.near()
        self.across[1].start()
        self.across[2].start()
        if own is not None:
            own.far()
        ahead.far()
        self.across[3].start()
        for plane in self.planes:
            plane.drain()
        for copy in self.across:
            copy.wait()
        self.to_behind.wait_send()


def halo_kernel(shards, p_hbm, u_hbm, window, u_ref, p_ref, p_sem, u_sem, *sems):
    at = Place(shards)
    partners = (at.partner, at.ahead, at.behind, at.right, at.left)
    signal_all(partners)
    blocks, columns, width = window.shape[2:]
    order = (at.y, at.last_y, at.next_y, at.far_y)

    def span(chunk):
        return pl.ds(pl.multiple_of(chunk * (blocks * width), width), blocks * width)

    loads = [
        pltpu.make_async_copy(p_hbm.at[:, span(chunk)], p_ref.at[:, span(chunk)], p_sem.at[i])
        for i, chunk in enumerate(order)
    ]
    for load in loads:
        load.start()
    weights = pltpu.make_async_copy(u_hbm, u_ref, u_sem)
    weights.start()

    def cast(index):
        chunk = order[index]
        loads[index].wait()

        def one(i, carry):
            first = pl.multiple_of((chunk * blocks + i) * width, width)
            window[0, chunk, i] = p_ref[:, pl.ds(first, width)].astype(BF16)
            return carry

        loop(blocks, one)

    gather = Gather(at, window, False, *sems)
    cast(0)
    wait_all(partners)
    gather.to_behind.start()
    for index in (1, 2, 3):
        cast(index)
    gather.run()
    weights.wait()


GATHER_SEMS = [
    pltpu.SemaphoreType.DMA((2, 6)),
    pltpu.SemaphoreType.DMA((2, 6)),
    pltpu.SemaphoreType.DMA,
    pltpu.SemaphoreType.DMA,
    pltpu.SemaphoreType.DMA((4,)),
    pltpu.SemaphoreType.DMA((4,)),
]
REDUCE_SEMS = [
    pltpu.SemaphoreType.DMA((4,)),
    pltpu.SemaphoreType.DMA((4,)),
    pltpu.SemaphoreType.DMA((2, 6)),
    pltpu.SemaphoreType.DMA((2, 6)),
    pltpu.SemaphoreType.DMA,
    pltpu.SemaphoreType.DMA,
]


def reduce_scratch(blocks, sub, width):
    return [
        pltpu.VMEM((RING, blocks, sub, width), BF16),
        pltpu.VMEM((2, RING, blocks, sub, width), BF16),
        pltpu.VMEM((2, 6, blocks // 2, sub, width), BF16),
        pltpu.VMEM((blocks, sub, width), BF16),
        pltpu.VMEM((blocks, sub, width), BF16),
    ] + REDUCE_SEMS


class Reduce:
    def __init__(self, at, part, crossed, total, landed, outgoing, incoming, c_send, c_recv, send, recv, x_send, x_recv):
        self.at, self.part, self.crossed, self.total, self.landed = at, part, crossed, total, landed
        self.outgoing, self.incoming = outgoing, incoming
        self.half = crossed.shape[1] // 2
        half = self.half
        self.order = (at.far_y, at.next_y, at.last_y, at.y)
        self.across = [
            remote(part.at[1, chunk], crossed.at[chunk], c_send.at[i], c_recv.at[i], at.partner)
            for i, chunk in enumerate(self.order)
        ]
        low, high = pl.ds(0, half), pl.ds(half, half)
        routes = (
            (at.far_y, low, at.right),
            (at.far_y, high, at.left),
            (at.next_y, high, at.right),
            (at.last_y, low, at.left),
            (at.next_y, low, at.right),
            (at.last_y, high, at.left),
        )
        self.copies = [
            [
                remote(total.at[j, chunk, part_], landed.at[j, i], send.at[j, i], recv.at[j, i], device)
                for i, (chunk, part_, device) in enumerate(routes)
            ]
            for j in range(2)
        ]
        self.to_ahead = remote(outgoing, incoming, x_send, x_recv, at.ahead)

    def start(self):
        for copy in self.across:
            copy.start()

    def combine(self, index):
        at, chunk = self.at, self.order[index]
        joined = 1 - at.odd
        kept = at.odd
        self.across[index].wait_recv()

        def one(i, carry):
            term = self.part[2 * joined, chunk, i].astype(F32) + self.crossed[chunk, i].astype(F32)
            self.total[joined, chunk, i] = term.astype(BF16)
            self.total[kept, chunk, i] = self.part[2 * kept, chunk, i]
            return carry

        loop(2 * self.half, one)

    def add_landed(self, j, slot, chunk, first):
        def one(i, carry):
            term = self.total[j, chunk, first + i].astype(F32) + self.landed[j, slot, i].astype(F32)
            self.total[j, chunk, first + i] = term.astype(BF16)
            return carry

        loop(self.half, one)

    def run(self, finish, fill=None):
        at, half = self.at, self.half
        self.combine(0)
        for j in (1, 0):
            self.copies[j][0].start()
            self.copies[j][1].start()
        self.combine(1)
        for j in (1, 0):
            self.copies[j][2].start()
        self.combine(2)
        for j in (1, 0):
            self.copies[j][3].start()
        self.combine(3)
        if fill is not None:
            fill()
        for j in (1, 0):
            self.copies[j][0].wait_recv()
            self.add_landed(j, 0, at.next_y, 0)
            self.copies[j][4].start()
            self.copies[j][1].wait_recv()
            self.add_landed(j, 1, at.last_y, half)
            self.copies[j][5].start()
        for j in (1, 0):
            for slot in (2, 3, 4, 5):
                self.copies[j][slot].wait_recv()
            if j == 0:
                self.to_ahead.wait_recv()
            for first, slots in ((0, (3, 4)), (half, (2, 5))):

                def one(i, carry, j=j, first=first, slots=slots):
                    value = self.total[j, at.y, first + i].astype(F32)
                    for slot in slots:
                        value += self.landed[j, slot, i].astype(F32)
                    if j == 1:
                        self.outgoing[first + i] = value.astype(BF16)
                    else:
                        value += self.incoming[first + i].astype(F32)
                        finish(first + i, 0.5 * value)
                    return carry

                loop(half, one)
            if j == 1:
                self.to_ahead.start()

    def drain(self):
        for copy in self.across:
            copy.wait_send()
        for copies in self.copies:
            for copy in copies:
                copy.wait_send()
        self.to_ahead.wait_send()


def middle_kernel(shards, part, window, *scratch):
    at = Place(shards)
    partners = (at.partner, at.ahead, at.behind, at.right, at.left)
    signal_all(partners)
    wait_all(partners)
    count = 5 + len(REDUCE_SEMS)
    reduce = Reduce(at, part, *scratch[:count])
    reduce.start()

    def keep(i, value):
        window[0, at.y, i] = value.astype(BF16)

    reduce.run(keep)
    gather = Gather(at, window, True, *scratch[count:])
    gather.to_behind.start()
    gather.run()
    reduce.drain()


def last_kernel(shards, groups, part, p_ref, h_ref, x_ref, r_ref, q_ref, sums, *scratch):
    at = Place(shards)
    peers = [at.around(stride, size, step) for stride, size in groups for step in range(1, size)]
    partners = [at.partner, at.ahead, at.behind, at.right, at.left] + peers
    signal_all(partners)
    wait_all(partners)
    count = 5 + len(REDUCE_SEMS)
    reduce = Reduce(at, part, *scratch[:count])
    heard, g_send, g_recv = scratch[count:]
    reduce.start()
    blocks, sub, width = q_ref.shape
    zero = jnp.zeros((sub, width), F32)

    def p_of(i):
        return p_ref[pl.ds(pl.multiple_of(at.y * sub, sub), sub), pl.ds(pl.multiple_of(i * width, width), width)]

    def h_of(i):
        return h_ref[at.y, i].astype(F32)

    def fill():
        def one(i, carry):
            p, h = p_of(i), h_of(i)
            return carry[0] + p * p, carry[1] + p * h, carry[2] + h * h

        for k, value in enumerate(loop(blocks, one, (zero, zero, zero))):
            sums[k] = value

    def keep(i, value):
        q_ref[i] = value

    reduce.run(keep, fill)

    def dots(i, carry):
        q = q_ref[i]
        return carry[0] + p_of(i) * q, carry[1] + h_of(i) * q

    for k, value in enumerate(loop(blocks, dots, (zero, zero))):
        sums[3 + k] = value
    lanes = lax.broadcasted_iota(jnp.int32, (sub, width), 1)
    packed = zero
    for k in range(5):
        packed = jnp.where(lanes == k, jnp.sum(sums[k], axis=1, keepdims=True), packed)
    sums[0] = packed
    slot = 0
    for stride, size in groups:
        copies = []
        for step in range(1, size):
            copies.append(
                remote(sums.at[0], heard.at[slot], g_send.at[slot], g_recv.at[slot], at.around(stride, size, step))
            )
            slot += 1
        for copy in copies:
            copy.start()
        for copy in copies:
            copy.wait_recv()
        for copy in copies:
            copy.wait_send()
        packed = sums[0]
        for i in range(slot - len(copies), slot):
            packed += heard[i]
        sums[0] = packed
    packed = sums[0]
    pp, ph, hh, pq, hq = (
        jnp.broadcast_to(
            jnp.sum(jnp.where(lanes == k, packed, 0.0), axis=1, keepdims=True), (sub, width)
        )
        for k in range(5)
    )
    first = pp / (pp + ph)
    rest = ph / (pp + ph)
    norm = rest * rest * pp - 2.0 * rest * first * ph + first * first * hh
    a = rest + norm / pp
    c = first
    curve = a * a * pp + a * (a - c) * ph - a * c * pq - c * a * ph - c * (a - c) * hh + c * c * hq
    second = norm / curve
    x_p, x_h = first + second * a, second * c
    r_p, r_h, r_q = rest - second * a, first + second * (a - c), second * c

    def out(i, carry):
        at_i = pl.ds(pl.multiple_of(i * width, width), width)
        p, h, q = p_of(i), h_of(i), q_ref[i]
        x_ref[:, at_i] = x_p * p - x_h * h
        r_ref[:, at_i] = r_p * p - r_h * h + r_q * q
        return carry

    loop(blocks, out)
    reduce.drain()


def apply_kernel(first, nbr_ref, u_ref, x_ref, *rest):
    if first:
        part, deg, back, along, deg_along = rest
    else:
        deg, part, h_out, back, along = rest
    columns, width = x_ref.shape[1:]
    rows = u_ref.shape[0]
    base = lax.axis_index("rows") * rows
    window = 3 * rows

    def clear(i, carry):
        back[i] = jnp.zeros((columns, width), F32)
        if first:
            deg[i] = jnp.zeros((8, width), F32)
        return carry

    loop(window, clear)
    ones = jnp.ones((ONES, 2 * width), BF16)

    def row(b, carry):
        t0, t1 = nbr_ref[0, b] - base, nbr_ref[1, b] - base
        pair = jnp.concatenate([u_ref[b, 0], u_ref[b, 1]], axis=1)
        own = x_ref[b]
        far = jnp.concatenate([x_ref[t0], x_ref[t1]], axis=1)
        if first:
            own = jnp.concatenate([own, ones[:, :width]], axis=0)
            far = jnp.concatenate([far, ones], axis=0)
        forward = lax.dot_general(far, pair, (((1,), (1,)), ((), ())), preferred_element_type=F32)
        returned = lax.dot_general(own, pair, (((1,), (0,)), ((), ())), preferred_element_type=F32)
        along[b] = forward[:columns]
        back[t0] += returned[:columns, :width]
        back[t1] += returned[:columns, width:]
        if first:
            deg_along[b] = forward[columns : columns + 8]
            deg[t0] += returned[columns : columns + 8, :width]
            deg[t1] += returned[columns : columns + 8, width:]
        return carry

    loop(rows, row)

    def term(i, own):
        weight = deg[i]
        minus = back[i]
        if own:
            minus += along[i]
            if first:
                weight += deg_along[i]
                deg[i] = weight
        x = x_ref[i].astype(F32)
        return x, jnp.concatenate([weight] * (columns // 8), axis=0) * x - minus

    for d in range(3):

        def one(i, carry, d=d):
            x, value = term(d * rows + i, d == 0)
            if first:
                part[d * rows + i] = value.astype(BF16)
            else:
                for g in range(RING):
                    at = slice(g * (columns // RING), (g + 1) * (columns // RING))
                    part[d, g, i] = value[at].astype(BF16)
                    if d == 0:
                        h_out[g, i] = x[at].astype(BF16)
            return carry

        loop(rows, one)


def apply(first, nbr, upper, window, deg=None):
    rows, slots, width, _ = upper.shape
    columns = window.shape[-2]
    x = window.reshape(3 * rows, columns, width)
    deg_shape = jax.ShapeDtypeStruct((3 * rows, 8, width), F32)
    scratch = [pltpu.VMEM(x.shape, F32), pltpu.VMEM((rows, columns, width), F32)]
    if first:
        out_shape = [jax.ShapeDtypeStruct(x.shape, BF16), deg_shape]
        scratch.append(pltpu.VMEM((rows, 8, width), F32))
        args = (nbr, upper, x)
    else:
        sub = columns // RING
        out_shape = [
            jax.ShapeDtypeStruct((3, RING, rows, sub, width), BF16),
            jax.ShapeDtypeStruct((RING, rows, sub, width), BF16),
        ]
        args = (nbr, upper, x, deg)
    return pl.pallas_call(
        functools.partial(apply_kernel, first),
        out_shape=out_shape,
        in_specs=[pl.BlockSpec(memory_space=pltpu.SMEM)] + [VMEM] * (len(args) - 1),
        out_specs=[VMEM] * len(out_shape),
        scratch_shapes=scratch,
        compiler_params=pltpu.CompilerParams(vmem_limit_bytes=LIMITS["apply"]),
        cost_estimate=pl.CostEstimate(
            flops=4 * rows * slots * width * width * columns, transcendentals=0, bytes_accessed=upper.size * 2
        ),
        name="apply_first" if first else "apply_second",
    )(*args)


def talk(body, out_shape, scratch, collective_id, name, *args, in_specs=None):
    return pl.pallas_call(
        body,
        out_shape=out_shape,
        in_specs=in_specs or [VMEM] * len(args),
        out_specs=jax.tree.map(lambda _: VMEM, out_shape),
        scratch_shapes=scratch,
        compiler_params=pltpu.CompilerParams(
            collective_id=collective_id, has_side_effects=True, vmem_limit_bytes=LIMITS[name]
        ),
        cost_estimate=pl.CostEstimate(flops=0, transcendentals=0, bytes_accessed=TRAFFIC[name]),
        name=name,
    )(*args)


def per_device(pass_rates, upper_blocks, neighbours):
    rows, _, width, _ = upper_blocks.shape
    columns = pass_rates.shape[0]
    shards = lax.axis_size("rows")
    if lax.axis_size("cols") != RING or shards % 8:
        raise ValueError("mesh shape")
    quarter, sub = rows // RING, columns // RING
    groups = [(1, 2), (2, 4), (8, shards // 8)]
    messages = sum(size - 1 for _, size in groups)
    nbr = neighbours.T
    window_shape = jax.ShapeDtypeStruct((3, RING, quarter, columns, width), BF16)

    window, upper = talk(
        functools.partial(halo_kernel, shards),
        (window_shape, jax.ShapeDtypeStruct(upper_blocks.shape, BF16)),
        [pltpu.VMEM(pass_rates.shape, F32), pltpu.SemaphoreType.DMA((RING,)), pltpu.SemaphoreType.DMA] + GATHER_SEMS,
        0,
        "halo",
        pltpu.with_memory_space_constraint(pass_rates, pltpu.HBM),
        pltpu.with_memory_space_constraint(upper_blocks, pltpu.HBM),
        in_specs=[pl.BlockSpec(memory_space=pltpu.HBM)] * 2,
    )
    part, deg = apply(True, nbr, upper, window)
    window = talk(
        functools.partial(middle_kernel, shards),
        window_shape,
        reduce_scratch(quarter, columns, width) + GATHER_SEMS,
        1,
        "middle",
        part.reshape(window_shape.shape),
    )
    part, h = apply(False, nbr, upper, window, deg)
    out_shape = jax.ShapeDtypeStruct((sub, rows * width), F32)
    return talk(
        functools.partial(last_kernel, shards, groups),
        (out_shape, out_shape),
        [pltpu.VMEM((rows, sub, width), F32), pltpu.VMEM((5, sub, width), F32)]
        + reduce_scratch(rows, sub, width)
        + [
            pltpu.VMEM((messages, sub, width), F32),
            pltpu.SemaphoreType.DMA((messages,)),
            pltpu.SemaphoreType.DMA((messages,)),
        ],
        2,
        "last",
        part,
        pass_rates,
        h,
    )


def solution(mesh):
    in_specs = (P(None, "rows"), P("rows", "cols", None, None), P("rows", "cols"))
    out_specs = (P("cols", "rows"), P("cols", "rows"))
    return jax.shard_map(per_device, mesh=mesh, in_specs=in_specs, out_specs=out_specs, check_vma=False)
```

```python
import functools

import jax
import jax.numpy as jnp
from jax import lax
from jax.experimental import pallas as pl
from jax.experimental.pallas import tpu as pltpu
from jax.sharding import PartitionSpec as P

MESH = pl.DeviceIdType.MESH
F32 = jnp.float32
BF16 = jnp.bfloat16
RING = 4
VMEM = pl.BlockSpec(memory_space=pltpu.VMEM)
MIB = 2**20
ONES = 16
UNROLL = 8
TRAFFIC = {"halo": 60 * MIB, "middle": 150 * MIB, "last": 120 * MIB}
LIMITS = {"halo": 20 * MIB, "apply": 32 * MIB, "middle": 24 * MIB, "last": 24 * MIB}


def rem(value, count):
    return lax.rem(value, jnp.int32(count))


def loop(count, body, carry=0):
    return lax.fori_loop(0, count, body, carry, unroll=min(UNROLL, count))


class Place:
    def __init__(self, shards):
        self.shards = shards
        self.s = lax.axis_index("rows")
        self.y = lax.axis_index("cols")
        self.odd = rem(self.s, 2)
        self.next_y = rem(self.y + 1, RING)
        self.last_y = rem(self.y + RING - 1, RING)
        self.far_y = rem(self.y + 2, RING)
        self.partner = (self.s + 1 - 2 * self.odd, self.y)
        self.ahead = (rem(self.s + 2, shards), self.y)
        self.behind = (rem(self.s + shards - 2, shards), self.y)
        self.right = (self.s, self.next_y)
        self.left = (self.s, self.last_y)

    def around(self, stride, size, step):
        at = rem(self.s // stride, size)
        return (self.s + (rem(at + step, size) - at) * stride, self.y)


def signal_all(devices):
    barrier = pltpu.get_barrier_semaphore()
    for device in devices:
        pl.semaphore_signal(barrier, inc=1, device_id=device, device_id_type=MESH)


def wait_all(devices):
    pl.semaphore_wait(pltpu.get_barrier_semaphore(), len(devices))


def remote(src, dst, send_sem, recv_sem, device):
    return pltpu.make_async_remote_copy(
        src_ref=src, dst_ref=dst, send_sem=send_sem, recv_sem=recv_sem, device_id=device, device_id_type=MESH
    )


class Spread:
    def __init__(self, at, plane, first, count, send, recv):
        half = count // 2
        low, high = pl.ds(first, half), pl.ds(first + half, half)
        routes = (
            (at.y, low, at.right),
            (at.y, high, at.left),
            (at.y, high, at.right),
            (at.y, low, at.left),
            (at.last_y, low, at.right),
            (at.next_y, high, at.left),
        )
        self.copies = [
            remote(plane.at[chunk, part], plane.at[chunk, part], send.at[i], recv.at[i], device)
            for i, (chunk, part, device) in enumerate(routes)
        ]

    def start(self):
        for copy in self.copies[:4]:
            copy.start()

    def relay(self):
        for first, second in ((0, 4), (1, 5)):
            self.copies[first].wait_recv()
            self.copies[second].start()

    def near(self):
        for i in (2, 3):
            self.copies[i].wait_recv()

    def far(self):
        for i in (4, 5):
            self.copies[i].wait_recv()

    def drain(self):
        for copy in self.copies:
            copy.wait_send()


def gather(at, window, send, recv, low_send, low_recv, high_send, high_recv, c_send, c_recv):
    count = window.shape[2]
    half = count // 2
    low, high = pl.ds(0, half), pl.ds(half, half)
    order = (at.y, at.last_y, at.next_y, at.far_y)
    own_high = Spread(at, window.at[0], half, half, send.at[0], recv.at[0])
    next_low = Spread(at, window.at[2], 0, half, send.at[1], recv.at[1])
    own_low = Spread(at, window.at[0], 0, half, send.at[2], recv.at[2])
    x_low = remote(window.at[0, at.y, low], window.at[2, at.y, low], low_send, low_recv, at.behind)
    x_high = [
        remote(window.at[0, chunk, high], window.at[2, chunk, high], high_send.at[i], high_recv.at[i], at.behind)
        for i, chunk in enumerate(order)
    ]
    source = 2 - 2 * at.odd
    across = [
        [
            remote(
                window.at[source, chunk, part], window.at[1, chunk, part], c_send.at[k, i], c_recv.at[k, i], at.partner
            )
            for i, chunk in enumerate(order)
        ]
        for k, part in enumerate((low, high))
    ]
    x_low.start()
    own_high.start()
    x_high[0].start()
    own_high.relay()
    own_high.near()
    x_high[1].start()
    x_high[2].start()
    x_low.wait_recv()
    next_low.start()
    across[0][0].start()
    own_low.start()
    own_high.far()
    x_high[3].start()
    next_low.relay()
    own_low.relay()
    x_high[0].wait_recv()
    across[1][0].start()
    next_low.near()
    own_low.near()
    across[0][1].start()
    across[0][2].start()
    for i in (1, 2):
        x_high[i].wait_recv()
        across[1][i].start()
    next_low.far()
    own_low.far()
    across[0][3].start()
    x_high[3].wait_recv()
    across[1][3].start()
    for spread in (own_high, next_low, own_low):
        spread.drain()
    x_low.wait_send()
    for copy in x_high:
        copy.wait_send()
    for copy in across[0] + across[1]:
        copy.wait()


def halo_kernel(
    shards, p_hbm, u_hbm, window, u_ref, p_ref, p_sem, u_sem, send, recv, q_send, q_recv, d_send, d_recv, c_send, c_recv
):
    at = Place(shards)
    partners = (at.partner, at.ahead, at.behind, at.right, at.left)
    signal_all(partners)
    blocks, columns, width = window.shape[2:]
    order = (at.y, at.last_y, at.next_y, at.far_y)

    def span(chunk):
        return pl.ds(pl.multiple_of(chunk * (blocks * width), width), blocks * width)

    loads = [
        pltpu.make_async_copy(p_hbm.at[:, span(chunk)], p_ref.at[:, span(chunk)], p_sem.at[i])
        for i, chunk in enumerate(order)
    ]
    for load in loads:
        load.start()
    weights = pltpu.make_async_copy(u_hbm, u_ref, u_sem)
    weights.start()

    def cast(index):
        chunk = order[index]
        loads[index].wait()

        def one(i, carry):
            first = pl.multiple_of((chunk * blocks + i) * width, width)
            window[0, chunk, i] = p_ref[:, pl.ds(first, width)].astype(BF16)
            return carry

        loop(blocks, one)

    quarter = blocks // 4
    parts = [pl.ds(k * quarter, quarter) for k in range(4)]
    pieces = [
        remote(window.at[0, at.y, parts[k]], window.at[2, at.y, parts[k]], q_send.at[k], q_recv.at[k], at.behind)
        for k in range(3)
    ]
    direct = [
        remote(window.at[0, chunk, parts[3]], window.at[2, chunk, parts[3]], d_send.at[i], d_recv.at[i], at.behind)
        for i, chunk in enumerate(order)
    ]
    spreads = [Spread(at, window.at[2], k * quarter, quarter, send.at[k], recv.at[k]) for k in range(3)]
    source = 2 - 2 * at.odd
    across = [
        remote(window.at[source, chunk], window.at[1, chunk], c_send.at[i], c_recv.at[i], at.partner)
        for i, chunk in enumerate(order)
    ]
    cast(0)
    wait_all(partners)
    for piece in pieces:
        piece.start()
    direct[0].start()
    for index in (1, 2, 3):
        cast(index)
        direct[index].start()
    for k in range(3):
        pieces[k].wait_recv()
        spreads[k].start()
        if k:
            spreads[k - 1].relay()
    direct[0].wait_recv()
    across[0].start()
    spreads[2].relay()
    for spread in spreads:
        spread.near()
    for i in (1, 2):
        direct[i].wait_recv()
        across[i].start()
    for spread in spreads:
        spread.far()
    direct[3].wait_recv()
    across[3].start()
    for spread in spreads:
        spread.drain()
    for copy in pieces + direct:
        copy.wait_send()
    for copy in across:
        copy.wait()
    weights.wait()


def pairs(*shapes):
    return [pltpu.SemaphoreType.DMA(shape) for shape in shapes for _ in range(2)]


HALO_SEMS = pairs((3, 6), (3,), (4,), (4,))
GATHER_SEMS = pairs((3, 6), (), (4,), (2, 4))
REDUCE_SEMS = pairs((4,), (3, 6), (4,), ())


def reduce_scratch(blocks, sub, width):
    return [
        pltpu.VMEM((RING, blocks, sub, width), BF16),
        pltpu.VMEM((2, RING, blocks, sub, width), BF16),
        pltpu.VMEM((3, 6, blocks // 4, sub, width), BF16),
        pltpu.VMEM((RING, blocks // 2, sub, width), BF16),
        pltpu.VMEM((blocks // 2, sub, width), BF16),
        pltpu.VMEM((blocks // 2, sub, width), BF16),
    ] + REDUCE_SEMS


class Fold:
    def __init__(self, at, plane, landed, first, count, send, recv):
        self.at, self.plane, self.landed, self.first, self.half = at, plane, landed, first, count // 2
        low, high = pl.ds(first, self.half), pl.ds(first + self.half, self.half)
        routes = (
            (at.far_y, low, at.right),
            (at.far_y, high, at.left),
            (at.next_y, high, at.right),
            (at.last_y, low, at.left),
            (at.next_y, low, at.right),
            (at.last_y, high, at.left),
        )
        self.copies = [
            remote(plane.at[chunk, part], landed.at[i], send.at[i], recv.at[i], device)
            for i, (chunk, part, device) in enumerate(routes)
        ]

    def far(self):
        self.copies[0].start()
        self.copies[1].start()

    def next(self):
        self.copies[2].start()

    def last(self):
        self.copies[3].start()

    def relay(self):
        for slot, chunk, first in ((0, self.at.next_y, self.first), (1, self.at.last_y, self.first + self.half)):
            self.copies[slot].wait_recv()

            def one(i, carry, slot=slot, chunk=chunk, first=first):
                term = self.plane[chunk, first + i].astype(F32) + self.landed[slot, i].astype(F32)
                self.plane[chunk, first + i] = term.astype(BF16)
                return carry

            loop(self.half, one)
            self.copies[slot + 4].start()

    def result(self, take):
        for offset, slots in ((0, (3, 4)), (self.half, (2, 5))):
            for slot in slots:
                self.copies[slot].wait_recv()

            def one(i, carry, offset=offset, slots=slots):
                value = self.plane[self.at.y, self.first + offset + i].astype(F32)
                for slot in slots:
                    value += self.landed[slot, i].astype(F32)
                take(offset + i, value)
                return carry

            loop(self.half, one)

    def drain(self):
        for copy in self.copies:
            copy.wait_send()


def reduce(
    at, finish, fill,
    part, crossed, total, landed, behind, outgoing, incoming,
    c_send, c_recv, send, recv, h_send, h_recv, low_send, low_recv,
):
    half = crossed.shape[1] // 2
    order = (at.far_y, at.next_y, at.last_y, at.y)
    across = [
        remote(part.at[1, chunk], crossed.at[chunk], c_send.at[i], c_recv.at[i], at.partner)
        for i, chunk in enumerate(order)
    ]
    ahead_low = Fold(at, total.at[1], landed.at[0], 0, half, send.at[0], recv.at[0])
    own_low = Fold(at, total.at[0], landed.at[1], 0, half, send.at[1], recv.at[1])
    own_high = Fold(at, total.at[0], landed.at[2], half, half, send.at[2], recv.at[2])
    x_high = [
        remote(total.at[1, chunk, pl.ds(half, half)], behind.at[chunk], h_send.at[i], h_recv.at[i], at.ahead)
        for i, chunk in enumerate(order)
    ]
    x_low = remote(outgoing, incoming, low_send, low_recv, at.ahead)
    for copy in across:
        copy.start()

    def combine(index):
        chunk = order[index]
        joined, kept = 1 - at.odd, at.odd
        across[index].wait_recv()

        def one(i, carry):
            term = part[2 * joined, chunk, i].astype(F32) + crossed[chunk, i].astype(F32)
            total[joined, chunk, i] = term.astype(BF16)
            total[kept, chunk, i] = part[2 * kept, chunk, i]
            return carry

        loop(2 * half, one)
        x_high[index].start()

    def join(index):
        chunk = order[index]
        x_high[index].wait_recv()

        def one(i, carry):
            term = total[0, chunk, half + i].astype(F32) + behind[chunk, i].astype(F32)
            total[0, chunk, half + i] = term.astype(BF16)
            return carry

        loop(half, one)

    combine(0)
    ahead_low.far()
    combine(1)
    ahead_low.next()
    combine(2)
    ahead_low.last()
    own_low.far()
    own_low.next()
    own_low.last()
    combine(3)
    ahead_low.relay()
    join(0)
    own_high.far()
    own_low.relay()

    def send_on(i, value):
        outgoing[i] = value.astype(BF16)

    ahead_low.result(send_on)
    x_low.start()
    join(1)
    own_high.next()
    join(2)
    own_high.last()
    if fill is not None:
        fill()
    join(3)
    own_high.relay()
    x_low.wait_recv()
    own_low.result(lambda i, value: finish(i, 0.5 * (value + incoming[i].astype(F32))))
    own_high.result(lambda i, value: finish(half + i, 0.5 * value))

    def drain():
        for copy in across + x_high + [x_low]:
            copy.wait_send()
        for fold in (ahead_low, own_low, own_high):
            fold.drain()

    return drain


def middle_kernel(shards, part, window, *scratch):
    at = Place(shards)
    partners = (at.partner, at.ahead, at.behind, at.right, at.left)
    signal_all(partners)
    wait_all(partners)

    def keep(i, value):
        window[0, at.y, i] = value.astype(BF16)

    count = 6 + len(REDUCE_SEMS)
    drain = reduce(at, keep, None, part, *scratch[:count])
    gather(at, window, *scratch[count:])
    drain()


def last_kernel(shards, groups, part, p_ref, h_ref, x_ref, r_ref, q_ref, sums, *scratch):
    at = Place(shards)
    peers = [at.around(stride, size, step) for stride, size in groups for step in range(1, size)]
    partners = [at.partner, at.ahead, at.behind, at.right, at.left] + peers
    signal_all(partners)
    wait_all(partners)
    count = 6 + len(REDUCE_SEMS)
    heard, g_send, g_recv = scratch[count:]
    blocks, sub, width = q_ref.shape
    zero = jnp.zeros((sub, width), F32)

    def p_of(i):
        return p_ref[pl.ds(pl.multiple_of(at.y * sub, sub), sub), pl.ds(pl.multiple_of(i * width, width), width)]

    def h_of(i):
        return h_ref[at.y, i].astype(F32)

    def fill():
        def one(i, carry):
            p, h = p_of(i), h_of(i)
            return carry[0] + p * p, carry[1] + p * h, carry[2] + h * h

        for k, value in enumerate(loop(blocks, one, (zero, zero, zero))):
            sums[k] = value

    def keep(i, value):
        q_ref[i] = value

    drain = reduce(at, keep, fill, part, *scratch[:count])

    def dots(i, carry):
        q = q_ref[i]
        return carry[0] + p_of(i) * q, carry[1] + h_of(i) * q

    for k, value in enumerate(loop(blocks, dots, (zero, zero))):
        sums[3 + k] = value
    lanes = lax.broadcasted_iota(jnp.int32, (sub, width), 1)
    packed = zero
    for k in range(5):
        packed = jnp.where(lanes == k, jnp.sum(sums[k], axis=1, keepdims=True), packed)
    sums[0] = packed
    slot = 0
    for stride, size in groups:
        copies = []
        for step in range(1, size):
            copies.append(
                remote(sums.at[0], heard.at[slot], g_send.at[slot], g_recv.at[slot], at.around(stride, size, step))
            )
            slot += 1
        for copy in copies:
            copy.start()
        for copy in copies:
            copy.wait_recv()
        for copy in copies:
            copy.wait_send()
        packed = sums[0]
        for i in range(slot - len(copies), slot):
            packed += heard[i]
        sums[0] = packed
    packed = sums[0]
    pp, ph, hh, pq, hq = (
        jnp.broadcast_to(
            jnp.sum(jnp.where(lanes == k, packed, 0.0), axis=1, keepdims=True), (sub, width)
        )
        for k in range(5)
    )
    first = pp / (pp + ph)
    rest = ph / (pp + ph)
    norm = rest * rest * pp - 2.0 * rest * first * ph + first * first * hh
    a = rest + norm / pp
    c = first
    curve = a * a * pp + a * (a - c) * ph - a * c * pq - c * a * ph - c * (a - c) * hh + c * c * hq
    second = norm / curve
    x_p, x_h = first + second * a, second * c
    r_p, r_h, r_q = rest - second * a, first + second * (a - c), second * c

    def out(i, carry):
        at_i = pl.ds(pl.multiple_of(i * width, width), width)
        p, h, q = p_of(i), h_of(i), q_ref[i]
        x_ref[:, at_i] = x_p * p - x_h * h
        r_ref[:, at_i] = r_p * p - r_h * h + r_q * q
        return carry

    loop(blocks, out)
    drain()


def apply_kernel(first, nbr_ref, u_ref, x_ref, *rest):
    if first:
        part, deg, back, along, deg_along = rest
    else:
        deg, part, h_out, back, along = rest
    columns, width = x_ref.shape[1:]
    rows = u_ref.shape[0]
    base = lax.axis_index("rows") * rows
    window = 3 * rows

    def clear(i, carry):
        back[i] = jnp.zeros((columns, width), F32)
        if first:
            deg[i] = jnp.zeros((8, width), F32)
        return carry

    loop(window, clear)
    ones = jnp.ones((ONES, 2 * width), BF16)

    def row(b, carry):
        t0, t1 = nbr_ref[0, b] - base, nbr_ref[1, b] - base
        pair = jnp.concatenate([u_ref[b, 0], u_ref[b, 1]], axis=1)
        own = x_ref[b]
        far = jnp.concatenate([x_ref[t0], x_ref[t1]], axis=1)
        if first:
            own = jnp.concatenate([own, ones[:, :width]], axis=0)
            far = jnp.concatenate([far, ones], axis=0)
        forward = lax.dot_general(far, pair, (((1,), (1,)), ((), ())), preferred_element_type=F32)
        returned = lax.dot_general(own, pair, (((1,), (0,)), ((), ())), preferred_element_type=F32)
        along[b] = forward[:columns]
        back[t0] += returned[:columns, :width]
        back[t1] += returned[:columns, width:]
        if first:
            deg_along[b] = forward[columns : columns + 8]
            deg[t0] += returned[columns : columns + 8, :width]
            deg[t1] += returned[columns : columns + 8, width:]
        return carry

    loop(rows, row)

    def term(i, own):
        weight = deg[i]
        minus = back[i]
        if own:
            minus += along[i]
            if first:
                weight += deg_along[i]
                deg[i] = weight
        x = x_ref[i].astype(F32)
        return x, jnp.concatenate([weight] * (columns // 8), axis=0) * x - minus

    for d in range(3):

        def one(i, carry, d=d):
            x, value = term(d * rows + i, d == 0)
            if first:
                part[d * rows + i] = value.astype(BF16)
            else:
                for g in range(RING):
                    at = slice(g * (columns // RING), (g + 1) * (columns // RING))
                    part[d, g, i] = value[at].astype(BF16)
                    if d == 0:
                        h_out[g, i] = x[at].astype(BF16)
            return carry

        loop(rows, one)


def apply(first, nbr, upper, window, deg=None):
    rows, slots, width, _ = upper.shape
    columns = window.shape[-2]
    x = window.reshape(3 * rows, columns, width)
    deg_shape = jax.ShapeDtypeStruct((3 * rows, 8, width), F32)
    scratch = [pltpu.VMEM(x.shape, F32), pltpu.VMEM((rows, columns, width), F32)]
    if first:
        out_shape = [jax.ShapeDtypeStruct(x.shape, BF16), deg_shape]
        scratch.append(pltpu.VMEM((rows, 8, width), F32))
        args = (nbr, upper, x)
    else:
        sub = columns // RING
        out_shape = [
            jax.ShapeDtypeStruct((3, RING, rows, sub, width), BF16),
            jax.ShapeDtypeStruct((RING, rows, sub, width), BF16),
        ]
        args = (nbr, upper, x, deg)
    return pl.pallas_call(
        functools.partial(apply_kernel, first),
        out_shape=out_shape,
        in_specs=[pl.BlockSpec(memory_space=pltpu.SMEM)] + [VMEM] * (len(args) - 1),
        out_specs=[VMEM] * len(out_shape),
        scratch_shapes=scratch,
        compiler_params=pltpu.CompilerParams(vmem_limit_bytes=LIMITS["apply"]),
        cost_estimate=pl.CostEstimate(
            flops=4 * rows * slots * width * width * columns, transcendentals=0, bytes_accessed=upper.size * 2
        ),
        name="apply_first" if first else "apply_second",
    )(*args)


def talk(body, out_shape, scratch, collective_id, name, *args, in_specs=None):
    return pl.pallas_call(
        body,
        out_shape=out_shape,
        in_specs=in_specs or [VMEM] * len(args),
        out_specs=jax.tree.map(lambda _: VMEM, out_shape),
        scratch_shapes=scratch,
        compiler_params=pltpu.CompilerParams(
            collective_id=collective_id, has_side_effects=True, vmem_limit_bytes=LIMITS[name]
        ),
        cost_estimate=pl.CostEstimate(flops=0, transcendentals=0, bytes_accessed=TRAFFIC[name]),
        name=name,
    )(*args)


def per_device(pass_rates, upper_blocks, neighbours):
    rows, _, width, _ = upper_blocks.shape
    columns = pass_rates.shape[0]
    shards = lax.axis_size("rows")
    if lax.axis_size("cols") != RING or shards % 8:
        raise ValueError("mesh shape")
    quarter, sub = rows // RING, columns // RING
    groups = [(1, 8), (8, shards // 8)]
    messages = sum(size - 1 for _, size in groups)
    nbr = neighbours.T
    window_shape = jax.ShapeDtypeStruct((3, RING, quarter, columns, width), BF16)

    window, upper = talk(
        functools.partial(halo_kernel, shards),
        (window_shape, jax.ShapeDtypeStruct(upper_blocks.shape, BF16)),
        [pltpu.VMEM(pass_rates.shape, F32), pltpu.SemaphoreType.DMA((RING,)), pltpu.SemaphoreType.DMA] + HALO_SEMS,
        0,
        "halo",
        pltpu.with_memory_space_constraint(pass_rates, pltpu.HBM),
        pltpu.with_memory_space_constraint(upper_blocks, pltpu.HBM),
        in_specs=[pl.BlockSpec(memory_space=pltpu.HBM)] * 2,
    )
    part, deg = apply(True, nbr, upper, window)
    window = talk(
        functools.partial(middle_kernel, shards),
        window_shape,
        reduce_scratch(quarter, columns, width) + GATHER_SEMS,
        1,
        "middle",
        part.reshape(window_shape.shape),
    )
    part, h = apply(False, nbr, upper, window, deg)
    out_shape = jax.ShapeDtypeStruct((sub, rows * width), F32)
    return talk(
        functools.partial(last_kernel, shards, groups),
        (out_shape, out_shape),
        [pltpu.VMEM((rows, sub, width), F32), pltpu.VMEM((5, sub, width), F32)]
        + reduce_scratch(rows, sub, width)
        + [
            pltpu.VMEM((messages, sub, width), F32),
            pltpu.SemaphoreType.DMA((messages,)),
            pltpu.SemaphoreType.DMA((messages,)),
        ],
        2,
        "last",
        part,
        pass_rates,
        h,
    )


def solution(mesh):
    in_specs = (P(None, "rows"), P("rows", "cols", None, None), P("rows", "cols"))
    out_specs = (P("cols", "rows"), P("cols", "rows"))
    return jax.shard_map(per_device, mesh=mesh, in_specs=in_specs, out_specs=out_specs, check_vma=False)
```

```python
import functools

import jax
import jax.numpy as jnp
from jax import lax
from jax.experimental import pallas as pl
from jax.experimental.pallas import tpu as pltpu
from jax.sharding import PartitionSpec as P

MESH = pl.DeviceIdType.MESH
F32 = jnp.float32
BF16 = jnp.bfloat16
RING = 4
VMEM = pl.BlockSpec(memory_space=pltpu.VMEM)
MIB = 2**20
ONES = 16
UNROLL = 8
TRAFFIC = {"halo": 60 * MIB, "middle": 150 * MIB, "last": 120 * MIB}
LIMITS = {"halo": 20 * MIB, "apply": 32 * MIB, "middle": 24 * MIB, "last": 24 * MIB}


def rem(value, count):
    return lax.rem(value, jnp.int32(count))


def loop(count, body, carry=0):
    unroll = max(n for n in range(1, UNROLL + 1) if count % n == 0)
    return lax.fori_loop(0, count, body, carry, unroll=unroll)


def low_of(count):
    return count * 5 // 16 * 2


class Place:
    def __init__(self, shards):
        self.shards = shards
        self.s = lax.axis_index("rows")
        self.y = lax.axis_index("cols")
        self.odd = rem(self.s, 2)
        self.next_y = rem(self.y + 1, RING)
        self.last_y = rem(self.y + RING - 1, RING)
        self.far_y = rem(self.y + 2, RING)
        self.partner = (self.s + 1 - 2 * self.odd, self.y)
        self.ahead = (rem(self.s + 2, shards), self.y)
        self.behind = (rem(self.s + shards - 2, shards), self.y)
        self.right = (self.s, self.next_y)
        self.left = (self.s, self.last_y)

    def around(self, stride, size, step):
        at = rem(self.s // stride, size)
        return (self.s + (rem(at + step, size) - at) * stride, self.y)


def signal_all(devices):
    barrier = pltpu.get_barrier_semaphore()
    for device in devices:
        pl.semaphore_signal(barrier, inc=1, device_id=device, device_id_type=MESH)


def wait_all(devices):
    pl.semaphore_wait(pltpu.get_barrier_semaphore(), len(devices))


def remote(src, dst, send_sem, recv_sem, device):
    return pltpu.make_async_remote_copy(
        src_ref=src, dst_ref=dst, send_sem=send_sem, recv_sem=recv_sem, device_id=device, device_id_type=MESH
    )


class Spread:
    def __init__(self, at, plane, first, count, send, recv):
        half = count // 2
        low, high = pl.ds(first, half), pl.ds(first + half, half)
        routes = (
            (at.y, low, at.right),
            (at.y, high, at.left),
            (at.y, high, at.right),
            (at.y, low, at.left),
            (at.last_y, low, at.right),
            (at.next_y, high, at.left),
        )
        self.copies = [
            remote(plane.at[chunk, part], plane.at[chunk, part], send.at[i], recv.at[i], device)
            for i, (chunk, part, device) in enumerate(routes)
        ]

    def start(self):
        for copy in self.copies[:4]:
            copy.start()

    def relay(self):
        for first, second in ((0, 4), (1, 5)):
            self.copies[first].wait_recv()
            self.copies[second].start()

    def near(self):
        for i in (2, 3):
            self.copies[i].wait_recv()

    def far(self):
        for i in (4, 5):
            self.copies[i].wait_recv()

    def drain(self):
        for copy in self.copies:
            copy.wait_send()


def gather(at, window, send, recv, low_send, low_recv, high_send, high_recv, c_send, c_recv):
    count = window.shape[2]
    split = low_of(count)
    low, high = pl.ds(0, split), pl.ds(split, count - split)
    order = (at.y, at.last_y, at.next_y, at.far_y)
    own_high = Spread(at, window.at[0], split, count - split, send.at[0], recv.at[0])
    next_low = Spread(at, window.at[2], 0, split, send.at[1], recv.at[1])
    own_low = Spread(at, window.at[0], 0, split, send.at[2], recv.at[2])
    x_low = remote(window.at[0, at.y, low], window.at[2, at.y, low], low_send, low_recv, at.behind)
    x_high = [
        remote(window.at[0, chunk, high], window.at[2, chunk, high], high_send.at[i], high_recv.at[i], at.behind)
        for i, chunk in enumerate(order)
    ]
    source = 2 - 2 * at.odd
    across = [
        [
            remote(
                window.at[source, chunk, part], window.at[1, chunk, part], c_send.at[k, i], c_recv.at[k, i], at.partner
            )
            for i, chunk in enumerate(order)
        ]
        for k, part in enumerate((low, high))
    ]
    x_low.start()
    own_high.start()
    own_high.relay()
    x_high[0].start()
    own_high.near()
    x_high[1].start()
    x_high[2].start()
    own_low.start()
    x_low.wait_recv()
    next_low.start()
    across[0][0].start()
    own_high.far()
    x_high[3].start()
    own_low.relay()
    next_low.relay()
    x_high[0].wait_recv()
    across[1][0].start()
    next_low.near()
    own_low.near()
    across[0][1].start()
    across[0][2].start()
    for i in (1, 2):
        x_high[i].wait_recv()
        across[1][i].start()
    next_low.far()
    own_low.far()
    across[0][3].start()
    x_high[3].wait_recv()
    across[1][3].start()
    for spread in (own_high, next_low, own_low):
        spread.drain()
    x_low.wait_send()
    for copy in x_high:
        copy.wait_send()
    for copy in across[0] + across[1]:
        copy.wait()


def halo_kernel(
    shards, p_hbm, u_hbm, window, u_ref, p_ref, p_sem, u_sem, send, recv, q_send, q_recv, d_send, d_recv, c_send, c_recv
):
    at = Place(shards)
    partners = (at.partner, at.ahead, at.behind, at.right, at.left)
    signal_all(partners)
    blocks, columns, width = window.shape[2:]
    order = (at.y, at.last_y, at.next_y, at.far_y)

    def span(chunk):
        return pl.ds(pl.multiple_of(chunk * (blocks * width), width), blocks * width)

    loads = [
        pltpu.make_async_copy(p_hbm.at[:, span(chunk)], p_ref.at[:, span(chunk)], p_sem.at[i])
        for i, chunk in enumerate(order)
    ]
    for load in loads:
        load.start()
    weights = pltpu.make_async_copy(u_hbm, u_ref, u_sem)

    def cast(index):
        chunk = order[index]
        loads[index].wait()

        def one(i, carry):
            first = pl.multiple_of((chunk * blocks + i) * width, width)
            window[0, chunk, i] = p_ref[:, pl.ds(first, width)].astype(BF16)
            return carry

        loop(blocks, one)

    quarter = blocks // 4
    parts = [pl.ds(k * quarter, quarter) for k in range(4)]
    pieces = [
        remote(window.at[0, at.y, parts[k]], window.at[2, at.y, parts[k]], q_send.at[k], q_recv.at[k], at.behind)
        for k in range(3)
    ]
    direct = [
        remote(window.at[0, chunk, parts[3]], window.at[2, chunk, parts[3]], d_send.at[i], d_recv.at[i], at.behind)
        for i, chunk in enumerate(order)
    ]
    spreads = [Spread(at, window.at[2], k * quarter, quarter, send.at[k], recv.at[k]) for k in range(3)]
    source = 2 - 2 * at.odd
    across = [
        remote(window.at[source, chunk], window.at[1, chunk], c_send.at[i], c_recv.at[i], at.partner)
        for i, chunk in enumerate(order)
    ]
    cast(0)
    wait_all(partners)
    for piece in pieces:
        piece.start()
    direct[0].start()
    weights.start()
    for index in (1, 2, 3):
        cast(index)
        direct[index].start()
    for k in range(3):
        pieces[k].wait_recv()
        spreads[k].start()
        if k:
            spreads[k - 1].relay()
    direct[0].wait_recv()
    across[0].start()
    spreads[2].relay()
    for spread in spreads:
        spread.near()
    for i in (1, 2):
        direct[i].wait_recv()
        across[i].start()
    for spread in spreads:
        spread.far()
    direct[3].wait_recv()
    across[3].start()
    for spread in spreads:
        spread.drain()
    for copy in pieces + direct:
        copy.wait_send()
    for copy in across:
        copy.wait()
    weights.wait()


def pairs(*shapes):
    return [pltpu.SemaphoreType.DMA(shape) for shape in shapes for _ in range(2)]


HALO_SEMS = pairs((3, 6), (3,), (4,), (4,))
GATHER_SEMS = pairs((3, 6), (), (4,), (2, 4))
REDUCE_SEMS = pairs((4,), (3, 6), (4,), ())


def reduce_scratch(blocks, sub, width):
    return [
        pltpu.VMEM((RING, blocks, sub, width), BF16),
        pltpu.VMEM((2, RING, blocks, sub, width), BF16),
        pltpu.VMEM((3, 6, low_of(blocks) // 2, sub, width), BF16),
        pltpu.VMEM((RING, blocks - low_of(blocks), sub, width), BF16),
        pltpu.VMEM((low_of(blocks), sub, width), BF16),
        pltpu.VMEM((low_of(blocks), sub, width), BF16),
    ] + REDUCE_SEMS


class Fold:
    def __init__(self, at, plane, landed, first, count, send, recv):
        self.at, self.plane, self.landed, self.first, self.half = at, plane, landed, first, count // 2
        low, high = pl.ds(first, self.half), pl.ds(first + self.half, self.half)
        routes = (
            (at.far_y, low, at.right),
            (at.far_y, high, at.left),
            (at.next_y, high, at.right),
            (at.last_y, low, at.left),
            (at.next_y, low, at.right),
            (at.last_y, high, at.left),
        )
        self.copies = [
            remote(plane.at[chunk, part], landed.at[i, pl.ds(0, self.half)], send.at[i], recv.at[i], device)
            for i, (chunk, part, device) in enumerate(routes)
        ]

    def far(self):
        self.copies[0].start()
        self.copies[1].start()

    def next(self):
        self.copies[2].start()

    def last(self):
        self.copies[3].start()

    def relay(self):
        for slot, chunk, first in ((0, self.at.next_y, self.first), (1, self.at.last_y, self.first + self.half)):
            self.copies[slot].wait_recv()

            def one(i, carry, slot=slot, chunk=chunk, first=first):
                term = self.plane[chunk, first + i].astype(F32) + self.landed[slot, i].astype(F32)
                self.plane[chunk, first + i] = term.astype(BF16)
                return carry

            loop(self.half, one)
            self.copies[slot + 4].start()

    def result(self, take):
        for offset, slots in ((0, (3, 4)), (self.half, (2, 5))):
            for slot in slots:
                self.copies[slot].wait_recv()

            def one(i, carry, offset=offset, slots=slots):
                value = self.plane[self.at.y, self.first + offset + i].astype(F32)
                for slot in slots:
                    value += self.landed[slot, i].astype(F32)
                take(offset + i, value)
                return carry

            loop(self.half, one)

    def drain(self):
        for copy in self.copies:
            copy.wait_send()


def reduce(
    at, finish, beside,
    part, crossed, total, landed, behind, outgoing, incoming,
    c_send, c_recv, send, recv, h_send, h_recv, low_send, low_recv,
):
    count = crossed.shape[1]
    split = low_of(count)
    high = count - split
    order = (at.far_y, at.next_y, at.last_y, at.y)
    across = [
        remote(part.at[1, chunk], crossed.at[chunk], c_send.at[i], c_recv.at[i], at.partner)
        for i, chunk in enumerate(order)
    ]
    ahead_low = Fold(at, total.at[1], landed.at[0], 0, split, send.at[0], recv.at[0])
    own_low = Fold(at, total.at[0], landed.at[1], 0, split, send.at[1], recv.at[1])
    own_high = Fold(at, total.at[0], landed.at[2], split, high, send.at[2], recv.at[2])
    x_high = [
        remote(total.at[1, chunk, pl.ds(split, high)], behind.at[chunk], h_send.at[i], h_recv.at[i], at.ahead)
        for i, chunk in enumerate(order)
    ]
    x_low = remote(outgoing, incoming, low_send, low_recv, at.ahead)
    for copy in across:
        copy.start()

    def combine(index):
        chunk = order[index]
        joined, kept = 1 - at.odd, at.odd
        across[index].wait_recv()

        def one(i, carry):
            term = part[2 * joined, chunk, i].astype(F32) + crossed[chunk, i].astype(F32)
            total[joined, chunk, i] = term.astype(BF16)
            total[kept, chunk, i] = part[2 * kept, chunk, i]
            return carry

        loop(count, one)
        x_high[index].start()

    def join(index):
        chunk = order[index]
        x_high[index].wait_recv()

        def one(i, carry):
            term = total[0, chunk, split + i].astype(F32) + behind[chunk, i].astype(F32)
            total[0, chunk, split + i] = term.astype(BF16)
            return carry

        loop(high, one)

    def send_on(i, value):
        outgoing[i] = value.astype(BF16)

    beside = beside or [lambda: None] * 5
    combine(0)
    ahead_low.far()
    beside[0]()
    combine(1)
    ahead_low.next()
    combine(2)
    ahead_low.last()
    own_low.far()
    own_low.next()
    own_low.last()
    combine(3)
    beside[1]()
    ahead_low.relay()
    join(0)
    own_high.far()
    own_low.relay()
    ahead_low.result(send_on)
    x_low.start()
    beside[2]()
    join(1)
    own_high.next()
    join(2)
    own_high.last()
    beside[3]()
    own_high.relay()
    join(3)
    beside[4]()
    own_high.result(lambda i, value: finish(split + i, 0.5 * value))
    x_low.wait_recv()
    own_low.result(lambda i, value: finish(i, 0.5 * (value + incoming[i].astype(F32))))

    def drain():
        for copy in across + x_high + [x_low]:
            copy.wait_send()
        for fold in (ahead_low, own_low, own_high):
            fold.drain()

    return drain


def middle_kernel(shards, part, window, *scratch):
    at = Place(shards)
    partners = (at.partner, at.ahead, at.behind, at.right, at.left)
    signal_all(partners)
    wait_all(partners)

    def keep(i, value):
        window[0, at.y, i] = value.astype(BF16)

    count = 6 + len(REDUCE_SEMS)
    drain = reduce(at, keep, None, part, *scratch[:count])
    gather(at, window, *scratch[count:])
    drain()


def last_kernel(shards, groups, part, p_ref, h_ref, hq_ref, x_ref, r_ref, sums, heard, s_send, s_recv, *scratch):
    at = Place(shards)
    opposite = (at.s, at.far_y)
    peers = [at.around(stride, size, step) for stride, size in groups for step in range(1, size)]
    partners = [at.partner, at.ahead, at.behind, at.right, at.left, opposite] + peers
    signal_all(partners)
    wait_all(partners)
    _, blocks, sub, width = h_ref.shape
    zero = jnp.zeros((sub, width), F32)
    lanes = lax.broadcasted_iota(jnp.int32, (sub, width), 1)
    rounds = [[(hq_ref.at[y], at_y) for y, at_y in ((at.next_y, at.right), (at.last_y, at.left), (at.far_y, opposite))]]
    rounds += [[(sums, at.around(stride, size, step)) for step in range(1, size)] for stride, size in groups]
    messages = []
    for one_round in rounds:
        first = sum(map(len, messages))
        messages.append(
            [
                remote(source, heard.at[slot], s_send.at[slot], s_recv.at[slot], device)
                for slot, (source, device) in enumerate(one_round, first)
            ]
        )

    def tell(k):
        for message in messages[k]:
            message.start()

    def hear(k):
        for message in messages[k]:
            message.wait_recv()
        for message in messages[k]:
            message.wait_send()
        first = sum(map(len, messages[:k]))
        return sum((heard[slot] for slot in range(first, first + len(messages[k]))), zero)

    def p_of(i):
        return p_ref[pl.ds(pl.multiple_of(at.y * sub, sub), sub), pl.ds(pl.multiple_of(i * width, width), width)]

    def h_of(i):
        return h_ref[at.y, i].astype(F32)

    def square():
        def one(i, carry):
            p, h = p_of(i), h_of(i)
            return carry[0] + p * p, carry[1] + p * h, carry[2] + h * h

        packed = zero
        for k, value in enumerate(loop(blocks, one, (zero, zero, zero))):
            packed = jnp.where(lanes == k, jnp.sum(value, axis=1, keepdims=True), packed)
        sums[...] = packed

    def start_sums():
        value = jnp.sum(hear(0) + hq_ref[at.y], axis=1, keepdims=True)
        sums[...] = jnp.where(lanes == 3, value, sums[...])
        tell(1)

    def pass_sums():
        sums[...] = sums[...] + hear(1)
        tell(2)

    scale = []

    def end_sums():
        packed = sums[...] + hear(2)
        pp, ph, hh, hq = (
            jnp.broadcast_to(jnp.sum(jnp.where(lanes == k, packed, 0.0), axis=1, keepdims=True), (sub, width))
            for k in range(4)
        )
        first = pp / (pp + ph)
        rest = ph / (pp + ph)
        norm = rest * rest * pp - 2.0 * rest * first * ph + first * first * hh
        a = rest + norm / pp
        c = first
        curve = a * a * pp + a * (a - 2.0 * c) * ph + c * (c - 2.0 * a) * hh + c * c * hq
        second = norm / curve
        x_p, x_h = first + second * a, second * c
        scale.extend((rest - second * a, first + second * (a - c), second * c))

        def one(i, carry):
            x_ref[:, pl.ds(pl.multiple_of(i * width, width), width)] = x_p * p_of(i) - x_h * h_of(i)
            return carry

        loop(blocks, one)

    def keep(i, q):
        r_p, r_h, r_q = scale
        r_ref[:, pl.ds(pl.multiple_of(i * width, width), width)] = r_p * p_of(i) - r_h * h_of(i) + r_q * q

    tell(0)
    drain = reduce(at, keep, [square, start_sums, pass_sums, lambda: None, end_sums], part, *scratch)
    drain()


def apply_kernel(first, nbr_ref, u_ref, x_ref, *rest):
    if first:
        part, deg, back, along, deg_along = rest
    else:
        deg, part, h_out, hq_out, back, along = rest
    columns, width = x_ref.shape[1:]
    rows = u_ref.shape[0]
    base = lax.axis_index("rows") * rows
    window = 3 * rows

    def clear(i, carry):
        back[i] = jnp.zeros((columns, width), F32)
        if first:
            deg[i] = jnp.zeros((8, width), F32)
        return carry

    loop(window, clear)
    ones = jnp.ones((ONES, 2 * width), BF16)

    def row(b, carry):
        t0, t1 = nbr_ref[0, b] - base, nbr_ref[1, b] - base
        pair = jnp.concatenate([u_ref[b, 0], u_ref[b, 1]], axis=1)
        own = x_ref[b]
        far = jnp.concatenate([x_ref[t0], x_ref[t1]], axis=1)
        if first:
            own = jnp.concatenate([own, ones[:, :width]], axis=0)
            far = jnp.concatenate([far, ones], axis=0)
        forward = lax.dot_general(far, pair, (((1,), (1,)), ((), ())), preferred_element_type=F32)
        returned = lax.dot_general(own, pair, (((1,), (0,)), ((), ())), preferred_element_type=F32)
        along[b] = forward[:columns]
        back[t0] += returned[:columns, :width]
        back[t1] += returned[:columns, width:]
        if first:
            deg_along[b] = forward[columns : columns + 8]
            deg[t0] += returned[columns : columns + 8, :width]
            deg[t1] += returned[columns : columns + 8, width:]
        return carry

    loop(rows, row)

    def term(i, own):
        weight = deg[i]
        minus = back[i]
        if own:
            minus += along[i]
            if first:
                weight += deg_along[i]
                deg[i] = weight
        x = x_ref[i].astype(F32)
        return x, jnp.concatenate([weight] * (columns // 8), axis=0) * x - minus

    dots = jnp.zeros((columns, width), F32)
    for d in range(3):

        def one(i, carry, d=d):
            x, value = term(d * rows + i, d == 0)
            carry += x * value
            if first:
                part[d * rows + i] = value.astype(BF16)
            else:
                for g in range(RING):
                    at = slice(g * (columns // RING), (g + 1) * (columns // RING))
                    part[d, g, i] = value[at].astype(BF16)
                    if d == 0:
                        h_out[g, i] = x[at].astype(BF16)
            return carry

        dots = loop(rows, one, dots)
    if not first:
        for g in range(RING):
            hq_out[g] = 0.5 * dots[g * (columns // RING) : (g + 1) * (columns // RING)]


def apply(first, nbr, upper, window, deg=None):
    rows, slots, width, _ = upper.shape
    columns = window.shape[-2]
    x = window.reshape(3 * rows, columns, width)
    deg_shape = jax.ShapeDtypeStruct((3 * rows, 8, width), F32)
    scratch = [pltpu.VMEM(x.shape, F32), pltpu.VMEM((rows, columns, width), F32)]
    if first:
        out_shape = [jax.ShapeDtypeStruct(x.shape, BF16), deg_shape]
        scratch.append(pltpu.VMEM((rows, 8, width), F32))
        args = (nbr, upper, x)
    else:
        sub = columns // RING
        out_shape = [
            jax.ShapeDtypeStruct((3, RING, rows, sub, width), BF16),
            jax.ShapeDtypeStruct((RING, rows, sub, width), BF16),
            jax.ShapeDtypeStruct((RING, sub, width), F32),
        ]
        args = (nbr, upper, x, deg)
    return pl.pallas_call(
        functools.partial(apply_kernel, first),
        out_shape=out_shape,
        in_specs=[pl.BlockSpec(memory_space=pltpu.SMEM)] + [VMEM] * (len(args) - 1),
        out_specs=[VMEM] * len(out_shape),
        scratch_shapes=scratch,
        compiler_params=pltpu.CompilerParams(vmem_limit_bytes=LIMITS["apply"]),
        cost_estimate=pl.CostEstimate(
            flops=4 * rows * slots * width * width * columns, transcendentals=0, bytes_accessed=upper.size * 2
        ),
        name="apply_first" if first else "apply_second",
    )(*args)


def talk(body, out_shape, scratch, collective_id, name, *args, in_specs=None):
    return pl.pallas_call(
        body,
        out_shape=out_shape,
        in_specs=in_specs or [VMEM] * len(args),
        out_specs=jax.tree.map(lambda _: VMEM, out_shape),
        scratch_shapes=scratch,
        compiler_params=pltpu.CompilerParams(
            collective_id=collective_id, has_side_effects=True, vmem_limit_bytes=LIMITS[name]
        ),
        cost_estimate=pl.CostEstimate(flops=0, transcendentals=0, bytes_accessed=TRAFFIC[name]),
        name=name,
    )(*args)


def per_device(pass_rates, upper_blocks, neighbours):
    rows, _, width, _ = upper_blocks.shape
    columns = pass_rates.shape[0]
    shards = lax.axis_size("rows")
    if lax.axis_size("cols") != RING or shards % 8:
        raise ValueError("mesh shape")
    quarter, sub = rows // RING, columns // RING
    groups = [(1, 8), (8, shards // 8)]
    messages = RING - 1 + sum(size - 1 for _, size in groups)
    nbr = neighbours.T
    window_shape = jax.ShapeDtypeStruct((3, RING, quarter, columns, width), BF16)

    window, upper = talk(
        functools.partial(halo_kernel, shards),
        (window_shape, jax.ShapeDtypeStruct(upper_blocks.shape, BF16)),
        [pltpu.VMEM(pass_rates.shape, F32), pltpu.SemaphoreType.DMA((RING,)), pltpu.SemaphoreType.DMA] + HALO_SEMS,
        0,
        "halo",
        pltpu.with_memory_space_constraint(pass_rates, pltpu.HBM),
        pltpu.with_memory_space_constraint(upper_blocks, pltpu.HBM),
        in_specs=[pl.BlockSpec(memory_space=pltpu.HBM)] * 2,
    )
    part, deg = apply(True, nbr, upper, window)
    window = talk(
        functools.partial(middle_kernel, shards),
        window_shape,
        reduce_scratch(quarter, columns, width) + GATHER_SEMS,
        1,
        "middle",
        part.reshape(window_shape.shape),
    )
    part, h, hq = apply(False, nbr, upper, window, deg)
    out_shape = jax.ShapeDtypeStruct((sub, rows * width), F32)
    return talk(
        functools.partial(last_kernel, shards, groups),
        (out_shape, out_shape),
        [pltpu.VMEM((sub, width), F32), pltpu.VMEM((messages, sub, width), F32)]
        + pairs((messages,))
        + reduce_scratch(rows, sub, width),
        2,
        "last",
        part,
        pass_rates,
        h,
        hq,
    )


def solution(mesh):
    in_specs = (P(None, "rows"), P("rows", "cols", None, None), P("rows", "cols"))
    out_specs = (P("cols", "rows"), P("cols", "rows"))
    return jax.shard_map(per_device, mesh=mesh, in_specs=in_specs, out_specs=out_specs, check_vma=False)
```

```python
import functools

import jax
import jax.numpy as jnp
from jax import lax
from jax.experimental import pallas as pl
from jax.experimental.pallas import tpu as pltpu
from jax.sharding import PartitionSpec as P

MESH = pl.DeviceIdType.MESH
F32 = jnp.float32
BF16 = jnp.bfloat16
RING = 4
VMEM = pl.BlockSpec(memory_space=pltpu.VMEM)
MIB = 2**20
ONES = 16
UNROLL = 8
ROW_UNROLL = 32
TRAFFIC = {"halo": 60 * MIB, "middle": 150 * MIB, "last": 120 * MIB}
LIMITS = {"halo": 20 * MIB, "apply": 32 * MIB, "middle": 24 * MIB, "last": 24 * MIB}


def rem(value, count):
    return lax.rem(value, jnp.int32(count))


def loop(count, body, carry=0):
    unroll = max(n for n in range(1, UNROLL + 1) if count % n == 0)
    return lax.fori_loop(0, count, body, carry, unroll=unroll)


def nothing():
    pass


def low_of(count):
    return count * 5 // 16 * 2


class Place:
    def __init__(self, shards):
        self.shards = shards
        self.s = lax.axis_index("rows")
        self.y = lax.axis_index("cols")
        self.odd = rem(self.s, 2)
        self.next_y = rem(self.y + 1, RING)
        self.last_y = rem(self.y + RING - 1, RING)
        self.far_y = rem(self.y + 2, RING)
        self.partner = (self.s + 1 - 2 * self.odd, self.y)
        self.ahead = (rem(self.s + 2, shards), self.y)
        self.behind = (rem(self.s + shards - 2, shards), self.y)
        self.right = (self.s, self.next_y)
        self.left = (self.s, self.last_y)

    def around(self, stride, size, step):
        at = rem(self.s // stride, size)
        return (self.s + (rem(at + step, size) - at) * stride, self.y)


def signal_all(devices):
    barrier = pltpu.get_barrier_semaphore()
    for device in devices:
        pl.semaphore_signal(barrier, inc=1, device_id=device, device_id_type=MESH)


def wait_all(devices):
    pl.semaphore_wait(pltpu.get_barrier_semaphore(), len(devices))


def remote(src, dst, send_sem, recv_sem, device):
    return pltpu.make_async_remote_copy(
        src_ref=src, dst_ref=dst, send_sem=send_sem, recv_sem=recv_sem, device_id=device, device_id_type=MESH
    )


class Spread:
    def __init__(self, at, plane, first, count, send, recv):
        half = count // 2
        low, high = pl.ds(first, half), pl.ds(first + half, half)
        routes = (
            (at.y, low, at.right),
            (at.y, high, at.left),
            (at.y, high, at.right),
            (at.y, low, at.left),
            (at.last_y, low, at.right),
            (at.next_y, high, at.left),
        )
        self.copies = [
            remote(plane.at[chunk, part], plane.at[chunk, part], send.at[i], recv.at[i], device)
            for i, (chunk, part, device) in enumerate(routes)
        ]

    def start(self):
        for copy in self.copies[:4]:
            copy.start()

    def relay(self):
        for first, second in ((0, 4), (1, 5)):
            self.copies[first].wait_recv()
            self.copies[second].start()

    def near(self):
        for i in (2, 3):
            self.copies[i].wait_recv()

    def far(self):
        for i in (4, 5):
            self.copies[i].wait_recv()

    def drain(self):
        for copy in self.copies:
            copy.wait_send()


def gather(at, window, send, recv, low_send, low_recv, high_send, high_recv, c_send, c_recv):
    count = window.shape[2]
    split = low_of(count)
    low, high = pl.ds(0, split), pl.ds(split, count - split)
    order = (at.y, at.last_y, at.next_y, at.far_y)
    own_high = Spread(at, window.at[0], split, count - split, send.at[0], recv.at[0])
    next_low = Spread(at, window.at[2], 0, split, send.at[1], recv.at[1])
    own_low = Spread(at, window.at[0], 0, split, send.at[2], recv.at[2])
    x_low = remote(window.at[0, at.y, low], window.at[2, at.y, low], low_send, low_recv, at.behind)
    x_high = [
        remote(window.at[0, chunk, high], window.at[2, chunk, high], high_send.at[i], high_recv.at[i], at.behind)
        for i, chunk in enumerate(order)
    ]
    source = 2 - 2 * at.odd
    across = [
        [
            remote(
                window.at[source, chunk, part], window.at[1, chunk, part], c_send.at[k, i], c_recv.at[k, i], at.partner
            )
            for i, chunk in enumerate(order)
        ]
        for k, part in enumerate((low, high))
    ]
    own_high.start()
    x_high[0].start()
    yield
    x_low.start()
    own_high.relay()
    own_high.near()
    x_high[1].start()
    x_high[2].start()
    own_low.start()
    x_low.wait_recv()
    next_low.start()
    across[0][0].start()
    own_high.far()
    x_high[3].start()
    own_low.relay()
    next_low.relay()
    x_high[0].wait_recv()
    across[1][0].start()
    next_low.near()
    own_low.near()
    across[0][1].start()
    across[0][2].start()
    for i in (1, 2):
        x_high[i].wait_recv()
        across[1][i].start()
    next_low.far()
    own_low.far()
    across[0][3].start()
    x_high[3].wait_recv()
    across[1][3].start()
    for spread in (own_high, next_low, own_low):
        spread.drain()
    x_low.wait_send()
    for copy in x_high:
        copy.wait_send()
    for copy in across[0] + across[1]:
        copy.wait()
    yield


def halo_kernel(
    shards, p_hbm, u_hbm, window, u_ref, p_ref, p_sem, u_sem, send, recv, q_send, q_recv, d_send, d_recv, c_send, c_recv
):
    at = Place(shards)
    partners = (at.partner, at.ahead, at.behind, at.right, at.left)
    signal_all(partners)
    blocks, columns, width = window.shape[2:]
    order = (at.y, at.last_y, at.next_y, at.far_y)

    def span(chunk):
        return pl.ds(pl.multiple_of(chunk * (blocks * width), width), blocks * width)

    loads = [
        pltpu.make_async_copy(p_hbm.at[:, span(chunk)], p_ref.at[:, span(chunk)], p_sem.at[i])
        for i, chunk in enumerate(order)
    ]
    for load in loads:
        load.start()
    weights = pltpu.make_async_copy(u_hbm, u_ref, u_sem)

    def cast(index):
        chunk = order[index]
        loads[index].wait()

        def one(i, carry):
            first = pl.multiple_of((chunk * blocks + i) * width, width)
            window[0, chunk, i] = p_ref[:, pl.ds(first, width)].astype(BF16)
            return carry

        loop(blocks, one)

    split = low_of(blocks)
    piece = split // 2
    parts = [pl.ds(0, piece), pl.ds(piece, piece), pl.ds(split, blocks - split)]
    pieces = [
        remote(window.at[0, at.y, parts[k]], window.at[2, at.y, parts[k]], q_send.at[k], q_recv.at[k], at.behind)
        for k in range(2)
    ]
    direct = [
        remote(window.at[0, chunk, parts[2]], window.at[2, chunk, parts[2]], d_send.at[i], d_recv.at[i], at.behind)
        for i, chunk in enumerate(order)
    ]
    spreads = [Spread(at, window.at[2], k * piece, piece, send.at[k], recv.at[k]) for k in range(2)]
    source = 2 - 2 * at.odd
    across = [
        remote(window.at[source, chunk], window.at[1, chunk], c_send.at[i], c_recv.at[i], at.partner)
        for i, chunk in enumerate(order)
    ]
    cast(0)
    wait_all(partners)
    pieces[0].start()
    pieces[1].start()
    weights.start()
    for index in (1, 2, 3):
        cast(index)
    pieces[0].wait_recv()
    spreads[0].start()
    for copy in direct:
        copy.start()
    pieces[1].wait_recv()
    spreads[1].start()
    spreads[0].relay()
    direct[0].wait_recv()
    across[0].start()
    spreads[1].relay()
    for spread in spreads:
        spread.near()
    for i in (1, 2):
        direct[i].wait_recv()
        across[i].start()
    for spread in spreads:
        spread.far()
    direct[3].wait_recv()
    across[3].start()
    for spread in spreads:
        spread.drain()
    for copy in pieces + direct:
        copy.wait_send()
    for copy in across:
        copy.wait()
    weights.wait()


def pairs(*shapes):
    return [pltpu.SemaphoreType.DMA(shape) for shape in shapes for _ in range(2)]


HALO_SEMS = pairs((2, 6), (2,), (4,), (4,))
GATHER_SEMS = pairs((3, 6), (), (4,), (2, 4))
REDUCE_SEMS = pairs((4,), (3, 6), (4,), ())


def reduce_scratch(blocks, sub, width):
    return [
        pltpu.VMEM((RING, blocks, sub, width), BF16),
        pltpu.VMEM((2, RING, blocks, sub, width), BF16),
        pltpu.VMEM((3, 6, low_of(blocks) // 2, sub, width), BF16),
        pltpu.VMEM((RING, blocks - low_of(blocks), sub, width), BF16),
        pltpu.VMEM((low_of(blocks), sub, width), BF16),
        pltpu.VMEM((low_of(blocks), sub, width), BF16),
    ] + REDUCE_SEMS


class Fold:
    def __init__(self, at, plane, landed, first, count, send, recv):
        self.at, self.plane, self.landed, self.first, self.half = at, plane, landed, first, count // 2
        low, high = pl.ds(first, self.half), pl.ds(first + self.half, self.half)
        routes = (
            (at.far_y, low, at.right),
            (at.far_y, high, at.left),
            (at.next_y, high, at.right),
            (at.last_y, low, at.left),
            (at.next_y, low, at.right),
            (at.last_y, high, at.left),
        )
        self.copies = [
            remote(plane.at[chunk, part], landed.at[i, pl.ds(0, self.half)], send.at[i], recv.at[i], device)
            for i, (chunk, part, device) in enumerate(routes)
        ]

    def far(self):
        self.copies[0].start()
        self.copies[1].start()

    def next(self):
        self.copies[2].start()

    def last(self):
        self.copies[3].start()

    def relay(self):
        for slot, chunk, first in ((0, self.at.next_y, self.first), (1, self.at.last_y, self.first + self.half)):
            self.copies[slot].wait_recv()

            def one(i, carry, slot=slot, chunk=chunk, first=first):
                term = self.plane[chunk, first + i].astype(F32) + self.landed[slot, i].astype(F32)
                self.plane[chunk, first + i] = term.astype(BF16)
                return carry

            loop(self.half, one)
            self.copies[slot + 4].start()

    def result(self, take):
        for offset, slots in ((0, (3, 4)), (self.half, (2, 5))):
            for slot in slots:
                self.copies[slot].wait_recv()

            def one(i, carry, offset=offset, slots=slots):
                value = self.plane[self.at.y, self.first + offset + i].astype(F32)
                for slot in slots:
                    value += self.landed[slot, i].astype(F32)
                take(offset + i, value)
                return carry

            loop(self.half, one)

    def drain(self):
        for copy in self.copies:
            copy.wait_send()


def reduce(
    at, finish, beside,
    part, crossed, total, landed, behind, outgoing, incoming,
    c_send, c_recv, send, recv, h_send, h_recv, low_send, low_recv,
):
    count = crossed.shape[1]
    split = low_of(count)
    high = count - split
    order = (at.far_y, at.next_y, at.last_y, at.y)
    across = [
        remote(part.at[1, chunk], crossed.at[chunk], c_send.at[i], c_recv.at[i], at.partner)
        for i, chunk in enumerate(order)
    ]
    ahead_low = Fold(at, total.at[1], landed.at[0], 0, split, send.at[0], recv.at[0])
    own_low = Fold(at, total.at[0], landed.at[1], 0, split, send.at[1], recv.at[1])
    own_high = Fold(at, total.at[0], landed.at[2], split, high, send.at[2], recv.at[2])
    x_high = [
        remote(total.at[1, chunk, pl.ds(split, high)], behind.at[chunk], h_send.at[i], h_recv.at[i], at.ahead)
        for i, chunk in enumerate(order)
    ]
    x_low = remote(outgoing, incoming, low_send, low_recv, at.ahead)
    for copy in across:
        copy.start()

    def combine(index):
        chunk = order[index]
        joined, kept = 1 - at.odd, at.odd
        across[index].wait_recv()

        def one(i, carry):
            term = part[2 * joined, chunk, i].astype(F32) + crossed[chunk, i].astype(F32)
            total[joined, chunk, i] = term.astype(BF16)
            total[kept, chunk, i] = part[2 * kept, chunk, i]
            return carry

        loop(count, one)
        x_high[index].start()

    def join(index):
        chunk = order[index]
        x_high[index].wait_recv()

        def one(i, carry):
            term = total[0, chunk, split + i].astype(F32) + behind[chunk, i].astype(F32)
            total[0, chunk, split + i] = term.astype(BF16)
            return carry

        loop(high, one)

    def send_on(i, value):
        outgoing[i] = value.astype(BF16)

    combine(0)
    ahead_low.far()
    beside[0]()
    combine(1)
    ahead_low.next()
    combine(2)
    ahead_low.last()
    own_low.far()
    own_low.next()
    own_low.last()
    combine(3)
    beside[1]()
    ahead_low.relay()
    join(0)
    own_high.far()
    own_low.relay()
    ahead_low.result(send_on)
    x_low.start()
    beside[2]()
    join(1)
    own_high.next()
    join(2)
    own_high.last()
    beside[3]()
    own_high.relay()
    join(3)
    beside[4]()
    own_high.result(lambda i, value: finish(split + i, 0.5 * value))
    beside[5]()
    x_low.wait_recv()
    own_low.result(lambda i, value: finish(i, 0.5 * (value + incoming[i].astype(F32))))

    def drain():
        for copy in across + x_high + [x_low]:
            copy.wait_send()
        for fold in (ahead_low, own_low, own_high):
            fold.drain()

    return drain


def middle_kernel(shards, part, window, *scratch):
    at = Place(shards)
    partners = (at.partner, at.ahead, at.behind, at.right, at.left)
    signal_all(partners)
    wait_all(partners)

    def keep(i, value):
        window[0, at.y, i] = value.astype(BF16)

    count = 6 + len(REDUCE_SEMS)
    steps = gather(at, window, *scratch[count:])
    drain = reduce(at, keep, [nothing] * 5 + [lambda: next(steps)], part, *scratch[:count])
    next(steps)
    drain()


def last_kernel(shards, groups, part, p_ref, h_ref, hq_ref, x_ref, r_ref, sums, heard, s_send, s_recv, *scratch):
    at = Place(shards)
    opposite = (at.s, at.far_y)
    peers = [at.around(stride, size, step) for stride, size in groups for step in range(1, size)]
    partners = [at.partner, at.ahead, at.behind, at.right, at.left, opposite] + peers
    signal_all(partners)
    wait_all(partners)
    _, blocks, sub, width = h_ref.shape
    zero = jnp.zeros((sub, width), F32)
    lanes = lax.broadcasted_iota(jnp.int32, (sub, width), 1)
    rounds = [[(hq_ref.at[y], at_y) for y, at_y in ((at.next_y, at.right), (at.last_y, at.left), (at.far_y, opposite))]]
    rounds += [[(sums, at.around(stride, size, step)) for step in range(1, size)] for stride, size in groups]
    messages = []
    for one_round in rounds:
        first = sum(map(len, messages))
        messages.append(
            [
                remote(source, heard.at[slot], s_send.at[slot], s_recv.at[slot], device)
                for slot, (source, device) in enumerate(one_round, first)
            ]
        )

    def tell(k):
        for message in messages[k]:
            message.start()

    def hear(k):
        for message in messages[k]:
            message.wait_recv()
        for message in messages[k]:
            message.wait_send()
        first = sum(map(len, messages[:k]))
        return sum((heard[slot] for slot in range(first, first + len(messages[k]))), zero)

    def p_of(i):
        return p_ref[pl.ds(pl.multiple_of(at.y * sub, sub), sub), pl.ds(pl.multiple_of(i * width, width), width)]

    def h_of(i):
        return h_ref[at.y, i].astype(F32)

    def square():
        def one(i, carry):
            p, h = p_of(i), h_of(i)
            return carry[0] + p * p, carry[1] + p * h, carry[2] + h * h

        packed = zero
        for k, value in enumerate(loop(blocks, one, (zero, zero, zero))):
            packed = jnp.where(lanes == k, jnp.sum(value, axis=1, keepdims=True), packed)
        sums[...] = packed

    def start_sums():
        value = jnp.sum(hear(0) + hq_ref[at.y], axis=1, keepdims=True)
        sums[...] = jnp.where(lanes == 3, value, sums[...])
        tell(1)

    def pass_sums():
        sums[...] = sums[...] + hear(1)
        tell(2)

    scale = []

    def end_sums():
        packed = sums[...] + hear(2)
        pp, ph, hh, hq = (
            jnp.broadcast_to(jnp.sum(jnp.where(lanes == k, packed, 0.0), axis=1, keepdims=True), (sub, width))
            for k in range(4)
        )
        first = pp / (pp + ph)
        rest = ph / (pp + ph)
        norm = rest * rest * pp - 2.0 * rest * first * ph + first * first * hh
        a = rest + norm / pp
        c = first
        curve = a * a * pp + a * (a - 2.0 * c) * ph + c * (c - 2.0 * a) * hh + c * c * hq
        second = norm / curve
        x_p, x_h = first + second * a, second * c
        scale.extend((rest - second * a, first + second * (a - c), second * c))

        def one(i, carry):
            x_ref[:, pl.ds(pl.multiple_of(i * width, width), width)] = x_p * p_of(i) - x_h * h_of(i)
            return carry

        loop(blocks, one)

    def keep(i, q):
        r_p, r_h, r_q = scale
        r_ref[:, pl.ds(pl.multiple_of(i * width, width), width)] = r_p * p_of(i) - r_h * h_of(i) + r_q * q

    tell(0)
    drain = reduce(at, keep, [square, start_sums, pass_sums, nothing, end_sums, nothing], part, *scratch)
    drain()


def apply_kernel(first, nbr_ref, u_ref, x_ref, *rest):
    if first:
        part, deg, back, along, deg_along = rest
    else:
        deg, part, h_out, hq_out, back, along = rest
    columns, width = x_ref.shape[1:]
    rows = u_ref.shape[0]
    base = lax.axis_index("rows") * rows
    window = 3 * rows

    def clear(i, carry):
        back[i] = jnp.zeros((columns, width), F32)
        if first:
            deg[i] = jnp.zeros((8, width), F32)
        return carry

    loop(window, clear)
    ones = jnp.ones((ONES, 2 * width), BF16)

    def row(b, carry):
        t0, t1 = nbr_ref[0, b] - base, nbr_ref[1, b] - base
        pair = jnp.concatenate([u_ref[b, 0], u_ref[b, 1]], axis=1)
        own = x_ref[b]
        far = jnp.concatenate([x_ref[t0], x_ref[t1]], axis=1)
        if first:
            own = jnp.concatenate([own, ones[:, :width]], axis=0)
            far = jnp.concatenate([far, ones], axis=0)
        forward = lax.dot_general(far, pair, (((1,), (1,)), ((), ())), preferred_element_type=F32)
        returned = lax.dot_general(own, pair, (((1,), (0,)), ((), ())), preferred_element_type=F32)
        along[b] = forward[:columns]
        back[t0] += returned[:columns, :width]
        back[t1] += returned[:columns, width:]
        if first:
            deg_along[b] = forward[columns : columns + 8]
            deg[t0] += returned[columns : columns + 8, :width]
            deg[t1] += returned[columns : columns + 8, width:]
        return carry

    lax.fori_loop(0, rows, row, 0, unroll=min(ROW_UNROLL, rows))

    def term(i, own):
        weight = deg[i]
        minus = back[i]
        if own:
            minus += along[i]
            if first:
                weight += deg_along[i]
                deg[i] = weight
        x = x_ref[i].astype(F32)
        return x, jnp.concatenate([weight] * (columns // 8), axis=0) * x - minus

    dots = jnp.zeros((columns, width), F32)
    for d in range(3):

        def one(i, carry, d=d):
            x, value = term(d * rows + i, d == 0)
            carry += x * value
            if first:
                part[d * rows + i] = value.astype(BF16)
            else:
                for g in range(RING):
                    at = slice(g * (columns // RING), (g + 1) * (columns // RING))
                    part[d, g, i] = value[at].astype(BF16)
                    if d == 0:
                        h_out[g, i] = x[at].astype(BF16)
            return carry

        dots = loop(rows, one, dots)
    if not first:
        for g in range(RING):
            hq_out[g] = 0.5 * dots[g * (columns // RING) : (g + 1) * (columns // RING)]


def apply(first, nbr, upper, window, deg=None):
    rows, slots, width, _ = upper.shape
    columns = window.shape[-2]
    x = window.reshape(3 * rows, columns, width)
    deg_shape = jax.ShapeDtypeStruct((3 * rows, 8, width), F32)
    scratch = [pltpu.VMEM(x.shape, F32), pltpu.VMEM((rows, columns, width), F32)]
    if first:
        out_shape = [jax.ShapeDtypeStruct(x.shape, BF16), deg_shape]
        scratch.append(pltpu.VMEM((rows, 8, width), F32))
        args = (nbr, upper, x)
    else:
        sub = columns // RING
        out_shape = [
            jax.ShapeDtypeStruct((3, RING, rows, sub, width), BF16),
            jax.ShapeDtypeStruct((RING, rows, sub, width), BF16),
            jax.ShapeDtypeStruct((RING, sub, width), F32),
        ]
        args = (nbr, upper, x, deg)
    return pl.pallas_call(
        functools.partial(apply_kernel, first),
        out_shape=out_shape,
        in_specs=[pl.BlockSpec(memory_space=pltpu.SMEM)] + [VMEM] * (len(args) - 1),
        out_specs=[VMEM] * len(out_shape),
        scratch_shapes=scratch,
        compiler_params=pltpu.CompilerParams(vmem_limit_bytes=LIMITS["apply"]),
        cost_estimate=pl.CostEstimate(
            flops=4 * rows * slots * width * width * columns, transcendentals=0, bytes_accessed=upper.size * 2
        ),
        name="apply_first" if first else "apply_second",
    )(*args)


def talk(body, out_shape, scratch, collective_id, name, *args, in_specs=None):
    return pl.pallas_call(
        body,
        out_shape=out_shape,
        in_specs=in_specs or [VMEM] * len(args),
        out_specs=jax.tree.map(lambda _: VMEM, out_shape),
        scratch_shapes=scratch,
        compiler_params=pltpu.CompilerParams(
            collective_id=collective_id, has_side_effects=True, vmem_limit_bytes=LIMITS[name]
        ),
        cost_estimate=pl.CostEstimate(flops=0, transcendentals=0, bytes_accessed=TRAFFIC[name]),
        name=name,
    )(*args)


def per_device(pass_rates, upper_blocks, neighbours):
    rows, _, width, _ = upper_blocks.shape
    columns = pass_rates.shape[0]
    shards = lax.axis_size("rows")
    if lax.axis_size("cols") != RING or shards % 8:
        raise ValueError("mesh shape")
    quarter, sub = rows // RING, columns // RING
    groups = [(1, 8), (8, shards // 8)]
    messages = RING - 1 + sum(size - 1 for _, size in groups)
    nbr = neighbours.T
    window_shape = jax.ShapeDtypeStruct((3, RING, quarter, columns, width), BF16)

    window, upper = talk(
        functools.partial(halo_kernel, shards),
        (window_shape, jax.ShapeDtypeStruct(upper_blocks.shape, BF16)),
        [pltpu.VMEM(pass_rates.shape, F32), pltpu.SemaphoreType.DMA((RING,)), pltpu.SemaphoreType.DMA] + HALO_SEMS,
        0,
        "halo",
        pltpu.with_memory_space_constraint(pass_rates, pltpu.HBM),
        pltpu.with_memory_space_constraint(upper_blocks, pltpu.HBM),
        in_specs=[pl.BlockSpec(memory_space=pltpu.HBM)] * 2,
    )
    part, deg = apply(True, nbr, upper, window)
    window = talk(
        functools.partial(middle_kernel, shards),
        window_shape,
        reduce_scratch(quarter, columns, width) + GATHER_SEMS,
        1,
        "middle",
        part.reshape(window_shape.shape),
    )
    part, h, hq = apply(False, nbr, upper, window, deg)
    out_shape = jax.ShapeDtypeStruct((sub, rows * width), F32)
    return talk(
        functools.partial(last_kernel, shards, groups),
        (out_shape, out_shape),
        [pltpu.VMEM((sub, width), F32), pltpu.VMEM((messages, sub, width), F32)]
        + pairs((messages,))
        + reduce_scratch(rows, sub, width),
        2,
        "last",
        part,
        pass_rates,
        h,
        hq,
    )


def solution(mesh):
    in_specs = (P(None, "rows"), P("rows", "cols", None, None), P("rows", "cols"))
    out_specs = (P("cols", "rows"), P("cols", "rows"))
    return jax.shard_map(per_device, mesh=mesh, in_specs=in_specs, out_specs=out_specs, check_vma=False)
```

```python
import functools

import jax
import jax.numpy as jnp
from jax import lax
from jax.experimental import pallas as pl
from jax.experimental.pallas import tpu as pltpu
from jax.sharding import PartitionSpec as P

MESH = pl.DeviceIdType.MESH
F32 = jnp.float32
BF16 = jnp.bfloat16
RING = 4
VMEM = pl.BlockSpec(memory_space=pltpu.VMEM)
MIB = 2**20
ONES = 16
UNROLL = 8
ROW_UNROLL = 32
TRAFFIC = {"halo": 60 * MIB, "middle": 150 * MIB, "last": 120 * MIB}
LIMITS = {"halo": 20 * MIB, "apply": 32 * MIB, "middle": 24 * MIB, "last": 24 * MIB}


def rem(value, count):
    return lax.rem(value, jnp.int32(count))


def loop(count, body, carry=0):
    unroll = max(n for n in range(1, UNROLL + 1) if count % n == 0)
    return lax.fori_loop(0, count, body, carry, unroll=unroll)


def nothing():
    pass


def low_of(count):
    return count * 5 // 16 * 2


class Place:
    def __init__(self, shards):
        self.shards = shards
        self.s = lax.axis_index("rows")
        self.y = lax.axis_index("cols")
        self.odd = rem(self.s, 2)
        self.next_y = rem(self.y + 1, RING)
        self.last_y = rem(self.y + RING - 1, RING)
        self.far_y = rem(self.y + 2, RING)
        self.partner = (self.s + 1 - 2 * self.odd, self.y)
        self.ahead = (rem(self.s + 2, shards), self.y)
        self.behind = (rem(self.s + shards - 2, shards), self.y)
        self.right = (self.s, self.next_y)
        self.left = (self.s, self.last_y)

    def around(self, stride, size, step):
        at = rem(self.s // stride, size)
        return (self.s + (rem(at + step, size) - at) * stride, self.y)


def signal_all(devices):
    barrier = pltpu.get_barrier_semaphore()
    for device in devices:
        pl.semaphore_signal(barrier, inc=1, device_id=device, device_id_type=MESH)


def wait_all(devices):
    pl.semaphore_wait(pltpu.get_barrier_semaphore(), len(devices))


def remote(src, dst, send_sem, recv_sem, device):
    return pltpu.make_async_remote_copy(
        src_ref=src, dst_ref=dst, send_sem=send_sem, recv_sem=recv_sem, device_id=device, device_id_type=MESH
    )


class Spread:
    def __init__(self, at, plane, first, count, send, recv):
        half = count // 2
        low, high = pl.ds(first, half), pl.ds(first + half, half)
        routes = (
            (at.y, low, at.right),
            (at.y, high, at.left),
            (at.y, high, at.right),
            (at.y, low, at.left),
            (at.last_y, low, at.right),
            (at.next_y, high, at.left),
        )
        self.copies = [
            remote(plane.at[chunk, part], plane.at[chunk, part], send.at[i], recv.at[i], device)
            for i, (chunk, part, device) in enumerate(routes)
        ]

    def start(self):
        for copy in self.copies[:4]:
            copy.start()

    def relay(self):
        for first, second in ((0, 4), (1, 5)):
            self.copies[first].wait_recv()
            self.copies[second].start()

    def near(self):
        for i in (2, 3):
            self.copies[i].wait_recv()

    def far(self):
        for i in (4, 5):
            self.copies[i].wait_recv()

    def drain(self):
        for copy in self.copies:
            copy.wait_send()


def gather(at, window, send, recv, low_send, low_recv, high_send, high_recv, c_send, c_recv):
    count = window.shape[2]
    split = low_of(count)
    low, high = pl.ds(0, split), pl.ds(split, count - split)
    order = (at.y, at.last_y, at.next_y, at.far_y)
    own_high = Spread(at, window.at[0], split, count - split, send.at[0], recv.at[0])
    next_low = Spread(at, window.at[2], 0, split, send.at[1], recv.at[1])
    own_low = Spread(at, window.at[0], 0, split, send.at[2], recv.at[2])
    x_low = remote(window.at[0, at.y, low], window.at[2, at.y, low], low_send, low_recv, at.behind)
    x_high = [
        remote(window.at[0, chunk, high], window.at[2, chunk, high], high_send.at[i], high_recv.at[i], at.behind)
        for i, chunk in enumerate(order)
    ]
    source = 2 - 2 * at.odd
    across = [
        [
            remote(
                window.at[source, chunk, part], window.at[1, chunk, part], c_send.at[k, i], c_recv.at[k, i], at.partner
            )
            for i, chunk in enumerate(order)
        ]
        for k, part in enumerate((low, high))
    ]
    own_high.start()
    x_high[0].start()
    yield
    x_low.start()
    own_high.relay()
    own_high.near()
    x_high[1].start()
    x_high[2].start()
    own_low.start()
    x_low.wait_recv()
    next_low.start()
    across[0][0].start()
    own_high.far()
    x_high[3].start()
    own_low.relay()
    next_low.relay()
    x_high[0].wait_recv()
    across[1][0].start()
    next_low.near()
    own_low.near()
    across[0][1].start()
    across[0][2].start()
    for i in (1, 2):
        x_high[i].wait_recv()
        across[1][i].start()
    next_low.far()
    own_low.far()
    across[0][3].start()
    x_high[3].wait_recv()
    across[1][3].start()
    for spread in (own_high, next_low, own_low):
        spread.drain()
    x_low.wait_send()
    for copy in x_high:
        copy.wait_send()
    for copy in across[0] + across[1]:
        copy.wait()
    yield


def halo_kernel(
    shards, p_hbm, u_hbm, window, u_ref, p_ref, p_sem, u_sem, send, recv, q_send, q_recv, d_send, d_recv, c_send, c_recv
):
    at = Place(shards)
    partners = (at.partner, at.ahead, at.behind, at.right, at.left)
    signal_all(partners)
    blocks, columns, width = window.shape[2:]
    order = (at.y, at.last_y, at.next_y, at.far_y)

    def span(chunk):
        return pl.ds(pl.multiple_of(chunk * (blocks * width), width), blocks * width)

    loads = [
        pltpu.make_async_copy(p_hbm.at[:, span(chunk)], p_ref.at[:, span(chunk)], p_sem.at[i])
        for i, chunk in enumerate(order)
    ]
    for load in loads:
        load.start()
    weights = pltpu.make_async_copy(u_hbm, u_ref, u_sem)

    def cast(index):
        chunk = order[index]
        loads[index].wait()

        def one(i, carry):
            first = pl.multiple_of((chunk * blocks + i) * width, width)
            window[0, chunk, i] = p_ref[:, pl.ds(first, width)].astype(BF16)
            return carry

        loop(blocks, one)

    split = low_of(blocks)
    piece = split // 2
    parts = [pl.ds(0, piece), pl.ds(piece, piece), pl.ds(split, blocks - split)]
    pieces = [
        remote(window.at[0, at.y, parts[k]], window.at[2, at.y, parts[k]], q_send.at[k], q_recv.at[k], at.behind)
        for k in range(2)
    ]
    direct = [
        remote(window.at[0, chunk, parts[2]], window.at[2, chunk, parts[2]], d_send.at[i], d_recv.at[i], at.behind)
        for i, chunk in enumerate(order)
    ]
    spreads = [Spread(at, window.at[2], k * piece, piece, send.at[k], recv.at[k]) for k in range(2)]
    source = 2 - 2 * at.odd
    across = [
        remote(window.at[source, chunk], window.at[1, chunk], c_send.at[i], c_recv.at[i], at.partner)
        for i, chunk in enumerate(order)
    ]
    cast(0)
    wait_all(partners)
    pieces[0].start()
    pieces[1].start()
    weights.start()
    for index in (1, 2, 3):
        cast(index)
    pieces[0].wait_recv()
    spreads[0].start()
    for copy in direct:
        copy.start()
    pieces[1].wait_recv()
    spreads[1].start()
    spreads[0].relay()
    direct[0].wait_recv()
    across[0].start()
    spreads[1].relay()
    for spread in spreads:
        spread.near()
    for i in (1, 2):
        direct[i].wait_recv()
        across[i].start()
    for spread in spreads:
        spread.far()
    direct[3].wait_recv()
    across[3].start()
    for spread in spreads:
        spread.drain()
    for copy in pieces + direct:
        copy.wait_send()
    for copy in across:
        copy.wait()
    weights.wait()


def pairs(*shapes):
    return [pltpu.SemaphoreType.DMA(shape) for shape in shapes for _ in range(2)]


HALO_SEMS = pairs((2, 6), (2,), (4,), (4,))
GATHER_SEMS = pairs((3, 6), (), (4,), (2, 4))
REDUCE_SEMS = pairs((4,), (3, 6), (4,), ())


def reduce_scratch(blocks, sub, width):
    return [
        pltpu.VMEM((RING, blocks, sub, width), BF16),
        pltpu.VMEM((2, RING, blocks, sub, width), BF16),
        pltpu.VMEM((3, 6, low_of(blocks) // 2, sub, width), BF16),
        pltpu.VMEM((RING, blocks - low_of(blocks), sub, width), BF16),
        pltpu.VMEM((low_of(blocks), sub, width), BF16),
        pltpu.VMEM((low_of(blocks), sub, width), BF16),
    ] + REDUCE_SEMS


class Fold:
    def __init__(self, at, plane, whole, landed, first, count, send, recv):
        self.at, self.plane, self.landed, self.first, self.half = at, plane, landed, first, count // 2
        low, high = pl.ds(first, self.half), pl.ds(first + self.half, self.half)
        routes = (
            (at.far_y, low, at.right),
            (at.far_y, high, at.left),
            (at.next_y, high, at.right),
            (at.last_y, low, at.left),
            (at.next_y, low, at.right),
            (at.last_y, high, at.left),
        )
        self.copies, self.soon = (
            [
                remote(source.at[chunk, part], landed.at[i, pl.ds(0, self.half)], send.at[i], recv.at[i], device)
                for i, (chunk, part, device) in enumerate(routes[:most])
            ]
            for source, most in ((plane, 6), (whole, 4 if whole is not None else 0))
        )

    def far(self):
        self.copies[0].start()
        self.copies[1].start()

    def next(self):
        self.copies[2].start()

    def last(self):
        self.copies[3].start()

    def begin(self):
        for copy in self.soon:
            copy.start()

    def relay(self):
        for slot, chunk, first in ((0, self.at.next_y, self.first), (1, self.at.last_y, self.first + self.half)):
            self.copies[slot].wait_recv()

            def one(i, carry, slot=slot, chunk=chunk, first=first):
                term = self.plane[chunk, first + i].astype(F32) + self.landed[slot, i].astype(F32)
                self.plane[chunk, first + i] = term.astype(BF16)
                return carry

            loop(self.half, one)
            self.copies[slot + 4].start()

    def result(self, take):
        for offset, slots in ((0, (3, 4)), (self.half, (2, 5))):
            for slot in slots:
                self.copies[slot].wait_recv()

            def one(i, carry, offset=offset, slots=slots):
                value = self.plane[self.at.y, self.first + offset + i].astype(F32)
                for slot in slots:
                    value += self.landed[slot, i].astype(F32)
                take(offset + i, value)
                return carry

            loop(self.half, one)

    def drain(self):
        for copy in self.copies:
            copy.wait_send()


def reduce(
    at, finish, beside,
    part, crossed, total, landed, behind, outgoing, incoming,
    c_send, c_recv, send, recv, h_send, h_recv, low_send, low_recv,
):
    count = crossed.shape[1]
    split = low_of(count)
    high = count - split
    order = (at.far_y, at.next_y, at.last_y, at.y)
    across = [
        remote(part.at[1, chunk], crossed.at[chunk], c_send.at[i], c_recv.at[i], at.partner)
        for i, chunk in enumerate(order)
    ]
    ahead_low = Fold(at, total.at[1], part.at[2], landed.at[0], 0, split, send.at[0], recv.at[0])
    own_low = Fold(at, total.at[0], part.at[0], landed.at[1], 0, split, send.at[1], recv.at[1])
    own_high = Fold(at, total.at[0], None, landed.at[2], split, high, send.at[2], recv.at[2])
    x_high, x_soon = (
        [
            remote(source.at[chunk, pl.ds(split, high)], behind.at[chunk], h_send.at[i], h_recv.at[i], at.ahead)
            for i, chunk in enumerate(order)
        ]
        for source in (total.at[1], part.at[2])
    )
    x_low = remote(outgoing, incoming, low_send, low_recv, at.ahead)
    for copy in across:
        copy.start()

    @pl.when(at.odd == 1)
    def _():
        for copy in x_soon[:1]:
            copy.start()
        ahead_low.begin()
        for copy in x_soon[1:]:
            copy.start()

    @pl.when(at.odd == 0)
    def _():
        own_low.begin()

    def combine(index):
        chunk = order[index]
        joined, kept = 1 - at.odd, at.odd
        across[index].wait_recv()

        def one(i, carry):
            term = part[2 * joined, chunk, i].astype(F32) + crossed[chunk, i].astype(F32)
            total[joined, chunk, i] = term.astype(BF16)
            total[kept, chunk, i] = part[2 * kept, chunk, i]
            return carry

        loop(count, one)

    def join(index):
        chunk = order[index]
        x_high[index].wait_recv()

        def one(i, carry):
            term = total[0, chunk, split + i].astype(F32) + behind[chunk, i].astype(F32)
            total[0, chunk, split + i] = term.astype(BF16)
            return carry

        loop(high, one)

    def send_on(i, value):
        outgoing[i] = value.astype(BF16)

    for index in range(4):
        combine(index)

        @pl.when(at.odd == 0)
        def _(index=index):
            x_high[index].start()
            if index < 3:
                (ahead_low.far, ahead_low.next, ahead_low.last)[index]()

        @pl.when(at.odd == 1)
        def _(index=index):
            if index < 3:
                (own_low.far, own_low.next, own_low.last)[index]()

        if index == 0:
            beside[0]()
    beside[1]()
    ahead_low.relay()
    own_low.relay()
    join(0)
    own_high.far()
    ahead_low.result(send_on)
    x_low.start()
    beside[2]()
    join(1)
    own_high.next()
    join(2)
    own_high.last()
    beside[3]()
    own_high.relay()
    join(3)
    beside[4]()
    own_high.result(lambda i, value: finish(split + i, 0.5 * value))
    beside[5]()
    x_low.wait_recv()
    own_low.result(lambda i, value: finish(i, 0.5 * (value + incoming[i].astype(F32))))

    def drain():
        for copy in across + x_high + [x_low]:
            copy.wait_send()
        for fold in (ahead_low, own_low, own_high):
            fold.drain()

    return drain


def middle_kernel(shards, part, window, *scratch):
    at = Place(shards)
    partners = (at.partner, at.ahead, at.behind, at.right, at.left)
    signal_all(partners)
    wait_all(partners)

    def keep(i, value):
        window[0, at.y, i] = value.astype(BF16)

    count = 6 + len(REDUCE_SEMS)
    steps = gather(at, window, *scratch[count:])
    drain = reduce(at, keep, [nothing] * 5 + [lambda: next(steps)], part, *scratch[:count])
    next(steps)
    drain()


def last_kernel(shards, groups, part, p_ref, h_ref, hq_ref, x_ref, r_ref, sums, heard, s_send, s_recv, *scratch):
    at = Place(shards)
    opposite = (at.s, at.far_y)
    peers = [at.around(stride, size, step) for stride, size in groups for step in range(1, size)]
    partners = [at.partner, at.ahead, at.behind, at.right, at.left, opposite] + peers
    signal_all(partners)
    wait_all(partners)
    _, blocks, sub, width = h_ref.shape
    zero = jnp.zeros((sub, width), F32)
    lanes = lax.broadcasted_iota(jnp.int32, (sub, width), 1)
    rounds = [[(hq_ref.at[y], at_y) for y, at_y in ((at.next_y, at.right), (at.last_y, at.left), (at.far_y, opposite))]]
    rounds += [[(sums, at.around(stride, size, step)) for step in range(1, size)] for stride, size in groups]
    messages = []
    for one_round in rounds:
        first = sum(map(len, messages))
        messages.append(
            [
                remote(source, heard.at[slot], s_send.at[slot], s_recv.at[slot], device)
                for slot, (source, device) in enumerate(one_round, first)
            ]
        )

    def tell(k):
        for message in messages[k]:
            message.start()

    def hear(k):
        for message in messages[k]:
            message.wait_recv()
        for message in messages[k]:
            message.wait_send()
        first = sum(map(len, messages[:k]))
        return sum((heard[slot] for slot in range(first, first + len(messages[k]))), zero)

    def p_of(i):
        return p_ref[pl.ds(pl.multiple_of(at.y * sub, sub), sub), pl.ds(pl.multiple_of(i * width, width), width)]

    def h_of(i):
        return h_ref[at.y, i].astype(F32)

    def square():
        def one(i, carry):
            p, h = p_of(i), h_of(i)
            return carry[0] + p * p, carry[1] + p * h, carry[2] + h * h

        packed = zero
        for k, value in enumerate(loop(blocks, one, (zero, zero, zero))):
            packed = jnp.where(lanes == k, jnp.sum(value, axis=1, keepdims=True), packed)
        sums[...] = packed

    def start_sums():
        value = jnp.sum(hear(0) + hq_ref[at.y], axis=1, keepdims=True)
        sums[...] = jnp.where(lanes == 3, value, sums[...])
        tell(1)

    def pass_sums():
        sums[...] = sums[...] + hear(1)
        tell(2)

    scale = []

    def end_sums():
        packed = sums[...] + hear(2)
        pp, ph, hh, hq = (
            jnp.broadcast_to(jnp.sum(jnp.where(lanes == k, packed, 0.0), axis=1, keepdims=True), (sub, width))
            for k in range(4)
        )
        first = pp / (pp + ph)
        rest = ph / (pp + ph)
        norm = rest * rest * pp - 2.0 * rest * first * ph + first * first * hh
        a = rest + norm / pp
        c = first
        curve = a * a * pp + a * (a - 2.0 * c) * ph + c * (c - 2.0 * a) * hh + c * c * hq
        second = norm / curve
        x_p, x_h = first + second * a, second * c
        scale.extend((rest - second * a, first + second * (a - c), second * c))

        def one(i, carry):
            x_ref[:, pl.ds(pl.multiple_of(i * width, width), width)] = x_p * p_of(i) - x_h * h_of(i)
            return carry

        loop(blocks, one)

    def keep(i, q):
        r_p, r_h, r_q = scale
        r_ref[:, pl.ds(pl.multiple_of(i * width, width), width)] = r_p * p_of(i) - r_h * h_of(i) + r_q * q

    tell(0)
    drain = reduce(at, keep, [square, start_sums, pass_sums, nothing, end_sums, nothing], part, *scratch)
    drain()


def apply_kernel(first, nbr_ref, u_ref, x_ref, *rest):
    if first:
        part, deg, back, along, deg_along = rest
    else:
        deg, part, h_out, hq_out, back, along = rest
    columns, width = x_ref.shape[1:]
    rows = u_ref.shape[0]
    base = lax.axis_index("rows") * rows
    window = 3 * rows

    def clear(i, carry):
        back[i] = jnp.zeros((columns, width), F32)
        if first:
            deg[i] = jnp.zeros((8, width), F32)
        return carry

    loop(window, clear)
    ones = jnp.ones((ONES, 2 * width), BF16)

    def row(b, carry):
        t0, t1 = nbr_ref[0, b] - base, nbr_ref[1, b] - base
        pair = jnp.concatenate([u_ref[b, 0], u_ref[b, 1]], axis=1)
        own = x_ref[b]
        far = jnp.concatenate([x_ref[t0], x_ref[t1]], axis=1)
        if first:
            own = jnp.concatenate([own, ones[:, :width]], axis=0)
            far = jnp.concatenate([far, ones], axis=0)
        forward = lax.dot_general(far, pair, (((1,), (1,)), ((), ())), preferred_element_type=F32)
        returned = lax.dot_general(own, pair, (((1,), (0,)), ((), ())), preferred_element_type=F32)
        along[b] = forward[:columns]
        back[t0] += returned[:columns, :width]
        back[t1] += returned[:columns, width:]
        if first:
            deg_along[b] = forward[columns : columns + 8]
            deg[t0] += returned[columns : columns + 8, :width]
            deg[t1] += returned[columns : columns + 8, width:]
        return carry

    lax.fori_loop(0, rows, row, 0, unroll=min(ROW_UNROLL, rows))

    def term(i, own):
        weight = deg[i]
        minus = back[i]
        if own:
            minus += along[i]
            if first:
                weight += deg_along[i]
                deg[i] = weight
        x = x_ref[i].astype(F32)
        return x, jnp.concatenate([weight] * (columns // 8), axis=0) * x - minus

    dots = jnp.zeros((columns, width), F32)
    for d in range(3):

        def one(i, carry, d=d):
            x, value = term(d * rows + i, d == 0)
            carry += x * value
            if first:
                part[d * rows + i] = value.astype(BF16)
            else:
                for g in range(RING):
                    at = slice(g * (columns // RING), (g + 1) * (columns // RING))
                    part[d, g, i] = value[at].astype(BF16)
                    if d == 0:
                        h_out[g, i] = x[at].astype(BF16)
            return carry

        dots = loop(rows, one, dots)
    if not first:
        for g in range(RING):
            hq_out[g] = 0.5 * dots[g * (columns // RING) : (g + 1) * (columns // RING)]


def apply(first, nbr, upper, window, deg=None):
    rows, slots, width, _ = upper.shape
    columns = window.shape[-2]
    x = window.reshape(3 * rows, columns, width)
    deg_shape = jax.ShapeDtypeStruct((3 * rows, 8, width), F32)
    scratch = [pltpu.VMEM(x.shape, F32), pltpu.VMEM((rows, columns, width), F32)]
    if first:
        out_shape = [jax.ShapeDtypeStruct(x.shape, BF16), deg_shape]
        scratch.append(pltpu.VMEM((rows, 8, width), F32))
        args = (nbr, upper, x)
    else:
        sub = columns // RING
        out_shape = [
            jax.ShapeDtypeStruct((3, RING, rows, sub, width), BF16),
            jax.ShapeDtypeStruct((RING, rows, sub, width), BF16),
            jax.ShapeDtypeStruct((RING, sub, width), F32),
        ]
        args = (nbr, upper, x, deg)
    return pl.pallas_call(
        functools.partial(apply_kernel, first),
        out_shape=out_shape,
        in_specs=[pl.BlockSpec(memory_space=pltpu.SMEM)] + [VMEM] * (len(args) - 1),
        out_specs=[VMEM] * len(out_shape),
        scratch_shapes=scratch,
        compiler_params=pltpu.CompilerParams(vmem_limit_bytes=LIMITS["apply"]),
        cost_estimate=pl.CostEstimate(
            flops=4 * rows * slots * width * width * columns, transcendentals=0, bytes_accessed=upper.size * 2
        ),
        name="apply_first" if first else "apply_second",
    )(*args)


def talk(body, out_shape, scratch, collective_id, name, *args, in_specs=None):
    return pl.pallas_call(
        body,
        out_shape=out_shape,
        in_specs=in_specs or [VMEM] * len(args),
        out_specs=jax.tree.map(lambda _: VMEM, out_shape),
        scratch_shapes=scratch,
        compiler_params=pltpu.CompilerParams(
            collective_id=collective_id, has_side_effects=True, vmem_limit_bytes=LIMITS[name]
        ),
        cost_estimate=pl.CostEstimate(flops=0, transcendentals=0, bytes_accessed=TRAFFIC[name]),
        name=name,
    )(*args)


def per_device(pass_rates, upper_blocks, neighbours):
    rows, _, width, _ = upper_blocks.shape
    columns = pass_rates.shape[0]
    shards = lax.axis_size("rows")
    if lax.axis_size("cols") != RING or shards % 8:
        raise ValueError("mesh shape")
    quarter, sub = rows // RING, columns // RING
    groups = [(1, 8), (8, shards // 8)]
    messages = RING - 1 + sum(size - 1 for _, size in groups)
    nbr = neighbours.T
    window_shape = jax.ShapeDtypeStruct((3, RING, quarter, columns, width), BF16)

    window, upper = talk(
        functools.partial(halo_kernel, shards),
        (window_shape, jax.ShapeDtypeStruct(upper_blocks.shape, BF16)),
        [pltpu.VMEM(pass_rates.shape, F32), pltpu.SemaphoreType.DMA((RING,)), pltpu.SemaphoreType.DMA] + HALO_SEMS,
        0,
        "halo",
        pltpu.with_memory_space_constraint(pass_rates, pltpu.HBM),
        pltpu.with_memory_space_constraint(upper_blocks, pltpu.HBM),
        in_specs=[pl.BlockSpec(memory_space=pltpu.HBM)] * 2,
    )
    part, deg = apply(True, nbr, upper, window)
    window = talk(
        functools.partial(middle_kernel, shards),
        window_shape,
        reduce_scratch(quarter, columns, width) + GATHER_SEMS,
        1,
        "middle",
        part.reshape(window_shape.shape),
    )
    part, h, hq = apply(False, nbr, upper, window, deg)
    out_shape = jax.ShapeDtypeStruct((sub, rows * width), F32)
    return talk(
        functools.partial(last_kernel, shards, groups),
        (out_shape, out_shape),
        [pltpu.VMEM((sub, width), F32), pltpu.VMEM((messages, sub, width), F32)]
        + pairs((messages,))
        + reduce_scratch(rows, sub, width),
        2,
        "last",
        part,
        pass_rates,
        h,
        hq,
    )


def solution(mesh):
    in_specs = (P(None, "rows"), P("rows", "cols", None, None), P("rows", "cols"))
    out_specs = (P("cols", "rows"), P("cols", "rows"))
    return jax.shard_map(per_device, mesh=mesh, in_specs=in_specs, out_specs=out_specs, check_vma=False)
```

```python
import functools

import jax
import jax.numpy as jnp
from jax import lax
from jax.experimental import pallas as pl
from jax.experimental.pallas import tpu as pltpu
from jax.sharding import PartitionSpec as P

MESH = pl.DeviceIdType.MESH
F32 = jnp.float32
BF16 = jnp.bfloat16
RING = 4
VMEM = pl.BlockSpec(memory_space=pltpu.VMEM)
MIB = 2**20
ONES = 16
UNROLL = 8
ROW_UNROLL = 32
PARTS = 2
TRAFFIC = {"halo": 60 * MIB, "middle": 150 * MIB, "last": 120 * MIB}
LIMITS = {"halo": 20 * MIB, "apply": 32 * MIB, "middle": 24 * MIB, "last": 24 * MIB}


def rem(value, count):
    return lax.rem(value, jnp.int32(count))


def loop(count, body, carry=0):
    unroll = max(n for n in range(1, UNROLL + 1) if count % n == 0)
    return lax.fori_loop(0, count, body, carry, unroll=unroll)


def parts_of(split):
    return [(k * (split // PARTS), split // PARTS) for k in range(PARTS)]


def nothing():
    pass


def low_of(count):
    return count * 5 // (16 * PARTS) * 2 * PARTS


class Place:
    def __init__(self, shards):
        self.shards = shards
        self.s = lax.axis_index("rows")
        self.y = lax.axis_index("cols")
        self.odd = rem(self.s, 2)
        self.next_y = rem(self.y + 1, RING)
        self.last_y = rem(self.y + RING - 1, RING)
        self.far_y = rem(self.y + 2, RING)
        self.partner = (self.s + 1 - 2 * self.odd, self.y)
        self.ahead = (rem(self.s + 2, shards), self.y)
        self.behind = (rem(self.s + shards - 2, shards), self.y)
        self.right = (self.s, self.next_y)
        self.left = (self.s, self.last_y)

    def around(self, stride, size, step):
        at = rem(self.s // stride, size)
        return (self.s + (rem(at + step, size) - at) * stride, self.y)


def signal_all(devices):
    barrier = pltpu.get_barrier_semaphore()
    for device in devices:
        pl.semaphore_signal(barrier, inc=1, device_id=device, device_id_type=MESH)


def wait_all(devices):
    pl.semaphore_wait(pltpu.get_barrier_semaphore(), len(devices))


def remote(src, dst, send_sem, recv_sem, device):
    return pltpu.make_async_remote_copy(
        src_ref=src, dst_ref=dst, send_sem=send_sem, recv_sem=recv_sem, device_id=device, device_id_type=MESH
    )


class Spread:
    def __init__(self, at, plane, first, count, send, recv):
        half = count // 2
        low, high = pl.ds(first, half), pl.ds(first + half, half)
        routes = (
            (at.y, low, at.right),
            (at.y, high, at.left),
            (at.y, high, at.right),
            (at.y, low, at.left),
            (at.last_y, low, at.right),
            (at.next_y, high, at.left),
        )
        self.copies = [
            remote(plane.at[chunk, part], plane.at[chunk, part], send.at[i], recv.at[i], device)
            for i, (chunk, part, device) in enumerate(routes)
        ]

    def start(self):
        for copy in self.copies[:4]:
            copy.start()

    def relay(self):
        for first, second in ((0, 4), (1, 5)):
            self.copies[first].wait_recv()
            self.copies[second].start()

    def near(self):
        for i in (2, 3):
            self.copies[i].wait_recv()

    def far(self):
        for i in (4, 5):
            self.copies[i].wait_recv()

    def drain(self):
        for copy in self.copies:
            copy.wait_send()


def gather(at, window, send, recv, low_send, low_recv, high_send, high_recv, c_send, c_recv):
    count = window.shape[2]
    split = low_of(count)
    low, high = pl.ds(0, split), pl.ds(split, count - split)
    order = (at.y, at.last_y, at.next_y, at.far_y)
    own_high = Spread(at, window.at[0], split, count - split, send.at[2 * PARTS], recv.at[2 * PARTS])
    next_low = [Spread(at, window.at[2], *part, send.at[k], recv.at[k]) for k, part in enumerate(parts_of(split))]
    own_low = [
        Spread(at, window.at[0], *part, send.at[PARTS + k], recv.at[PARTS + k])
        for k, part in enumerate(parts_of(split))
    ]
    x_low = [
        remote(
            window.at[0, at.y, pl.ds(*part)], window.at[2, at.y, pl.ds(*part)], low_send.at[k], low_recv.at[k], at.behind
        )
        for k, part in enumerate(parts_of(split))
    ]
    x_high = [
        remote(window.at[0, chunk, high], window.at[2, chunk, high], high_send.at[i], high_recv.at[i], at.behind)
        for i, chunk in enumerate(order)
    ]
    source = 2 - 2 * at.odd
    across = [
        [
            remote(
                window.at[source, chunk, part], window.at[1, chunk, part], c_send.at[k, i], c_recv.at[k, i], at.partner
            )
            for i, chunk in enumerate(order)
        ]
        for k, part in enumerate((low, high))
    ]
    own_high.start()
    x_high[0].start()
    for copy in x_low:
        yield
        copy.start()
    yield
    own_high.relay()
    own_high.near()
    x_high[1].start()
    x_high[2].start()
    for k in range(PARTS):
        x_low[k].wait_recv()
        next_low[k].start()
        if k:
            next_low[k - 1].relay()
        own_low[k].start()
        if not k:
            own_high.far()
            x_high[3].start()
    across[0][0].start()
    next_low[-1].relay()
    for spread in own_low:
        spread.relay()
    x_high[0].wait_recv()
    across[1][0].start()
    for spread in next_low + own_low:
        spread.near()
    across[0][1].start()
    across[0][2].start()
    for i in (1, 2):
        x_high[i].wait_recv()
        across[1][i].start()
    for spread in next_low + own_low:
        spread.far()
    across[0][3].start()
    x_high[3].wait_recv()
    across[1][3].start()
    for spread in [own_high] + next_low + own_low:
        spread.drain()
    for copy in x_low + x_high:
        copy.wait_send()
    for copy in across[0] + across[1]:
        copy.wait()
    yield


def halo_kernel(
    shards, p_hbm, u_hbm, window, u_ref, p_ref, p_sem, u_sem, send, recv, q_send, q_recv, d_send, d_recv, c_send, c_recv
):
    at = Place(shards)
    partners = (at.partner, at.ahead, at.behind, at.right, at.left)
    signal_all(partners)
    blocks, columns, width = window.shape[2:]
    order = (at.y, at.last_y, at.next_y, at.far_y)

    def span(chunk):
        return pl.ds(pl.multiple_of(chunk * (blocks * width), width), blocks * width)

    loads = [
        pltpu.make_async_copy(p_hbm.at[:, span(chunk)], p_ref.at[:, span(chunk)], p_sem.at[i])
        for i, chunk in enumerate(order)
    ]
    for load in loads:
        load.start()
    weights = pltpu.make_async_copy(u_hbm, u_ref, u_sem)

    def cast(index):
        chunk = order[index]
        loads[index].wait()

        def one(i, carry):
            first = pl.multiple_of((chunk * blocks + i) * width, width)
            window[0, chunk, i] = p_ref[:, pl.ds(first, width)].astype(BF16)
            return carry

        loop(blocks, one)

    split = low_of(blocks)
    piece = split // 2
    parts = [pl.ds(0, piece), pl.ds(piece, piece), pl.ds(split, blocks - split)]
    pieces = [
        remote(window.at[0, at.y, parts[k]], window.at[2, at.y, parts[k]], q_send.at[k], q_recv.at[k], at.behind)
        for k in range(2)
    ]
    direct = [
        remote(window.at[0, chunk, parts[2]], window.at[2, chunk, parts[2]], d_send.at[i], d_recv.at[i], at.behind)
        for i, chunk in enumerate(order)
    ]
    spreads = [Spread(at, window.at[2], k * piece, piece, send.at[k], recv.at[k]) for k in range(2)]
    source = 2 - 2 * at.odd
    across = [
        remote(window.at[source, chunk], window.at[1, chunk], c_send.at[i], c_recv.at[i], at.partner)
        for i, chunk in enumerate(order)
    ]
    cast(0)
    wait_all(partners)
    pieces[0].start()
    pieces[1].start()
    weights.start()
    for index in (1, 2, 3):
        cast(index)
    pieces[0].wait_recv()
    spreads[0].start()
    for copy in direct:
        copy.start()
    pieces[1].wait_recv()
    spreads[1].start()
    spreads[0].relay()
    direct[0].wait_recv()
    across[0].start()
    spreads[1].relay()
    for spread in spreads:
        spread.near()
    for i in (1, 2):
        direct[i].wait_recv()
        across[i].start()
    for spread in spreads:
        spread.far()
    direct[3].wait_recv()
    across[3].start()
    for spread in spreads:
        spread.drain()
    for copy in pieces + direct:
        copy.wait_send()
    for copy in across:
        copy.wait()
    weights.wait()


def pairs(*shapes):
    return [pltpu.SemaphoreType.DMA(shape) for shape in shapes for _ in range(2)]


HALO_SEMS = pairs((2, 6), (2,), (4,), (4,))
GATHER_SEMS = pairs((2 * PARTS + 1, 6), (PARTS,), (4,), (2, 4))
REDUCE_SEMS = pairs((4,), (2 * PARTS + 1, 6), (4,), (PARTS,))


def reduce_scratch(blocks, sub, width):
    most = max(low_of(blocks) // PARTS, blocks - low_of(blocks)) // 2
    return [
        pltpu.VMEM((RING, blocks, sub, width), BF16),
        pltpu.VMEM((2, RING, blocks, sub, width), BF16),
        pltpu.VMEM((2 * PARTS + 1, 6, most, sub, width), BF16),
        pltpu.VMEM((RING, blocks - low_of(blocks), sub, width), BF16),
        pltpu.VMEM((low_of(blocks), sub, width), BF16),
        pltpu.VMEM((low_of(blocks), sub, width), BF16),
    ] + REDUCE_SEMS


class Fold:
    def __init__(self, at, plane, whole, landed, first, count, send, recv):
        self.at, self.plane, self.landed, self.first, self.half = at, plane, landed, first, count // 2
        low, high = pl.ds(first, self.half), pl.ds(first + self.half, self.half)
        routes = (
            (at.far_y, low, at.right),
            (at.far_y, high, at.left),
            (at.next_y, high, at.right),
            (at.last_y, low, at.left),
            (at.next_y, low, at.right),
            (at.last_y, high, at.left),
        )
        self.copies, self.soon = (
            [
                remote(source.at[chunk, part], landed.at[i, pl.ds(0, self.half)], send.at[i], recv.at[i], device)
                for i, (chunk, part, device) in enumerate(routes[:most])
            ]
            for source, most in ((plane, 6), (whole, 4 if whole is not None else 0))
        )

    def far(self):
        self.copies[0].start()
        self.copies[1].start()

    def next(self):
        self.copies[2].start()

    def last(self):
        self.copies[3].start()

    def begin(self):
        for copy in self.soon:
            copy.start()

    def relay(self):
        for slot, chunk, first in ((0, self.at.next_y, self.first), (1, self.at.last_y, self.first + self.half)):
            self.copies[slot].wait_recv()

            def one(i, carry, slot=slot, chunk=chunk, first=first):
                term = self.plane[chunk, first + i].astype(F32) + self.landed[slot, i].astype(F32)
                self.plane[chunk, first + i] = term.astype(BF16)
                return carry

            loop(self.half, one)
            self.copies[slot + 4].start()

    def result(self, take):
        for offset, slots in ((0, (3, 4)), (self.half, (2, 5))):
            for slot in slots:
                self.copies[slot].wait_recv()

            def one(i, carry, offset=offset, slots=slots):
                value = self.plane[self.at.y, self.first + offset + i].astype(F32)
                for slot in slots:
                    value += self.landed[slot, i].astype(F32)
                take(offset + i, value)
                return carry

            loop(self.half, one)

    def drain(self):
        for copy in self.copies:
            copy.wait_send()


def reduce(
    at, finish, beside,
    part, crossed, total, landed, behind, outgoing, incoming,
    c_send, c_recv, send, recv, h_send, h_recv, low_send, low_recv,
):
    count = crossed.shape[1]
    split = low_of(count)
    high = count - split
    order = (at.far_y, at.next_y, at.last_y, at.y)
    across = [
        remote(part.at[1, chunk], crossed.at[chunk], c_send.at[i], c_recv.at[i], at.partner)
        for i, chunk in enumerate(order)
    ]
    parts = parts_of(split)
    ahead_low, own_low = (
        [
            Fold(at, total.at[j], part.at[2 * j], landed.at[stream], *parts[k], send.at[stream], recv.at[stream])
            for k, stream in enumerate(range(first, first + PARTS))
        ]
        for j, first in ((1, 0), (0, PARTS))
    )
    own_high = Fold(at, total.at[0], None, landed.at[2 * PARTS], split, high, send.at[2 * PARTS], recv.at[2 * PARTS])
    x_high, x_soon = (
        [
            remote(source.at[chunk, pl.ds(split, high)], behind.at[chunk], h_send.at[i], h_recv.at[i], at.ahead)
            for i, chunk in enumerate(order)
        ]
        for source in (total.at[1], part.at[2])
    )
    x_low = [
        remote(outgoing.at[pl.ds(*parts[k])], incoming.at[pl.ds(*parts[k])], low_send.at[k], low_recv.at[k], at.ahead)
        for k in range(PARTS)
    ]
    for copy in across:
        copy.start()

    @pl.when(at.odd == 1)
    def _():
        for copy in x_soon[:1]:
            copy.start()
        for fold in ahead_low:
            fold.begin()
        for copy in x_soon[1:]:
            copy.start()

    @pl.when(at.odd == 0)
    def _():
        for fold in own_low:
            fold.begin()

    def combine(index):
        chunk = order[index]
        joined, kept = 1 - at.odd, at.odd
        across[index].wait_recv()

        def one(i, carry):
            term = part[2 * joined, chunk, i].astype(F32) + crossed[chunk, i].astype(F32)
            total[joined, chunk, i] = term.astype(BF16)
            total[kept, chunk, i] = part[2 * kept, chunk, i]
            return carry

        loop(count, one)

    def join(index):
        chunk = order[index]
        x_high[index].wait_recv()

        def one(i, carry):
            term = total[0, chunk, split + i].astype(F32) + behind[chunk, i].astype(F32)
            total[0, chunk, split + i] = term.astype(BF16)
            return carry

        loop(high, one)

    def send_on(first, i, value):
        outgoing[first + i] = value.astype(BF16)

    def finish_low(first, i, value):
        finish(first + i, 0.5 * (value + incoming[first + i].astype(F32)))

    for index in range(4):
        combine(index)

        @pl.when(at.odd == 0)
        def _(index=index):
            x_high[index].start()
            for fold in ahead_low if index < 3 else []:
                (fold.far, fold.next, fold.last)[index]()

        @pl.when(at.odd == 1)
        def _(index=index):
            for fold in own_low if index < 3 else []:
                (fold.far, fold.next, fold.last)[index]()

        if index == 0:
            beside[0]()
    beside[1]()
    for fold in ahead_low + own_low:
        fold.relay()
    join(0)
    own_high.far()
    for k in range(PARTS):
        ahead_low[k].result(functools.partial(send_on, parts[k][0]))
        x_low[k].start()
    beside[2]()
    join(1)
    own_high.next()
    join(2)
    own_high.last()
    beside[3]()
    own_high.relay()
    join(3)
    beside[4]()
    own_high.result(lambda i, value: finish(split + i, 0.5 * value))
    beside[5]()
    for k in range(PARTS):
        x_low[k].wait_recv()
        own_low[k].result(functools.partial(finish_low, parts[k][0]))
        beside[6]()

    def drain():
        for copy in across + x_high + x_low:
            copy.wait_send()
        for fold in ahead_low + own_low + [own_high]:
            fold.drain()

    return drain


def middle_kernel(shards, part, window, *scratch):
    at = Place(shards)
    partners = (at.partner, at.ahead, at.behind, at.right, at.left)
    signal_all(partners)
    wait_all(partners)

    def keep(i, value):
        window[0, at.y, i] = value.astype(BF16)

    count = 6 + len(REDUCE_SEMS)
    steps = gather(at, window, *scratch[count:])
    drain = reduce(at, keep, [nothing] * 5 + [lambda: next(steps)] * 2, part, *scratch[:count])
    next(steps)
    drain()


def last_kernel(shards, groups, part, p_ref, h_ref, hq_ref, x_ref, r_ref, sums, heard, s_send, s_recv, *scratch):
    at = Place(shards)
    opposite = (at.s, at.far_y)
    peers = [at.around(stride, size, step) for stride, size in groups for step in range(1, size)]
    partners = [at.partner, at.ahead, at.behind, at.right, at.left, opposite] + peers
    signal_all(partners)
    wait_all(partners)
    _, blocks, sub, width = h_ref.shape
    zero = jnp.zeros((sub, width), F32)
    lanes = lax.broadcasted_iota(jnp.int32, (sub, width), 1)
    rounds = [[(hq_ref.at[y], at_y) for y, at_y in ((at.next_y, at.right), (at.last_y, at.left), (at.far_y, opposite))]]
    rounds += [[(sums, at.around(stride, size, step)) for step in range(1, size)] for stride, size in groups]
    messages = []
    for one_round in rounds:
        first = sum(map(len, messages))
        messages.append(
            [
                remote(source, heard.at[slot], s_send.at[slot], s_recv.at[slot], device)
                for slot, (source, device) in enumerate(one_round, first)
            ]
        )

    def tell(k):
        for message in messages[k]:
            message.start()

    def hear(k):
        for message in messages[k]:
            message.wait_recv()
        for message in messages[k]:
            message.wait_send()
        first = sum(map(len, messages[:k]))
        return sum((heard[slot] for slot in range(first, first + len(messages[k]))), zero)

    def p_of(i):
        return p_ref[pl.ds(pl.multiple_of(at.y * sub, sub), sub), pl.ds(pl.multiple_of(i * width, width), width)]

    def h_of(i):
        return h_ref[at.y, i].astype(F32)

    def square():
        def one(i, carry):
            p, h = p_of(i), h_of(i)
            return carry[0] + p * p, carry[1] + p * h, carry[2] + h * h

        packed = zero
        for k, value in enumerate(loop(blocks, one, (zero, zero, zero))):
            packed = jnp.where(lanes == k, jnp.sum(value, axis=1, keepdims=True), packed)
        sums[...] = packed

    def start_sums():
        value = jnp.sum(hear(0) + hq_ref[at.y], axis=1, keepdims=True)
        sums[...] = jnp.where(lanes == 3, value, sums[...])
        tell(1)

    def pass_sums():
        sums[...] = sums[...] + hear(1)
        tell(2)

    scale = []

    def end_sums():
        packed = sums[...] + hear(2)
        pp, ph, hh, hq = (
            jnp.broadcast_to(jnp.sum(jnp.where(lanes == k, packed, 0.0), axis=1, keepdims=True), (sub, width))
            for k in range(4)
        )
        first = pp / (pp + ph)
        rest = ph / (pp + ph)
        norm = rest * rest * pp - 2.0 * rest * first * ph + first * first * hh
        a = rest + norm / pp
        c = first
        curve = a * a * pp + a * (a - 2.0 * c) * ph + c * (c - 2.0 * a) * hh + c * c * hq
        second = norm / curve
        x_p, x_h = first + second * a, second * c
        scale.extend((rest - second * a, first + second * (a - c), second * c))

        def one(i, carry):
            x_ref[:, pl.ds(pl.multiple_of(i * width, width), width)] = x_p * p_of(i) - x_h * h_of(i)
            return carry

        loop(blocks, one)

    def keep(i, q):
        r_p, r_h, r_q = scale
        r_ref[:, pl.ds(pl.multiple_of(i * width, width), width)] = r_p * p_of(i) - r_h * h_of(i) + r_q * q

    tell(0)
    drain = reduce(at, keep, [square, start_sums, pass_sums, nothing, end_sums, nothing, nothing], part, *scratch)
    drain()


def apply_kernel(first, nbr_ref, u_ref, x_ref, *rest):
    if first:
        part, deg, back, along, deg_along = rest
    else:
        deg, part, h_out, hq_out, back, along = rest
    columns, width = x_ref.shape[1:]
    rows = u_ref.shape[0]
    base = lax.axis_index("rows") * rows
    window = 3 * rows

    def clear(i, carry):
        back[i] = jnp.zeros((columns, width), F32)
        if first:
            deg[i] = jnp.zeros((8, width), F32)
        return carry

    loop(window, clear)
    ones = jnp.ones((ONES, 2 * width), BF16)

    def row(b, carry):
        t0, t1 = nbr_ref[0, b] - base, nbr_ref[1, b] - base
        pair = jnp.concatenate([u_ref[b, 0], u_ref[b, 1]], axis=1)
        own = x_ref[b]
        far = jnp.concatenate([x_ref[t0], x_ref[t1]], axis=1)
        if first:
            own = jnp.concatenate([own, ones[:, :width]], axis=0)
            far = jnp.concatenate([far, ones], axis=0)
        forward = lax.dot_general(far, pair, (((1,), (1,)), ((), ())), preferred_element_type=F32)
        returned = lax.dot_general(own, pair, (((1,), (0,)), ((), ())), preferred_element_type=F32)
        along[b] = forward[:columns]
        back[t0] += returned[:columns, :width]
        back[t1] += returned[:columns, width:]
        if first:
            deg_along[b] = forward[columns : columns + 8]
            deg[t0] += returned[columns : columns + 8, :width]
            deg[t1] += returned[columns : columns + 8, width:]
        return carry

    lax.fori_loop(0, rows, row, 0, unroll=min(ROW_UNROLL, rows))

    def term(i, own):
        weight = deg[i]
        minus = back[i]
        if own:
            minus += along[i]
            if first:
                weight += deg_along[i]
                deg[i] = weight
        x = x_ref[i].astype(F32)
        return x, jnp.concatenate([weight] * (columns // 8), axis=0) * x - minus

    dots = jnp.zeros((columns, width), F32)
    for d in range(3):

        def one(i, carry, d=d):
            x, value = term(d * rows + i, d == 0)
            carry += x * value
            if first:
                part[d * rows + i] = value.astype(BF16)
            else:
                for g in range(RING):
                    at = slice(g * (columns // RING), (g + 1) * (columns // RING))
                    part[d, g, i] = value[at].astype(BF16)
                    if d == 0:
                        h_out[g, i] = x[at].astype(BF16)
            return carry

        dots = loop(rows, one, dots)
    if not first:
        for g in range(RING):
            hq_out[g] = 0.5 * dots[g * (columns // RING) : (g + 1) * (columns // RING)]


def apply(first, nbr, upper, window, deg=None):
    rows, slots, width, _ = upper.shape
    columns = window.shape[-2]
    x = window.reshape(3 * rows, columns, width)
    deg_shape = jax.ShapeDtypeStruct((3 * rows, 8, width), F32)
    scratch = [pltpu.VMEM(x.shape, F32), pltpu.VMEM((rows, columns, width), F32)]
    if first:
        out_shape = [jax.ShapeDtypeStruct(x.shape, BF16), deg_shape]
        scratch.append(pltpu.VMEM((rows, 8, width), F32))
        args = (nbr, upper, x)
    else:
        sub = columns // RING
        out_shape = [
            jax.ShapeDtypeStruct((3, RING, rows, sub, width), BF16),
            jax.ShapeDtypeStruct((RING, rows, sub, width), BF16),
            jax.ShapeDtypeStruct((RING, sub, width), F32),
        ]
        args = (nbr, upper, x, deg)
    return pl.pallas_call(
        functools.partial(apply_kernel, first),
        out_shape=out_shape,
        in_specs=[pl.BlockSpec(memory_space=pltpu.SMEM)] + [VMEM] * (len(args) - 1),
        out_specs=[VMEM] * len(out_shape),
        scratch_shapes=scratch,
        compiler_params=pltpu.CompilerParams(vmem_limit_bytes=LIMITS["apply"]),
        cost_estimate=pl.CostEstimate(
            flops=4 * rows * slots * width * width * columns, transcendentals=0, bytes_accessed=upper.size * 2
        ),
        name="apply_first" if first else "apply_second",
    )(*args)


def talk(body, out_shape, scratch, collective_id, name, *args, in_specs=None):
    return pl.pallas_call(
        body,
        out_shape=out_shape,
        in_specs=in_specs or [VMEM] * len(args),
        out_specs=jax.tree.map(lambda _: VMEM, out_shape),
        scratch_shapes=scratch,
        compiler_params=pltpu.CompilerParams(
            collective_id=collective_id, has_side_effects=True, vmem_limit_bytes=LIMITS[name]
        ),
        cost_estimate=pl.CostEstimate(flops=0, transcendentals=0, bytes_accessed=TRAFFIC[name]),
        name=name,
    )(*args)


def per_device(pass_rates, upper_blocks, neighbours):
    rows, _, width, _ = upper_blocks.shape
    columns = pass_rates.shape[0]
    shards = lax.axis_size("rows")
    if lax.axis_size("cols") != RING or shards % 8:
        raise ValueError("mesh shape")
    quarter, sub = rows // RING, columns // RING
    groups = [(1, 8), (8, shards // 8)]
    messages = RING - 1 + sum(size - 1 for _, size in groups)
    nbr = neighbours.T
    window_shape = jax.ShapeDtypeStruct((3, RING, quarter, columns, width), BF16)

    window, upper = talk(
        functools.partial(halo_kernel, shards),
        (window_shape, jax.ShapeDtypeStruct(upper_blocks.shape, BF16)),
        [pltpu.VMEM(pass_rates.shape, F32), pltpu.SemaphoreType.DMA((RING,)), pltpu.SemaphoreType.DMA] + HALO_SEMS,
        0,
        "halo",
        pltpu.with_memory_space_constraint(pass_rates, pltpu.HBM),
        pltpu.with_memory_space_constraint(upper_blocks, pltpu.HBM),
        in_specs=[pl.BlockSpec(memory_space=pltpu.HBM)] * 2,
    )
    part, deg = apply(True, nbr, upper, window)
    window = talk(
        functools.partial(middle_kernel, shards),
        window_shape,
        reduce_scratch(quarter, columns, width) + GATHER_SEMS,
        1,
        "middle",
        part.reshape(window_shape.shape),
    )
    part, h, hq = apply(False, nbr, upper, window, deg)
    out_shape = jax.ShapeDtypeStruct((sub, rows * width), F32)
    return talk(
        functools.partial(last_kernel, shards, groups),
        (out_shape, out_shape),
        [pltpu.VMEM((sub, width), F32), pltpu.VMEM((messages, sub, width), F32)]
        + pairs((messages,))
        + reduce_scratch(rows, sub, width),
        2,
        "last",
        part,
        pass_rates,
        h,
        hq,
    )


def solution(mesh):
    in_specs = (P(None, "rows"), P("rows", "cols", None, None), P("rows", "cols"))
    out_specs = (P("cols", "rows"), P("cols", "rows"))
    return jax.shard_map(per_device, mesh=mesh, in_specs=in_specs, out_specs=out_specs, check_vma=False)
```

```python
import functools

import jax
import jax.numpy as jnp
from jax import lax
from jax.experimental import pallas as pl
from jax.experimental.pallas import tpu as pltpu
from jax.sharding import PartitionSpec as P

MESH = pl.DeviceIdType.MESH
F32 = jnp.float32
BF16 = jnp.bfloat16
RING = 4
VMEM = pl.BlockSpec(memory_space=pltpu.VMEM)
MIB = 2**20
ONES = 16
UNROLL = 8
ROW_UNROLL = 32
TRAFFIC = {"halo": 60 * MIB, "middle": 150 * MIB, "last": 120 * MIB}
LIMITS = {"halo": 20 * MIB, "apply": 26 * MIB, "middle": 30 * MIB, "last": 32 * MIB}


def rem(value, count):
    return lax.rem(value, jnp.int32(count))


def loop(count, body, carry=0):
    unroll = max(n for n in range(1, UNROLL + 1) if count % n == 0)
    return lax.fori_loop(0, count, body, carry, unroll=unroll)


def nothing():
    pass


def low_of(count):
    return count * 5 // 16 * 2


class Place:
    def __init__(self, shards):
        self.shards = shards
        self.s = lax.axis_index("rows")
        self.y = lax.axis_index("cols")
        self.odd = rem(self.s, 2)
        self.next_y = rem(self.y + 1, RING)
        self.last_y = rem(self.y + RING - 1, RING)
        self.far_y = rem(self.y + 2, RING)
        self.partner = (self.s + 1 - 2 * self.odd, self.y)
        self.ahead = (rem(self.s + 2, shards), self.y)
        self.behind = (rem(self.s + shards - 2, shards), self.y)
        self.right = (self.s, self.next_y)
        self.left = (self.s, self.last_y)

    def around(self, stride, size, step):
        at = rem(self.s // stride, size)
        return (self.s + (rem(at + step, size) - at) * stride, self.y)


def signal_all(devices):
    barrier = pltpu.get_barrier_semaphore()
    for device in devices:
        pl.semaphore_signal(barrier, inc=1, device_id=device, device_id_type=MESH)


def wait_all(devices):
    pl.semaphore_wait(pltpu.get_barrier_semaphore(), len(devices))


def remote(src, dst, send_sem, recv_sem, device):
    return pltpu.make_async_remote_copy(
        src_ref=src, dst_ref=dst, send_sem=send_sem, recv_sem=recv_sem, device_id=device, device_id_type=MESH
    )


class Spread:
    def __init__(self, at, plane, first, count, send, recv):
        half = count // 2
        low, high = pl.ds(first, half), pl.ds(first + half, half)
        routes = (
            (at.y, low, at.right),
            (at.y, high, at.left),
            (at.y, high, at.right),
            (at.y, low, at.left),
            (at.last_y, low, at.right),
            (at.next_y, high, at.left),
        )
        self.copies = [
            remote(plane.at[chunk, part], plane.at[chunk, part], send.at[i], recv.at[i], device)
            for i, (chunk, part, device) in enumerate(routes)
        ]

    def start(self):
        for copy in self.copies[:4]:
            copy.start()

    def relay(self):
        for first, second in ((0, 4), (1, 5)):
            self.copies[first].wait_recv()
            self.copies[second].start()

    def near(self):
        for i in (2, 3):
            self.copies[i].wait_recv()

    def far(self):
        for i in (4, 5):
            self.copies[i].wait_recv()

    def drain(self):
        for copy in self.copies:
            copy.wait_send()


def gather(at, window, send, recv, low_send, low_recv, high_send, high_recv, c_send, c_recv):
    count = window.shape[2]
    split = low_of(count)
    low, high = pl.ds(0, split), pl.ds(split, count - split)
    order = (at.y, at.last_y, at.next_y, at.far_y)
    own_high = Spread(at, window.at[0], split, count - split, send.at[0], recv.at[0])
    next_low = Spread(at, window.at[2], 0, split, send.at[1], recv.at[1])
    own_low = Spread(at, window.at[0], 0, split, send.at[2], recv.at[2])
    x_low = remote(window.at[0, at.y, low], window.at[2, at.y, low], low_send, low_recv, at.behind)
    x_high = [
        remote(window.at[0, chunk, high], window.at[2, chunk, high], high_send.at[i], high_recv.at[i], at.behind)
        for i, chunk in enumerate(order)
    ]
    source = 2 - 2 * at.odd
    across = [
        [
            remote(
                window.at[source, chunk, part], window.at[1, chunk, part], c_send.at[k, i], c_recv.at[k, i], at.partner
            )
            for i, chunk in enumerate(order)
        ]
        for k, part in enumerate((low, high))
    ]
    own_high.start()
    x_high[0].start()
    yield
    x_low.start()
    own_high.relay()
    own_high.near()
    x_high[1].start()
    x_high[2].start()
    own_low.start()
    x_low.wait_recv()
    next_low.start()
    across[0][0].start()
    own_high.far()
    x_high[3].start()
    own_low.relay()
    next_low.relay()
    x_high[0].wait_recv()
    across[1][0].start()
    next_low.near()
    own_low.near()
    across[0][1].start()
    across[0][2].start()
    for i in (1, 2):
        x_high[i].wait_recv()
        across[1][i].start()
    next_low.far()
    own_low.far()
    across[0][3].start()
    x_high[3].wait_recv()
    across[1][3].start()
    for spread in (own_high, next_low, own_low):
        spread.drain()
    x_low.wait_send()
    for copy in x_high:
        copy.wait_send()
    for copy in across[0] + across[1]:
        copy.wait()
    yield


def halo_kernel(
    shards, p_hbm, u_hbm, window, u_ref, p_ref, p_sem, u_sem, send, recv, q_send, q_recv, d_send, d_recv, c_send, c_recv
):
    at = Place(shards)
    partners = (at.partner, at.ahead, at.behind, at.right, at.left)
    signal_all(partners)
    blocks, columns, width = window.shape[2:]
    order = (at.y, at.last_y, at.next_y, at.far_y)

    def span(chunk):
        return pl.ds(pl.multiple_of(chunk * (blocks * width), width), blocks * width)

    loads = [
        pltpu.make_async_copy(p_hbm.at[:, span(chunk)], p_ref.at[:, span(chunk)], p_sem.at[i])
        for i, chunk in enumerate(order)
    ]
    for load in loads:
        load.start()
    weights = pltpu.make_async_copy(u_hbm, u_ref, u_sem)

    def cast(index):
        chunk = order[index]
        loads[index].wait()

        def one(i, carry):
            first = pl.multiple_of((chunk * blocks + i) * width, width)
            window[0, chunk, i] = p_ref[:, pl.ds(first, width)].astype(BF16)
            return carry

        loop(blocks, one)

    split = low_of(blocks)
    piece = split // 2
    parts = [pl.ds(0, piece), pl.ds(piece, piece), pl.ds(split, blocks - split)]
    pieces = [
        remote(window.at[0, at.y, parts[k]], window.at[2, at.y, parts[k]], q_send.at[k], q_recv.at[k], at.behind)
        for k in range(2)
    ]
    direct = [
        remote(window.at[0, chunk, parts[2]], window.at[2, chunk, parts[2]], d_send.at[i], d_recv.at[i], at.behind)
        for i, chunk in enumerate(order)
    ]
    spreads = [Spread(at, window.at[2], k * piece, piece, send.at[k], recv.at[k]) for k in range(2)]
    source = 2 - 2 * at.odd
    across = [
        remote(window.at[source, chunk], window.at[1, chunk], c_send.at[i], c_recv.at[i], at.partner)
        for i, chunk in enumerate(order)
    ]
    cast(0)
    wait_all(partners)
    pieces[0].start()
    pieces[1].start()
    weights.start()
    for index in (1, 2, 3):
        cast(index)
    pieces[0].wait_recv()
    spreads[0].start()
    for copy in direct:
        copy.start()
    pieces[1].wait_recv()
    spreads[1].start()
    spreads[0].relay()
    direct[0].wait_recv()
    across[0].start()
    spreads[1].relay()
    for spread in spreads:
        spread.near()
    for i in (1, 2):
        direct[i].wait_recv()
        across[i].start()
    for spread in spreads:
        spread.far()
    direct[3].wait_recv()
    across[3].start()
    for spread in spreads:
        spread.drain()
    for copy in pieces + direct:
        copy.wait_send()
    for copy in across:
        copy.wait()
    weights.wait()


def pairs(*shapes):
    return [pltpu.SemaphoreType.DMA(shape) for shape in shapes for _ in range(2)]


HALO_SEMS = pairs((2, 6), (2,), (4,), (4,))
GATHER_SEMS = pairs((3, 6), (), (4,), (2, 4))
REDUCE_SEMS = pairs((4,), (3, 6), (4,), ())


def reduce_scratch(blocks, sub, width):
    return [
        pltpu.VMEM((RING, blocks, sub, width), BF16),
        pltpu.VMEM((2, RING, blocks, sub, width), BF16),
        pltpu.VMEM((3, 6, low_of(blocks) // 2, sub, width), BF16),
        pltpu.VMEM((RING, blocks - low_of(blocks), sub, width), BF16),
        pltpu.VMEM((low_of(blocks), sub, width), BF16),
        pltpu.VMEM((low_of(blocks), sub, width), BF16),
    ] + REDUCE_SEMS


class Fold:
    def __init__(self, at, plane, whole, landed, first, count, send, recv):
        self.at, self.plane, self.landed, self.first, self.half = at, plane, landed, first, count // 2
        low, high = pl.ds(first, self.half), pl.ds(first + self.half, self.half)
        routes = (
            (at.far_y, low, at.right),
            (at.far_y, high, at.left),
            (at.next_y, high, at.right),
            (at.last_y, low, at.left),
            (at.next_y, low, at.right),
            (at.last_y, high, at.left),
        )
        self.copies, self.soon = (
            [
                remote(source.at[chunk, part], landed.at[i, pl.ds(0, self.half)], send.at[i], recv.at[i], device)
                for i, (chunk, part, device) in enumerate(routes[:most])
            ]
            for source, most in ((plane, 6), (whole, 4 if whole is not None else 0))
        )

    def far(self):
        self.copies[0].start()
        self.copies[1].start()

    def next(self):
        self.copies[2].start()

    def last(self):
        self.copies[3].start()

    def begin(self):
        for copy in self.soon:
            copy.start()

    def relay(self):
        for slot, chunk, first in ((0, self.at.next_y, self.first), (1, self.at.last_y, self.first + self.half)):
            self.copies[slot].wait_recv()

            def one(i, carry, slot=slot, chunk=chunk, first=first):
                term = self.plane[chunk, first + i].astype(F32) + self.landed[slot, i].astype(F32)
                self.plane[chunk, first + i] = term.astype(BF16)
                return carry

            loop(self.half, one)
            self.copies[slot + 4].start()

    def result(self, take):
        for offset, slots in ((0, (3, 4)), (self.half, (2, 5))):
            for slot in slots:
                self.copies[slot].wait_recv()

            def one(i, carry, offset=offset, slots=slots):
                value = self.plane[self.at.y, self.first + offset + i].astype(F32)
                for slot in slots:
                    value += self.landed[slot, i].astype(F32)
                take(offset + i, value)
                return carry

            loop(self.half, one)

    def drain(self):
        for copy in self.copies:
            copy.wait_send()


def reduce(
    at, finish, beside,
    part, crossed, total, landed, behind, outgoing, incoming,
    c_send, c_recv, send, recv, h_send, h_recv, low_send, low_recv,
):
    count = crossed.shape[1]
    split = low_of(count)
    high = count - split
    order = (at.far_y, at.next_y, at.last_y, at.y)
    across = [
        remote(part.at[1, chunk], crossed.at[chunk], c_send.at[i], c_recv.at[i], at.partner)
        for i, chunk in enumerate(order)
    ]
    ahead_low = Fold(at, total.at[1], part.at[2], landed.at[0], 0, split, send.at[0], recv.at[0])
    own_low = Fold(at, total.at[0], part.at[0], landed.at[1], 0, split, send.at[1], recv.at[1])
    own_high = Fold(at, total.at[0], None, landed.at[2], split, high, send.at[2], recv.at[2])
    x_high, x_soon = (
        [
            remote(source.at[chunk, pl.ds(split, high)], behind.at[chunk], h_send.at[i], h_recv.at[i], at.ahead)
            for i, chunk in enumerate(order)
        ]
        for source in (total.at[1], part.at[2])
    )
    x_low = remote(outgoing, incoming, low_send, low_recv, at.ahead)
    for copy in across:
        copy.start()

    @pl.when(at.odd == 1)
    def _():
        for copy in x_soon[:1]:
            copy.start()
        ahead_low.begin()
        for copy in x_soon[1:]:
            copy.start()

    @pl.when(at.odd == 0)
    def _():
        own_low.begin()

    def combine(index):
        chunk = order[index]
        joined, kept = 1 - at.odd, at.odd
        across[index].wait_recv()

        def one(i, carry):
            term = part[2 * joined, chunk, i].astype(F32) + crossed[chunk, i].astype(F32)
            total[joined, chunk, i] = term.astype(BF16)
            total[kept, chunk, i] = part[2 * kept, chunk, i]
            return carry

        loop(count, one)

    def join(index):
        chunk = order[index]
        x_high[index].wait_recv()

        def one(i, carry):
            term = total[0, chunk, split + i].astype(F32) + behind[chunk, i].astype(F32)
            total[0, chunk, split + i] = term.astype(BF16)
            return carry

        loop(high, one)

    def send_on(i, value):
        outgoing[i] = value.astype(BF16)

    for index in range(4):
        combine(index)

        @pl.when(at.odd == 0)
        def _(index=index):
            x_high[index].start()
            if index < 3:
                (ahead_low.far, ahead_low.next, ahead_low.last)[index]()

        @pl.when(at.odd == 1)
        def _(index=index):
            if index < 3:
                (own_low.far, own_low.next, own_low.last)[index]()

        if index == 0:
            beside[0]()
    beside[1]()
    ahead_low.relay()
    own_low.relay()
    join(0)
    own_high.far()
    ahead_low.result(send_on)
    x_low.start()
    beside[2]()
    join(1)
    own_high.next()
    join(2)
    own_high.last()
    beside[3]()
    own_high.relay()
    join(3)
    beside[4]()
    own_high.result(lambda i, value: finish(split + i, 0.5 * value))
    beside[5]()
    x_low.wait_recv()
    own_low.result(lambda i, value: finish(i, 0.5 * (value + incoming[i].astype(F32))))

    def drain():
        for copy in across + x_high + [x_low]:
            copy.wait_send()
        for fold in (ahead_low, own_low, own_high):
            fold.drain()

    return drain


def terms(x_ref, back, along, deg, deg_along, take, dots=None):
    rows, columns, width = along.shape
    for d in (1, 0, 2):

        def one(i, carry, d=d):
            at_i = d * rows + i
            weight, minus, x = deg[at_i], back[at_i], x_ref[at_i].astype(F32)
            if d == 0:
                weight += deg_along[i]
                minus += along[i]
            term = jnp.concatenate([weight] * (columns // 8), axis=0) * x - minus
            take(d, i, x, term)
            return carry if dots is None else carry + x * term

        total = loop(rows, one, 0 if dots is None else dots)
        dots = dots if dots is None else total
    return dots


def middle_kernel(shards, x_ref, back, along, deg, deg_along, window, part, *scratch):
    at = Place(shards)
    partners = (at.partner, at.ahead, at.behind, at.right, at.left)
    signal_all(partners)
    quarter = window.shape[2]

    def take(d, i, x, term):
        part[d, i // quarter, rem(i, quarter)] = term.astype(BF16)

    terms(x_ref, back, along, deg, deg_along, take)
    wait_all(partners)

    def keep(i, value):
        window[0, at.y, i] = value.astype(BF16)

    count = 6 + len(REDUCE_SEMS)
    steps = gather(at, window, *scratch[count:])
    drain = reduce(at, keep, [nothing] * 5 + [lambda: next(steps)], part, *scratch[:count])
    next(steps)
    drain()


def last_kernel(
    shards, groups, w_ref, back, along, deg, deg_along, p_ref, x_ref, r_ref,
    part, h_ref, hq_ref, sums, heard, s_send, s_recv, *scratch,
):
    at = Place(shards)
    opposite = (at.s, at.far_y)
    peers = [at.around(stride, size, step) for stride, size in groups for step in range(1, size)]
    partners = [at.partner, at.ahead, at.behind, at.right, at.left, opposite] + peers
    signal_all(partners)
    _, blocks, sub, width = h_ref.shape

    def take(d, i, x, term):
        for g in range(RING):
            part[d, g, i] = term[g * sub : (g + 1) * sub].astype(BF16)
            if d == 0:
                h_ref[g, i] = x[g * sub : (g + 1) * sub].astype(BF16)

    dots = terms(w_ref, back, along, deg, deg_along, take, jnp.zeros((RING * sub, width), F32))
    for g in range(RING):
        hq_ref[g] = 0.5 * dots[g * sub : (g + 1) * sub]
    wait_all(partners)
    zero = jnp.zeros((sub, width), F32)
    lanes = lax.broadcasted_iota(jnp.int32, (sub, width), 1)
    rounds = [[(hq_ref.at[y], at_y) for y, at_y in ((at.next_y, at.right), (at.last_y, at.left), (at.far_y, opposite))]]
    rounds += [[(sums, at.around(stride, size, step)) for step in range(1, size)] for stride, size in groups]
    messages = []
    for one_round in rounds:
        first = sum(map(len, messages))
        messages.append(
            [
                remote(source, heard.at[slot], s_send.at[slot], s_recv.at[slot], device)
                for slot, (source, device) in enumerate(one_round, first)
            ]
        )

    def tell(k):
        for message in messages[k]:
            message.start()

    def hear(k):
        for message in messages[k]:
            message.wait_recv()
        for message in messages[k]:
            message.wait_send()
        first = sum(map(len, messages[:k]))
        return sum((heard[slot] for slot in range(first, first + len(messages[k]))), zero)

    def p_of(i):
        return p_ref[pl.ds(pl.multiple_of(at.y * sub, sub), sub), pl.ds(pl.multiple_of(i * width, width), width)]

    def h_of(i):
        return h_ref[at.y, i].astype(F32)

    def square():
        def one(i, carry):
            p, h = p_of(i), h_of(i)
            return carry[0] + p * p, carry[1] + p * h, carry[2] + h * h

        packed = zero
        for k, value in enumerate(loop(blocks, one, (zero, zero, zero))):
            packed = jnp.where(lanes == k, jnp.sum(value, axis=1, keepdims=True), packed)
        sums[...] = packed

    def start_sums():
        value = jnp.sum(hear(0) + hq_ref[at.y], axis=1, keepdims=True)
        sums[...] = jnp.where(lanes == 3, value, sums[...])
        tell(1)

    def pass_sums():
        sums[...] = sums[...] + hear(1)
        tell(2)

    scale = []

    def end_sums():
        packed = sums[...] + hear(2)
        pp, ph, hh, hq = (
            jnp.broadcast_to(jnp.sum(jnp.where(lanes == k, packed, 0.0), axis=1, keepdims=True), (sub, width))
            for k in range(4)
        )
        first = pp / (pp + ph)
        rest = ph / (pp + ph)
        norm = rest * rest * pp - 2.0 * rest * first * ph + first * first * hh
        a = rest + norm / pp
        c = first
        curve = a * a * pp + a * (a - 2.0 * c) * ph + c * (c - 2.0 * a) * hh + c * c * hq
        second = norm / curve
        x_p, x_h = first + second * a, second * c
        scale.extend((rest - second * a, first + second * (a - c), second * c))

        def one(i, carry):
            x_ref[:, pl.ds(pl.multiple_of(i * width, width), width)] = x_p * p_of(i) - x_h * h_of(i)
            return carry

        loop(blocks, one)

    def keep(i, q):
        r_p, r_h, r_q = scale
        r_ref[:, pl.ds(pl.multiple_of(i * width, width), width)] = r_p * p_of(i) - r_h * h_of(i) + r_q * q

    tell(0)
    drain = reduce(at, keep, [square, start_sums, pass_sums, nothing, end_sums, nothing], part, *scratch)
    drain()


def apply_kernel(first, nbr_ref, u_ref, x_ref, back, along, *weights):
    columns, width = x_ref.shape[1:]
    rows = u_ref.shape[0]
    base = lax.axis_index("rows") * rows
    if first:
        deg, deg_along = weights

    def clear(i, carry):
        back[i] = jnp.zeros((columns, width), F32)
        if first:
            deg[i] = jnp.zeros((8, width), F32)
        return carry

    loop(3 * rows, clear)
    ones = jnp.ones((ONES, 2 * width), BF16)

    def row(b, carry):
        t0, t1 = nbr_ref[0, b] - base, nbr_ref[1, b] - base
        pair = jnp.concatenate([u_ref[b, 0], u_ref[b, 1]], axis=1)
        own = x_ref[b]
        far = jnp.concatenate([x_ref[t0], x_ref[t1]], axis=1)
        if first:
            own = jnp.concatenate([own, ones[:, :width]], axis=0)
            far = jnp.concatenate([far, ones], axis=0)
        forward = lax.dot_general(far, pair, (((1,), (1,)), ((), ())), preferred_element_type=F32)
        returned = lax.dot_general(own, pair, (((1,), (0,)), ((), ())), preferred_element_type=F32)
        along[b] = forward[:columns]
        back[t0] += returned[:columns, :width]
        back[t1] += returned[:columns, width:]
        if first:
            deg_along[b] = forward[columns : columns + 8]
            deg[t0] += returned[columns : columns + 8, :width]
            deg[t1] += returned[columns : columns + 8, width:]
        return carry

    lax.fori_loop(0, rows, row, 0, unroll=min(ROW_UNROLL, rows))


def apply(first, nbr, upper, window):
    rows, slots, width, _ = upper.shape
    columns = window.shape[-2]
    out_shape = [
        jax.ShapeDtypeStruct((count, lines, width), F32)
        for lines in ((columns, 8) if first else (columns,))
        for count in (3 * rows, rows)
    ]
    return pl.pallas_call(
        functools.partial(apply_kernel, first),
        out_shape=out_shape,
        in_specs=[pl.BlockSpec(memory_space=pltpu.SMEM), VMEM, VMEM],
        out_specs=[VMEM] * len(out_shape),
        compiler_params=pltpu.CompilerParams(vmem_limit_bytes=LIMITS["apply"]),
        cost_estimate=pl.CostEstimate(
            flops=4 * rows * slots * width * width * columns, transcendentals=0, bytes_accessed=upper.size * 2
        ),
        name="apply_first" if first else "apply_second",
    )(nbr, upper, window.reshape(3 * rows, columns, width))


def talk(body, out_shape, scratch, collective_id, name, *args, in_specs=None):
    return pl.pallas_call(
        body,
        out_shape=out_shape,
        in_specs=in_specs or [VMEM] * len(args),
        out_specs=jax.tree.map(lambda _: VMEM, out_shape),
        scratch_shapes=scratch,
        compiler_params=pltpu.CompilerParams(
            collective_id=collective_id, has_side_effects=True, vmem_limit_bytes=LIMITS[name]
        ),
        cost_estimate=pl.CostEstimate(flops=0, transcendentals=0, bytes_accessed=TRAFFIC[name]),
        name=name,
    )(*args)


def per_device(pass_rates, upper_blocks, neighbours):
    rows, _, width, _ = upper_blocks.shape
    columns = pass_rates.shape[0]
    shards = lax.axis_size("rows")
    if lax.axis_size("cols") != RING or shards % 8:
        raise ValueError("mesh shape")
    quarter, sub = rows // RING, columns // RING
    groups = [(1, 8), (8, shards // 8)]
    messages = RING - 1 + sum(size - 1 for _, size in groups)
    nbr = neighbours.T
    window_shape = jax.ShapeDtypeStruct((3, RING, quarter, columns, width), BF16)

    window, upper = talk(
        functools.partial(halo_kernel, shards),
        (window_shape, jax.ShapeDtypeStruct(upper_blocks.shape, BF16)),
        [pltpu.VMEM(pass_rates.shape, F32), pltpu.SemaphoreType.DMA((RING,)), pltpu.SemaphoreType.DMA] + HALO_SEMS,
        0,
        "halo",
        pltpu.with_memory_space_constraint(pass_rates, pltpu.HBM),
        pltpu.with_memory_space_constraint(upper_blocks, pltpu.HBM),
        in_specs=[pl.BlockSpec(memory_space=pltpu.HBM)] * 2,
    )
    flat = lambda w: w.reshape(3 * rows, columns, width)
    back, along, deg, deg_along = apply(True, nbr, upper, window)
    window = talk(
        functools.partial(middle_kernel, shards),
        window_shape,
        [pltpu.VMEM(window_shape.shape, BF16)] + reduce_scratch(quarter, columns, width) + GATHER_SEMS,
        1,
        "middle",
        flat(window),
        back,
        along,
        deg,
        deg_along,
    )
    back, along = apply(False, nbr, upper, window)
    out_shape = jax.ShapeDtypeStruct((sub, rows * width), F32)
    return talk(
        functools.partial(last_kernel, shards, groups),
        (out_shape, out_shape),
        [
            pltpu.VMEM((3, RING, rows, sub, width), BF16),
            pltpu.VMEM((RING, rows, sub, width), BF16),
            pltpu.VMEM((RING, sub, width), F32),
            pltpu.VMEM((sub, width), F32),
            pltpu.VMEM((messages, sub, width), F32),
        ]
        + pairs((messages,))
        + reduce_scratch(rows, sub, width),
        2,
        "last",
        flat(window),
        back,
        along,
        deg,
        deg_along,
        pass_rates,
    )


def solution(mesh):
    in_specs = (P(None, "rows"), P("rows", "cols", None, None), P("rows", "cols"))
    out_specs = (P("cols", "rows"), P("cols", "rows"))
    return jax.shard_map(per_device, mesh=mesh, in_specs=in_specs, out_specs=out_specs, check_vma=False)
```

```python
import functools

import jax
import jax.numpy as jnp
from jax import lax
from jax.experimental import pallas as pl
from jax.experimental.pallas import tpu as pltpu
from jax.sharding import PartitionSpec as P

MESH = pl.DeviceIdType.MESH
F32 = jnp.float32
BF16 = jnp.bfloat16
RING = 4
VMEM = pl.BlockSpec(memory_space=pltpu.VMEM)
MIB = 2**20
ONES = 16
UNROLL = 8
ROW_UNROLL = 128
TRAFFIC = {"halo": 60 * MIB, "middle": 150 * MIB, "last": 120 * MIB}
LIMITS = {"halo": 20 * MIB, "apply": 26 * MIB, "middle": 30 * MIB, "last": 32 * MIB}


def rem(value, count):
    return lax.rem(value, jnp.int32(count))


def loop(count, body, carry=0):
    unroll = max(n for n in range(1, UNROLL + 1) if count % n == 0)
    return lax.fori_loop(0, count, body, carry, unroll=unroll)


def nothing():
    pass


def low_of(count):
    return count * 5 // 16 * 2


class Place:
    def __init__(self, shards):
        self.shards = shards
        self.s = lax.axis_index("rows")
        self.y = lax.axis_index("cols")
        self.odd = rem(self.s, 2)
        self.next_y = rem(self.y + 1, RING)
        self.last_y = rem(self.y + RING - 1, RING)
        self.far_y = rem(self.y + 2, RING)
        self.partner = (self.s + 1 - 2 * self.odd, self.y)
        self.ahead = (rem(self.s + 2, shards), self.y)
        self.behind = (rem(self.s + shards - 2, shards), self.y)
        self.right = (self.s, self.next_y)
        self.left = (self.s, self.last_y)

    def around(self, stride, size, step):
        at = rem(self.s // stride, size)
        return (self.s + (rem(at + step, size) - at) * stride, self.y)


def signal_all(devices):
    barrier = pltpu.get_barrier_semaphore()
    for device in devices:
        pl.semaphore_signal(barrier, inc=1, device_id=device, device_id_type=MESH)


def wait_all(devices):
    pl.semaphore_wait(pltpu.get_barrier_semaphore(), len(devices))


def remote(src, dst, send_sem, recv_sem, device):
    return pltpu.make_async_remote_copy(
        src_ref=src, dst_ref=dst, send_sem=send_sem, recv_sem=recv_sem, device_id=device, device_id_type=MESH
    )


class Spread:
    def __init__(self, at, plane, first, count, send, recv):
        half = count // 2
        low, high = pl.ds(first, half), pl.ds(first + half, half)
        routes = (
            (at.y, low, at.right),
            (at.y, high, at.left),
            (at.y, high, at.right),
            (at.y, low, at.left),
            (at.last_y, low, at.right),
            (at.next_y, high, at.left),
        )
        self.copies = [
            remote(plane.at[chunk, part], plane.at[chunk, part], send.at[i], recv.at[i], device)
            for i, (chunk, part, device) in enumerate(routes)
        ]

    def start(self):
        for copy in self.copies[:4]:
            copy.start()

    def relay(self):
        for first, second in ((0, 4), (1, 5)):
            self.copies[first].wait_recv()
            self.copies[second].start()

    def near(self):
        for i in (2, 3):
            self.copies[i].wait_recv()

    def far(self):
        for i in (4, 5):
            self.copies[i].wait_recv()

    def drain(self):
        for copy in self.copies:
            copy.wait_send()


def gather(at, window, send, recv, low_send, low_recv, high_send, high_recv, c_send, c_recv):
    count = window.shape[2]
    split = low_of(count)
    low, high = pl.ds(0, split), pl.ds(split, count - split)
    order = (at.y, at.last_y, at.next_y, at.far_y)
    own_high = Spread(at, window.at[0], split, count - split, send.at[0], recv.at[0])
    next_low = Spread(at, window.at[2], 0, split, send.at[1], recv.at[1])
    own_low = Spread(at, window.at[0], 0, split, send.at[2], recv.at[2])
    x_low = remote(window.at[0, at.y, low], window.at[2, at.y, low], low_send, low_recv, at.behind)
    x_high = [
        remote(window.at[0, chunk, high], window.at[2, chunk, high], high_send.at[i], high_recv.at[i], at.behind)
        for i, chunk in enumerate(order)
    ]
    source = 2 - 2 * at.odd
    across = [
        [
            remote(
                window.at[source, chunk, part], window.at[1, chunk, part], c_send.at[k, i], c_recv.at[k, i], at.partner
            )
            for i, chunk in enumerate(order)
        ]
        for k, part in enumerate((low, high))
    ]
    own_high.start()
    x_high[0].start()
    yield
    x_low.start()
    own_high.relay()
    own_high.near()
    x_high[1].start()
    x_high[2].start()
    own_low.start()
    x_low.wait_recv()
    next_low.start()
    across[0][0].start()
    own_high.far()
    x_high[3].start()
    own_low.relay()
    next_low.relay()
    x_high[0].wait_recv()
    across[1][0].start()
    next_low.near()
    own_low.near()
    across[0][1].start()
    across[0][2].start()
    for i in (1, 2):
        x_high[i].wait_recv()
        across[1][i].start()
    next_low.far()
    own_low.far()
    across[0][3].start()
    x_high[3].wait_recv()
    across[1][3].start()
    for spread in (own_high, next_low, own_low):
        spread.drain()
    x_low.wait_send()
    for copy in x_high:
        copy.wait_send()
    for copy in across[0] + across[1]:
        copy.wait()
    yield


def halo_kernel(
    shards, p_hbm, u_hbm, window, u_ref, p_ref, p_sem, u_sem, send, recv, q_send, q_recv, d_send, d_recv, c_send, c_recv
):
    at = Place(shards)
    partners = (at.partner, at.ahead, at.behind, at.right, at.left)
    signal_all(partners)
    blocks, columns, width = window.shape[2:]
    order = (at.y, at.last_y, at.next_y, at.far_y)

    def span(chunk):
        return pl.ds(pl.multiple_of(chunk * (blocks * width), width), blocks * width)

    loads = [
        pltpu.make_async_copy(p_hbm.at[:, span(chunk)], p_ref.at[:, span(chunk)], p_sem.at[i])
        for i, chunk in enumerate(order)
    ]
    for load in loads:
        load.start()
    weights = pltpu.make_async_copy(u_hbm, u_ref, u_sem)

    def cast(index):
        chunk = order[index]
        loads[index].wait()

        def one(i, carry):
            first = pl.multiple_of((chunk * blocks + i) * width, width)
            window[0, chunk, i] = p_ref[:, pl.ds(first, width)].astype(BF16)
            return carry

        loop(blocks, one)

    split = low_of(blocks)
    piece = split // 2
    parts = [pl.ds(0, piece), pl.ds(piece, piece), pl.ds(split, blocks - split)]
    pieces = [
        remote(window.at[0, at.y, parts[k]], window.at[2, at.y, parts[k]], q_send.at[k], q_recv.at[k], at.behind)
        for k in range(2)
    ]
    direct = [
        remote(window.at[0, chunk, parts[2]], window.at[2, chunk, parts[2]], d_send.at[i], d_recv.at[i], at.behind)
        for i, chunk in enumerate(order)
    ]
    spreads = [Spread(at, window.at[2], k * piece, piece, send.at[k], recv.at[k]) for k in range(2)]
    source = 2 - 2 * at.odd
    across = [
        remote(window.at[source, chunk], window.at[1, chunk], c_send.at[i], c_recv.at[i], at.partner)
        for i, chunk in enumerate(order)
    ]
    cast(0)
    wait_all(partners)
    pieces[0].start()
    pieces[1].start()
    weights.start()
    for index in (1, 2, 3):
        cast(index)
    pieces[0].wait_recv()
    spreads[0].start()
    for copy in direct:
        copy.start()
    pieces[1].wait_recv()
    spreads[1].start()
    spreads[0].relay()
    direct[0].wait_recv()
    across[0].start()
    spreads[1].relay()
    for spread in spreads:
        spread.near()
    for i in (1, 2):
        direct[i].wait_recv()
        across[i].start()
    for spread in spreads:
        spread.far()
    direct[3].wait_recv()
    across[3].start()
    for spread in spreads:
        spread.drain()
    for copy in pieces + direct:
        copy.wait_send()
    for copy in across:
        copy.wait()
    weights.wait()


def pairs(*shapes):
    return [pltpu.SemaphoreType.DMA(shape) for shape in shapes for _ in range(2)]


HALO_SEMS = pairs((2, 6), (2,), (4,), (4,))
GATHER_SEMS = pairs((3, 6), (), (4,), (2, 4))
REDUCE_SEMS = pairs((4,), (3, 6), (4,), ())


def reduce_scratch(blocks, sub, width):
    return [
        pltpu.VMEM((RING, blocks, sub, width), BF16),
        pltpu.VMEM((2, RING, blocks, sub, width), BF16),
        pltpu.VMEM((3, 6, low_of(blocks) // 2, sub, width), BF16),
        pltpu.VMEM((RING, blocks - low_of(blocks), sub, width), BF16),
        pltpu.VMEM((low_of(blocks), sub, width), BF16),
        pltpu.VMEM((low_of(blocks), sub, width), BF16),
    ] + REDUCE_SEMS


class Fold:
    def __init__(self, at, plane, whole, landed, first, count, send, recv):
        self.at, self.plane, self.landed, self.first, self.half = at, plane, landed, first, count // 2
        low, high = pl.ds(first, self.half), pl.ds(first + self.half, self.half)
        routes = (
            (at.far_y, low, at.right),
            (at.far_y, high, at.left),
            (at.next_y, high, at.right),
            (at.last_y, low, at.left),
            (at.next_y, low, at.right),
            (at.last_y, high, at.left),
        )
        self.copies, self.soon = (
            [
                remote(source.at[chunk, part], landed.at[i, pl.ds(0, self.half)], send.at[i], recv.at[i], device)
                for i, (chunk, part, device) in enumerate(routes[:most])
            ]
            for source, most in ((plane, 6), (whole, 4 if whole is not None else 0))
        )

    def far(self):
        self.copies[0].start()
        self.copies[1].start()

    def next(self):
        self.copies[2].start()

    def last(self):
        self.copies[3].start()

    def begin(self):
        for copy in self.soon:
            copy.start()

    def relay(self):
        for slot, chunk, first in ((0, self.at.next_y, self.first), (1, self.at.last_y, self.first + self.half)):
            self.copies[slot].wait_recv()

            def one(i, carry, slot=slot, chunk=chunk, first=first):
                term = self.plane[chunk, first + i].astype(F32) + self.landed[slot, i].astype(F32)
                self.plane[chunk, first + i] = term.astype(BF16)
                return carry

            loop(self.half, one)
            self.copies[slot + 4].start()

    def result(self, take):
        for offset, slots in ((0, (3, 4)), (self.half, (2, 5))):
            for slot in slots:
                self.copies[slot].wait_recv()

            def one(i, carry, offset=offset, slots=slots):
                value = self.plane[self.at.y, self.first + offset + i].astype(F32)
                for slot in slots:
                    value += self.landed[slot, i].astype(F32)
                take(offset + i, value)
                return carry

            loop(self.half, one)

    def drain(self):
        for copy in self.copies:
            copy.wait_send()


def reduce(
    at, finish, late, beside,
    part, crossed, total, landed, behind, outgoing, incoming,
    c_send, c_recv, send, recv, h_send, h_recv, low_send, low_recv,
):
    count = crossed.shape[1]
    split = low_of(count)
    high = count - split
    order = (at.far_y, at.next_y, at.last_y, at.y)
    across = [
        remote(part.at[1, chunk], crossed.at[chunk], c_send.at[i], c_recv.at[i], at.partner)
        for i, chunk in enumerate(order)
    ]
    ahead_low = Fold(at, total.at[1], part.at[2], landed.at[0], 0, split, send.at[0], recv.at[0])
    own_low = Fold(at, total.at[0], part.at[0], landed.at[1], 0, split, send.at[1], recv.at[1])
    own_high = Fold(at, total.at[0], None, landed.at[2], split, high, send.at[2], recv.at[2])
    x_high, x_soon = (
        [
            remote(source.at[chunk, pl.ds(split, high)], behind.at[chunk], h_send.at[i], h_recv.at[i], at.ahead)
            for i, chunk in enumerate(order)
        ]
        for source in (total.at[1], part.at[2])
    )
    x_low = remote(outgoing, incoming, low_send, low_recv, at.ahead)
    for copy in across:
        copy.start()

    @pl.when(at.odd == 0)
    def _():
        own_low.begin()

    late()

    @pl.when(at.odd == 1)
    def _():
        for copy in x_soon[:1]:
            copy.start()
        ahead_low.begin()
        for copy in x_soon[1:]:
            copy.start()

    def combine(index):
        chunk = order[index]
        joined, kept = 1 - at.odd, at.odd
        across[index].wait_recv()

        def one(i, carry):
            term = part[2 * joined, chunk, i].astype(F32) + crossed[chunk, i].astype(F32)
            total[joined, chunk, i] = term.astype(BF16)
            total[kept, chunk, i] = part[2 * kept, chunk, i]
            return carry

        loop(count, one)

    def join(index):
        chunk = order[index]
        x_high[index].wait_recv()

        def one(i, carry):
            term = total[0, chunk, split + i].astype(F32) + behind[chunk, i].astype(F32)
            total[0, chunk, split + i] = term.astype(BF16)
            return carry

        loop(high, one)

    def send_on(i, value):
        outgoing[i] = value.astype(BF16)

    for index in range(4):
        combine(index)

        @pl.when(at.odd == 0)
        def _(index=index):
            x_high[index].start()
            if index < 3:
                (ahead_low.far, ahead_low.next, ahead_low.last)[index]()

        @pl.when(at.odd == 1)
        def _(index=index):
            if index < 3:
                (own_low.far, own_low.next, own_low.last)[index]()

        if index == 0:
            beside[0]()
    beside[1]()
    ahead_low.relay()
    own_low.relay()
    join(0)
    own_high.far()
    ahead_low.result(send_on)
    x_low.start()
    beside[2]()
    join(1)
    own_high.next()
    join(2)
    own_high.last()
    beside[3]()
    own_high.relay()
    join(3)
    beside[4]()
    own_high.result(lambda i, value: finish(split + i, 0.5 * value))
    beside[5]()
    x_low.wait_recv()
    own_low.result(lambda i, value: finish(i, 0.5 * (value + incoming[i].astype(F32))))

    def drain():
        for copy in across + x_high + [x_low]:
            copy.wait_send()
        for fold in (ahead_low, own_low, own_high):
            fold.drain()

    return drain


def terms(planes, x_ref, back, along, deg, deg_along, take, dots=None):
    rows, columns, width = along.shape
    for d in planes:

        def one(i, carry, d=d):
            at_i = d * rows + i
            weight, minus, x = deg[at_i], back[at_i], x_ref[at_i].astype(F32)
            if d == 0:
                weight += deg_along[i]
                minus += along[i]
            term = jnp.concatenate([weight] * (columns // 8), axis=0) * x - minus
            take(d, i, x, term)
            return carry if dots is None else carry + x * term

        total = loop(rows, one, 0 if dots is None else dots)
        dots = dots if dots is None else total
    return dots


def middle_kernel(shards, x_ref, back, along, deg, deg_along, window, part, *scratch):
    at = Place(shards)
    partners = (at.partner, at.ahead, at.behind, at.right, at.left)
    signal_all(partners)
    quarter = window.shape[2]

    def take(d, i, x, term):
        part[d, i // quarter, rem(i, quarter)] = term.astype(BF16)

    given = (x_ref, back, along, deg, deg_along, take)
    terms((1, 0), *given)
    wait_all(partners)

    def keep(i, value):
        window[0, at.y, i] = value.astype(BF16)

    count = 6 + len(REDUCE_SEMS)
    steps = gather(at, window, *scratch[count:])
    drain = reduce(at, keep, lambda: terms((2,), *given), [nothing] * 5 + [lambda: next(steps)], part, *scratch[:count])
    next(steps)
    drain()


def last_kernel(
    shards, groups, w_ref, back, along, deg, deg_along, p_ref, x_ref, r_ref,
    part, h_ref, hq_ref, sums, heard, s_send, s_recv, *scratch,
):
    at = Place(shards)
    opposite = (at.s, at.far_y)
    peers = [at.around(stride, size, step) for stride, size in groups for step in range(1, size)]
    partners = [at.partner, at.ahead, at.behind, at.right, at.left, opposite] + peers
    signal_all(partners)
    _, blocks, sub, width = h_ref.shape

    def take(d, i, x, term):
        for g in range(RING):
            part[d, g, i] = term[g * sub : (g + 1) * sub].astype(BF16)
            if d == 0:
                h_ref[g, i] = x[g * sub : (g + 1) * sub].astype(BF16)

    given = (w_ref, back, along, deg, deg_along, take)
    dots = terms((1, 0), *given, jnp.zeros((RING * sub, width), F32))
    wait_all(partners)
    zero = jnp.zeros((sub, width), F32)
    lanes = lax.broadcasted_iota(jnp.int32, (sub, width), 1)
    rounds = [[(hq_ref.at[y], at_y) for y, at_y in ((at.next_y, at.right), (at.last_y, at.left), (at.far_y, opposite))]]
    rounds += [[(sums, at.around(stride, size, step)) for step in range(1, size)] for stride, size in groups]
    messages = []
    for one_round in rounds:
        first = sum(map(len, messages))
        messages.append(
            [
                remote(source, heard.at[slot], s_send.at[slot], s_recv.at[slot], device)
                for slot, (source, device) in enumerate(one_round, first)
            ]
        )

    def tell(k):
        for message in messages[k]:
            message.start()

    def hear(k):
        for message in messages[k]:
            message.wait_recv()
        for message in messages[k]:
            message.wait_send()
        first = sum(map(len, messages[:k]))
        return sum((heard[slot] for slot in range(first, first + len(messages[k]))), zero)

    def p_of(i):
        return p_ref[pl.ds(pl.multiple_of(at.y * sub, sub), sub), pl.ds(pl.multiple_of(i * width, width), width)]

    def h_of(i):
        return h_ref[at.y, i].astype(F32)

    def square():
        def one(i, carry):
            p, h = p_of(i), h_of(i)
            return carry[0] + p * p, carry[1] + p * h, carry[2] + h * h

        packed = zero
        for k, value in enumerate(loop(blocks, one, (zero, zero, zero))):
            packed = jnp.where(lanes == k, jnp.sum(value, axis=1, keepdims=True), packed)
        sums[...] = packed

    def start_sums():
        value = jnp.sum(hear(0) + hq_ref[at.y], axis=1, keepdims=True)
        sums[...] = jnp.where(lanes == 3, value, sums[...])
        tell(1)

    def pass_sums():
        sums[...] = sums[...] + hear(1)
        tell(2)

    scale = []

    def end_sums():
        packed = sums[...] + hear(2)
        pp, ph, hh, hq = (
            jnp.broadcast_to(jnp.sum(jnp.where(lanes == k, packed, 0.0), axis=1, keepdims=True), (sub, width))
            for k in range(4)
        )
        first = pp / (pp + ph)
        rest = ph / (pp + ph)
        norm = rest * rest * pp - 2.0 * rest * first * ph + first * first * hh
        a = rest + norm / pp
        c = first
        curve = a * a * pp + a * (a - 2.0 * c) * ph + c * (c - 2.0 * a) * hh + c * c * hq
        second = norm / curve
        x_p, x_h = first + second * a, second * c
        scale.extend((rest - second * a, first + second * (a - c), second * c))

        def one(i, carry):
            x_ref[:, pl.ds(pl.multiple_of(i * width, width), width)] = x_p * p_of(i) - x_h * h_of(i)
            return carry

        loop(blocks, one)

    def keep(i, q):
        r_p, r_h, r_q = scale
        r_ref[:, pl.ds(pl.multiple_of(i * width, width), width)] = r_p * p_of(i) - r_h * h_of(i) + r_q * q

    def late():
        total = terms((2,), *given, dots)
        for g in range(RING):
            hq_ref[g] = 0.5 * total[g * sub : (g + 1) * sub]
        tell(0)

    drain = reduce(at, keep, late, [square, start_sums, pass_sums, nothing, end_sums, nothing], part, *scratch)
    drain()


def apply_kernel(first, nbr_ref, u_ref, x_ref, back, along, *weights):
    columns, width = x_ref.shape[1:]
    rows = u_ref.shape[0]
    base = lax.axis_index("rows") * rows
    if first:
        deg, deg_along = weights

    def clear(i, carry):
        back[i] = jnp.zeros((columns, width), F32)
        if first:
            deg[i] = jnp.zeros((8, width), F32)
        return carry

    loop(3 * rows, clear)
    ones = jnp.ones((ONES, 2 * width), BF16)

    def row(b, carry):
        t0, t1 = nbr_ref[0, b] - base, nbr_ref[1, b] - base
        pair = jnp.concatenate([u_ref[b, 0], u_ref[b, 1]], axis=1)
        own = x_ref[b]
        far = jnp.concatenate([x_ref[t0], x_ref[t1]], axis=1)
        if first:
            own = jnp.concatenate([own, ones[:, :width]], axis=0)
            far = jnp.concatenate([far, ones], axis=0)
        forward = lax.dot_general(far, pair, (((1,), (1,)), ((), ())), preferred_element_type=F32)
        returned = lax.dot_general(own, pair, (((1,), (0,)), ((), ())), preferred_element_type=F32)
        along[b] = forward[:columns]
        back[t0] += returned[:columns, :width]
        back[t1] += returned[:columns, width:]
        if first:
            deg_along[b] = forward[columns : columns + 8]
            deg[t0] += returned[columns : columns + 8, :width]
            deg[t1] += returned[columns : columns + 8, width:]
        return carry

    lax.fori_loop(0, rows, row, 0, unroll=min(ROW_UNROLL, rows))


def apply(first, nbr, upper, window):
    rows, slots, width, _ = upper.shape
    columns = window.shape[-2]
    out_shape = [
        jax.ShapeDtypeStruct((count, lines, width), F32)
        for lines in ((columns, 8) if first else (columns,))
        for count in (3 * rows, rows)
    ]
    return pl.pallas_call(
        functools.partial(apply_kernel, first),
        out_shape=out_shape,
        in_specs=[pl.BlockSpec(memory_space=pltpu.SMEM), VMEM, VMEM],
        out_specs=[VMEM] * len(out_shape),
        compiler_params=pltpu.CompilerParams(vmem_limit_bytes=LIMITS["apply"]),
        cost_estimate=pl.CostEstimate(
            flops=4 * rows * slots * width * width * columns, transcendentals=0, bytes_accessed=upper.size * 2
        ),
        name="apply_first" if first else "apply_second",
    )(nbr, upper, window.reshape(3 * rows, columns, width))


def talk(body, out_shape, scratch, collective_id, name, *args, in_specs=None):
    return pl.pallas_call(
        body,
        out_shape=out_shape,
        in_specs=in_specs or [VMEM] * len(args),
        out_specs=jax.tree.map(lambda _: VMEM, out_shape),
        scratch_shapes=scratch,
        compiler_params=pltpu.CompilerParams(
            collective_id=collective_id, has_side_effects=True, vmem_limit_bytes=LIMITS[name]
        ),
        cost_estimate=pl.CostEstimate(flops=0, transcendentals=0, bytes_accessed=TRAFFIC[name]),
        name=name,
    )(*args)


def per_device(pass_rates, upper_blocks, neighbours):
    rows, _, width, _ = upper_blocks.shape
    columns = pass_rates.shape[0]
    shards = lax.axis_size("rows")
    if lax.axis_size("cols") != RING or shards % 8:
        raise ValueError("mesh shape")
    quarter, sub = rows // RING, columns // RING
    groups = [(1, 8), (8, shards // 8)]
    messages = RING - 1 + sum(size - 1 for _, size in groups)
    nbr = neighbours.T
    window_shape = jax.ShapeDtypeStruct((3, RING, quarter, columns, width), BF16)

    window, upper = talk(
        functools.partial(halo_kernel, shards),
        (window_shape, jax.ShapeDtypeStruct(upper_blocks.shape, BF16)),
        [pltpu.VMEM(pass_rates.shape, F32), pltpu.SemaphoreType.DMA((RING,)), pltpu.SemaphoreType.DMA] + HALO_SEMS,
        0,
        "halo",
        pltpu.with_memory_space_constraint(pass_rates, pltpu.HBM),
        pltpu.with_memory_space_constraint(upper_blocks, pltpu.HBM),
        in_specs=[pl.BlockSpec(memory_space=pltpu.HBM)] * 2,
    )
    flat = lambda w: w.reshape(3 * rows, columns, width)
    back, along, deg, deg_along = apply(True, nbr, upper, window)
    window = talk(
        functools.partial(middle_kernel, shards),
        window_shape,
        [pltpu.VMEM(window_shape.shape, BF16)] + reduce_scratch(quarter, columns, width) + GATHER_SEMS,
        1,
        "middle",
        flat(window),
        back,
        along,
        deg,
        deg_along,
    )
    back, along = apply(False, nbr, upper, window)
    out_shape = jax.ShapeDtypeStruct((sub, rows * width), F32)
    return talk(
        functools.partial(last_kernel, shards, groups),
        (out_shape, out_shape),
        [
            pltpu.VMEM((3, RING, rows, sub, width), BF16),
            pltpu.VMEM((RING, rows, sub, width), BF16),
            pltpu.VMEM((RING, sub, width), F32),
            pltpu.VMEM((sub, width), F32),
            pltpu.VMEM((messages, sub, width), F32),
        ]
        + pairs((messages,))
        + reduce_scratch(rows, sub, width),
        2,
        "last",
        flat(window),
        back,
        along,
        deg,
        deg_along,
        pass_rates,
    )


def solution(mesh):
    in_specs = (P(None, "rows"), P("rows", "cols", None, None), P("rows", "cols"))
    out_specs = (P("cols", "rows"), P("cols", "rows"))
    return jax.shard_map(per_device, mesh=mesh, in_specs=in_specs, out_specs=out_specs, check_vma=False)
```

```python
import functools

import jax
import jax.numpy as jnp
from jax import lax
from jax.experimental import pallas as pl
from jax.experimental.pallas import tpu as pltpu
from jax.sharding import PartitionSpec as P

MESH = pl.DeviceIdType.MESH
F32 = jnp.float32
BF16 = jnp.bfloat16
RING = 4
VMEM = pl.BlockSpec(memory_space=pltpu.VMEM)
MIB = 2**20
ONES = 16
UNROLL = 8
ROW_UNROLL = 128
TRAFFIC = {"halo": 60 * MIB, "middle": 150 * MIB, "last": 120 * MIB}
LIMITS = {"halo": 20 * MIB, "apply": 26 * MIB, "middle": 30 * MIB, "last": 32 * MIB}


def rem(value, count):
    return lax.rem(value, jnp.int32(count))


def loop(count, body, carry=0):
    unroll = max(n for n in range(1, UNROLL + 1) if count % n == 0)
    return lax.fori_loop(0, count, body, carry, unroll=unroll)


def nothing():
    pass


def low_of(count):
    return count * 5 // 16 * 2


class Place:
    def __init__(self, shards):
        self.shards = shards
        self.s = lax.axis_index("rows")
        self.y = lax.axis_index("cols")
        self.odd = rem(self.s, 2)
        self.next_y = rem(self.y + 1, RING)
        self.last_y = rem(self.y + RING - 1, RING)
        self.far_y = rem(self.y + 2, RING)
        self.partner = (self.s + 1 - 2 * self.odd, self.y)
        self.ahead = (rem(self.s + 2, shards), self.y)
        self.behind = (rem(self.s + shards - 2, shards), self.y)
        self.right = (self.s, self.next_y)
        self.left = (self.s, self.last_y)

    def around(self, stride, size, step):
        at = rem(self.s // stride, size)
        return (self.s + (rem(at + step, size) - at) * stride, self.y)


def signal_all(devices):
    barrier = pltpu.get_barrier_semaphore()
    for device in devices:
        pl.semaphore_signal(barrier, inc=1, device_id=device, device_id_type=MESH)


def wait_all(devices):
    pl.semaphore_wait(pltpu.get_barrier_semaphore(), len(devices))


def remote(src, dst, send_sem, recv_sem, device):
    return pltpu.make_async_remote_copy(
        src_ref=src, dst_ref=dst, send_sem=send_sem, recv_sem=recv_sem, device_id=device, device_id_type=MESH
    )


class Spread:
    def __init__(self, at, plane, first, count, send, recv):
        half = count // 2
        low, high = pl.ds(first, half), pl.ds(first + half, half)
        routes = (
            (at.y, low, at.right),
            (at.y, high, at.left),
            (at.y, high, at.right),
            (at.y, low, at.left),
            (at.last_y, low, at.right),
            (at.next_y, high, at.left),
        )
        self.copies = [
            remote(plane.at[chunk, part], plane.at[chunk, part], send.at[i], recv.at[i], device)
            for i, (chunk, part, device) in enumerate(routes)
        ]

    def start(self):
        for copy in self.copies[:4]:
            copy.start()

    def relay(self):
        for first, second in ((0, 4), (1, 5)):
            self.copies[first].wait_recv()
            self.copies[second].start()

    def near(self):
        for i in (2, 3):
            self.copies[i].wait_recv()

    def far(self):
        for i in (4, 5):
            self.copies[i].wait_recv()

    def drain(self):
        for copy in self.copies:
            copy.wait_send()


def gather(at, window, send, recv, low_send, low_recv, high_send, high_recv, c_send, c_recv):
    count = window.shape[2]
    split = low_of(count)
    low, high = pl.ds(0, split), pl.ds(split, count - split)
    order = (at.y, at.last_y, at.next_y, at.far_y)
    own_high = Spread(at, window.at[0], split, count - split, send.at[0], recv.at[0])
    next_low = Spread(at, window.at[2], 0, split, send.at[1], recv.at[1])
    own_low = Spread(at, window.at[0], 0, split, send.at[2], recv.at[2])
    x_low = remote(window.at[0, at.y, low], window.at[2, at.y, low], low_send, low_recv, at.behind)
    x_high = [
        remote(window.at[0, chunk, high], window.at[2, chunk, high], high_send.at[i], high_recv.at[i], at.behind)
        for i, chunk in enumerate(order)
    ]
    source = 2 - 2 * at.odd
    across = [
        [
            remote(
                window.at[source, chunk, part], window.at[1, chunk, part], c_send.at[k, i], c_recv.at[k, i], at.partner
            )
            for i, chunk in enumerate(order)
        ]
        for k, part in enumerate((low, high))
    ]
    own_high.start()
    x_high[0].start()
    yield
    x_low.start()
    own_high.relay()
    own_high.near()
    x_high[1].start()
    x_high[2].start()
    own_low.start()
    x_low.wait_recv()
    next_low.start()
    across[0][0].start()
    own_high.far()
    x_high[3].start()
    own_low.relay()
    next_low.relay()
    x_high[0].wait_recv()
    across[1][0].start()
    next_low.near()
    own_low.near()
    across[0][1].start()
    across[0][2].start()
    for i in (1, 2):
        x_high[i].wait_recv()
        across[1][i].start()
    next_low.far()
    own_low.far()
    across[0][3].start()
    x_high[3].wait_recv()
    across[1][3].start()
    for spread in (own_high, next_low, own_low):
        spread.drain()
    x_low.wait_send()
    for copy in x_high:
        copy.wait_send()
    for copy in across[0] + across[1]:
        copy.wait()
    yield


def halo_kernel(
    shards, p_hbm, u_hbm, window, u_ref, p_ref, p_sem, u_sem, send, recv, q_send, q_recv, d_send, d_recv, c_send, c_recv
):
    at = Place(shards)
    partners = (at.partner, at.ahead, at.behind, at.right, at.left)
    signal_all(partners)
    blocks, columns, width = window.shape[2:]
    order = (at.y, at.last_y, at.next_y, at.far_y)

    def span(chunk):
        return pl.ds(pl.multiple_of(chunk * (blocks * width), width), blocks * width)

    loads = [
        pltpu.make_async_copy(p_hbm.at[:, span(chunk)], p_ref.at[:, span(chunk)], p_sem.at[i])
        for i, chunk in enumerate(order)
    ]
    for load in loads:
        load.start()
    weights = pltpu.make_async_copy(u_hbm, u_ref, u_sem)

    def cast(index):
        chunk = order[index]
        loads[index].wait()

        def one(i, carry):
            first = pl.multiple_of((chunk * blocks + i) * width, width)
            window[0, chunk, i] = p_ref[:, pl.ds(first, width)].astype(BF16)
            return carry

        loop(blocks, one)

    split = low_of(blocks)
    piece = split // 2
    parts = [pl.ds(0, piece), pl.ds(piece, piece), pl.ds(split, blocks - split)]
    pieces = [
        remote(window.at[0, at.y, parts[k]], window.at[2, at.y, parts[k]], q_send.at[k], q_recv.at[k], at.behind)
        for k in range(2)
    ]
    direct = [
        remote(window.at[0, chunk, parts[2]], window.at[2, chunk, parts[2]], d_send.at[i], d_recv.at[i], at.behind)
        for i, chunk in enumerate(order)
    ]
    spreads = [Spread(at, window.at[2], k * piece, piece, send.at[k], recv.at[k]) for k in range(2)]
    source = 2 - 2 * at.odd
    across = [
        remote(window.at[source, chunk], window.at[1, chunk], c_send.at[i], c_recv.at[i], at.partner)
        for i, chunk in enumerate(order)
    ]
    cast(0)
    wait_all(partners)
    pieces[0].start()
    pieces[1].start()
    weights.start()
    for index in (1, 2, 3):
        cast(index)
    pieces[0].wait_recv()
    spreads[0].start()
    for copy in direct:
        copy.start()
    pieces[1].wait_recv()
    spreads[1].start()
    spreads[0].relay()
    direct[0].wait_recv()
    across[0].start()
    spreads[1].relay()
    for spread in spreads:
        spread.near()
    for i in (1, 2):
        direct[i].wait_recv()
        across[i].start()
    for spread in spreads:
        spread.far()
    direct[3].wait_recv()
    across[3].start()
    for spread in spreads:
        spread.drain()
    for copy in pieces + direct:
        copy.wait_send()
    for copy in across:
        copy.wait()
    weights.wait()


def pairs(*shapes):
    return [pltpu.SemaphoreType.DMA(shape) for shape in shapes for _ in range(2)]


HALO_SEMS = pairs((2, 6), (2,), (4,), (4,))
GATHER_SEMS = pairs((3, 6), (), (4,), (2, 4))
REDUCE_SEMS = pairs((4,), (3, 6), (4,), ())


def reduce_scratch(blocks, sub, width):
    return [
        pltpu.VMEM((RING, blocks, sub, width), BF16),
        pltpu.VMEM((2, RING, blocks, sub, width), BF16),
        pltpu.VMEM((3, 6, low_of(blocks) // 2, sub, width), BF16),
        pltpu.VMEM((RING, blocks - low_of(blocks), sub, width), BF16),
        pltpu.VMEM((low_of(blocks), sub, width), BF16),
        pltpu.VMEM((low_of(blocks), sub, width), BF16),
    ] + REDUCE_SEMS


class Fold:
    def __init__(self, at, plane, whole, landed, first, count, send, recv):
        self.at, self.plane, self.landed, self.first, self.half = at, plane, landed, first, count // 2
        low, high = pl.ds(first, self.half), pl.ds(first + self.half, self.half)
        routes = (
            (at.far_y, low, at.right),
            (at.far_y, high, at.left),
            (at.next_y, high, at.right),
            (at.last_y, low, at.left),
            (at.next_y, low, at.right),
            (at.last_y, high, at.left),
        )
        self.copies, self.soon = (
            [
                remote(source.at[chunk, part], landed.at[i, pl.ds(0, self.half)], send.at[i], recv.at[i], device)
                for i, (chunk, part, device) in enumerate(routes[:most])
            ]
            for source, most in ((plane, 6), (whole, 4 if whole is not None else 0))
        )

    def far(self):
        self.copies[0].start()
        self.copies[1].start()

    def next(self):
        self.copies[2].start()

    def last(self):
        self.copies[3].start()

    def begin(self):
        for copy in self.soon:
            copy.start()

    def relay(self):
        for slot, chunk, first in ((0, self.at.next_y, self.first), (1, self.at.last_y, self.first + self.half)):
            self.copies[slot].wait_recv()

            def one(i, carry, slot=slot, chunk=chunk, first=first):
                term = self.plane[chunk, first + i].astype(F32) + self.landed[slot, i].astype(F32)
                self.plane[chunk, first + i] = term.astype(BF16)
                return carry

            loop(self.half, one)
            self.copies[slot + 4].start()

    def result(self, take):
        for offset, slots in ((0, (3, 4)), (self.half, (2, 5))):
            for slot in slots:
                self.copies[slot].wait_recv()

            def one(i, carry, offset=offset, slots=slots):
                value = self.plane[self.at.y, self.first + offset + i].astype(F32)
                for slot in slots:
                    value += self.landed[slot, i].astype(F32)
                take(offset + i, value)
                return carry

            loop(self.half, one)

    def drain(self):
        for copy in self.copies:
            copy.wait_send()


def reduce(
    at, finish, late, beside,
    part, crossed, total, landed, behind, outgoing, incoming,
    c_send, c_recv, send, recv, h_send, h_recv, low_send, low_recv,
):
    count = crossed.shape[1]
    split = low_of(count)
    high = count - split
    order = (at.far_y, at.next_y, at.last_y, at.y)
    across = [
        remote(part.at[1, chunk], crossed.at[chunk], c_send.at[i], c_recv.at[i], at.partner)
        for i, chunk in enumerate(order)
    ]
    ahead_low = Fold(at, total.at[1], part.at[2], landed.at[0], 0, split, send.at[0], recv.at[0])
    own_low = Fold(at, total.at[0], part.at[0], landed.at[1], 0, split, send.at[1], recv.at[1])
    own_high = Fold(at, total.at[0], None, landed.at[2], split, high, send.at[2], recv.at[2])
    x_high, x_soon = (
        [
            remote(source.at[chunk, pl.ds(split, high)], behind.at[chunk], h_send.at[i], h_recv.at[i], at.ahead)
            for i, chunk in enumerate(order)
        ]
        for source in (total.at[1], part.at[2])
    )
    x_low = remote(outgoing, incoming, low_send, low_recv, at.ahead)
    for copy in across:
        copy.start()

    @pl.when(at.odd == 0)
    def _():
        own_low.begin()

    late()

    @pl.when(at.odd == 1)
    def _():
        ahead_low.begin()
        for copy in x_soon:
            copy.start()

    def combine(index):
        chunk = order[index]
        joined, kept = 1 - at.odd, at.odd
        across[index].wait_recv()

        def one(i, carry):
            term = part[2 * joined, chunk, i].astype(F32) + crossed[chunk, i].astype(F32)
            total[joined, chunk, i] = term.astype(BF16)
            total[kept, chunk, i] = part[2 * kept, chunk, i]
            return carry

        loop(count, one)

    def join(index):
        chunk = order[index]
        x_high[index].wait_recv()

        def one(i, carry):
            term = total[0, chunk, split + i].astype(F32) + behind[chunk, i].astype(F32)
            total[0, chunk, split + i] = term.astype(BF16)
            return carry

        loop(high, one)

    def send_on(i, value):
        outgoing[i] = value.astype(BF16)

    for index in range(4):
        combine(index)

        @pl.when(at.odd == 0)
        def _(index=index):
            if index < 3:
                (ahead_low.far, ahead_low.next, ahead_low.last)[index]()
            x_high[index].start()

        @pl.when(at.odd == 1)
        def _(index=index):
            if index < 3:
                (own_low.far, own_low.next, own_low.last)[index]()

        if index == 0:
            beside[0]()
    ahead_low.relay()
    own_low.relay()
    beside[1]()
    join(0)
    own_high.far()
    ahead_low.result(send_on)
    x_low.start()
    beside[2]()
    join(1)
    own_high.next()
    join(2)
    own_high.last()
    beside[3]()
    own_high.relay()
    join(3)
    beside[4]()
    own_high.result(lambda i, value: finish(split + i, 0.5 * value))
    beside[5]()
    x_low.wait_recv()
    own_low.result(lambda i, value: finish(i, 0.5 * (value + incoming[i].astype(F32))))

    def drain():
        for copy in across + x_high + [x_low]:
            copy.wait_send()
        for fold in (ahead_low, own_low, own_high):
            fold.drain()

    return drain


def terms(planes, x_ref, back, along, deg, deg_along, take, dots=None):
    rows, columns, width = along.shape
    for d in planes:

        def one(i, carry, d=d):
            at_i = d * rows + i
            weight, minus, x = deg[at_i], back[at_i], x_ref[at_i].astype(F32)
            if d == 0:
                weight += deg_along[i]
                minus += along[i]
            term = jnp.concatenate([weight] * (columns // 8), axis=0) * x - minus
            take(d, i, x, term)
            return carry if dots is None else carry + x * term

        total = loop(rows, one, 0 if dots is None else dots)
        dots = dots if dots is None else total
    return dots


def middle_kernel(shards, x_ref, back, along, deg, deg_along, window, part, *scratch):
    at = Place(shards)
    partners = (at.partner, at.ahead, at.behind, at.right, at.left)
    signal_all(partners)
    quarter = window.shape[2]

    def take(d, i, x, term):
        part[d, i // quarter, rem(i, quarter)] = term.astype(BF16)

    given = (x_ref, back, along, deg, deg_along, take)
    terms((1, 0), *given)
    wait_all(partners)

    def keep(i, value):
        window[0, at.y, i] = value.astype(BF16)

    count = 6 + len(REDUCE_SEMS)
    steps = gather(at, window, *scratch[count:])
    drain = reduce(at, keep, lambda: terms((2,), *given), [nothing] * 5 + [lambda: next(steps)], part, *scratch[:count])
    next(steps)
    drain()


def last_kernel(
    shards, groups, w_ref, back, along, deg, deg_along, p_ref, x_ref, r_ref,
    part, h_ref, hq_ref, sums, heard, s_send, s_recv, *scratch,
):
    at = Place(shards)
    opposite = (at.s, at.far_y)
    peers = [at.around(stride, size, step) for stride, size in groups for step in range(1, size)]
    partners = [at.partner, at.ahead, at.behind, at.right, at.left, opposite] + peers
    signal_all(partners)
    _, blocks, sub, width = h_ref.shape

    def take(d, i, x, term):
        for g in range(RING):
            part[d, g, i] = term[g * sub : (g + 1) * sub].astype(BF16)
            if d == 0:
                h_ref[g, i] = x[g * sub : (g + 1) * sub].astype(BF16)

    given = (w_ref, back, along, deg, deg_along, take)
    dots = terms((1, 0), *given, jnp.zeros((RING * sub, width), F32))
    wait_all(partners)
    zero = jnp.zeros((sub, width), F32)
    lanes = lax.broadcasted_iota(jnp.int32, (sub, width), 1)
    rounds = [[(hq_ref.at[y], at_y) for y, at_y in ((at.next_y, at.right), (at.last_y, at.left), (at.far_y, opposite))]]
    rounds += [[(sums, at.around(stride, size, step)) for step in range(1, size)] for stride, size in groups]
    messages = []
    for one_round in rounds:
        first = sum(map(len, messages))
        messages.append(
            [
                remote(source, heard.at[slot], s_send.at[slot], s_recv.at[slot], device)
                for slot, (source, device) in enumerate(one_round, first)
            ]
        )

    def tell(k):
        for message in messages[k]:
            message.start()

    def hear(k):
        for message in messages[k]:
            message.wait_recv()
        for message in messages[k]:
            message.wait_send()
        first = sum(map(len, messages[:k]))
        return sum((heard[slot] for slot in range(first, first + len(messages[k]))), zero)

    def p_of(i):
        return p_ref[pl.ds(pl.multiple_of(at.y * sub, sub), sub), pl.ds(pl.multiple_of(i * width, width), width)]

    def h_of(i):
        return h_ref[at.y, i].astype(F32)

    def square():
        def one(i, carry):
            p, h = p_of(i), h_of(i)
            return carry[0] + p * p, carry[1] + p * h, carry[2] + h * h

        packed = zero
        for k, value in enumerate(loop(blocks, one, (zero, zero, zero))):
            packed = jnp.where(lanes == k, jnp.sum(value, axis=1, keepdims=True), packed)
        sums[...] = packed

    def start_sums():
        value = jnp.sum(hear(0) + hq_ref[at.y], axis=1, keepdims=True)
        sums[...] = jnp.where(lanes == 3, value, sums[...])
        tell(1)

    def pass_sums():
        sums[...] = sums[...] + hear(1)
        tell(2)

    scale = []

    def end_sums():
        packed = sums[...] + hear(2)
        pp, ph, hh, hq = (
            jnp.broadcast_to(jnp.sum(jnp.where(lanes == k, packed, 0.0), axis=1, keepdims=True), (sub, width))
            for k in range(4)
        )
        first = pp / (pp + ph)
        rest = ph / (pp + ph)
        norm = rest * rest * pp - 2.0 * rest * first * ph + first * first * hh
        a = rest + norm / pp
        c = first
        curve = a * a * pp + a * (a - 2.0 * c) * ph + c * (c - 2.0 * a) * hh + c * c * hq
        second = norm / curve
        x_p, x_h = first + second * a, second * c
        scale.extend((rest - second * a, first + second * (a - c), second * c))

        def one(i, carry):
            x_ref[:, pl.ds(pl.multiple_of(i * width, width), width)] = x_p * p_of(i) - x_h * h_of(i)
            return carry

        loop(blocks, one)

    def keep(i, q):
        r_p, r_h, r_q = scale
        r_ref[:, pl.ds(pl.multiple_of(i * width, width), width)] = r_p * p_of(i) - r_h * h_of(i) + r_q * q

    def late():
        total = terms((2,), *given, dots)
        for g in range(RING):
            hq_ref[g] = 0.5 * total[g * sub : (g + 1) * sub]
        tell(0)

    drain = reduce(at, keep, late, [square, start_sums, pass_sums, nothing, end_sums, nothing], part, *scratch)
    drain()


def apply_kernel(first, nbr_ref, u_ref, x_ref, back, along, *weights):
    columns, width = x_ref.shape[1:]
    rows = u_ref.shape[0]
    base = lax.axis_index("rows") * rows
    if first:
        deg, deg_along = weights

    def clear(i, carry):
        back[i] = jnp.zeros((columns, width), F32)
        if first:
            deg[i] = jnp.zeros((8, width), F32)
        return carry

    loop(3 * rows, clear)
    ones = jnp.ones((ONES, 2 * width), BF16)

    def row(b, carry):
        t0, t1 = nbr_ref[0, b] - base, nbr_ref[1, b] - base
        pair = jnp.concatenate([u_ref[b, 0], u_ref[b, 1]], axis=1)
        own = x_ref[b]
        far = jnp.concatenate([x_ref[t0], x_ref[t1]], axis=1)
        if first:
            own = jnp.concatenate([own, ones[:, :width]], axis=0)
            far = jnp.concatenate([far, ones], axis=0)
        forward = lax.dot_general(far, pair, (((1,), (1,)), ((), ())), preferred_element_type=F32)
        returned = lax.dot_general(own, pair, (((1,), (0,)), ((), ())), preferred_element_type=F32)
        along[b] = forward[:columns]
        back[t0] += returned[:columns, :width]
        back[t1] += returned[:columns, width:]
        if first:
            deg_along[b] = forward[columns : columns + 8]
            deg[t0] += returned[columns : columns + 8, :width]
            deg[t1] += returned[columns : columns + 8, width:]
        return carry

    lax.fori_loop(0, rows, row, 0, unroll=min(ROW_UNROLL, rows))


def apply(first, nbr, upper, window):
    rows, slots, width, _ = upper.shape
    columns = window.shape[-2]
    out_shape = [
        jax.ShapeDtypeStruct((count, lines, width), F32)
        for lines in ((columns, 8) if first else (columns,))
        for count in (3 * rows, rows)
    ]
    return pl.pallas_call(
        functools.partial(apply_kernel, first),
        out_shape=out_shape,
        in_specs=[pl.BlockSpec(memory_space=pltpu.SMEM), VMEM, VMEM],
        out_specs=[VMEM] * len(out_shape),
        compiler_params=pltpu.CompilerParams(vmem_limit_bytes=LIMITS["apply"]),
        cost_estimate=pl.CostEstimate(
            flops=4 * rows * slots * width * width * columns, transcendentals=0, bytes_accessed=upper.size * 2
        ),
        name="apply_first" if first else "apply_second",
    )(nbr, upper, window.reshape(3 * rows, columns, width))


def talk(body, out_shape, scratch, collective_id, name, *args, in_specs=None):
    return pl.pallas_call(
        body,
        out_shape=out_shape,
        in_specs=in_specs or [VMEM] * len(args),
        out_specs=jax.tree.map(lambda _: VMEM, out_shape),
        scratch_shapes=scratch,
        compiler_params=pltpu.CompilerParams(
            collective_id=collective_id, has_side_effects=True, vmem_limit_bytes=LIMITS[name]
        ),
        cost_estimate=pl.CostEstimate(flops=0, transcendentals=0, bytes_accessed=TRAFFIC[name]),
        name=name,
    )(*args)


def per_device(pass_rates, upper_blocks, neighbours):
    rows, _, width, _ = upper_blocks.shape
    columns = pass_rates.shape[0]
    shards = lax.axis_size("rows")
    if lax.axis_size("cols") != RING or shards % 8:
        raise ValueError("mesh shape")
    quarter, sub = rows // RING, columns // RING
    groups = [(1, 8), (8, shards // 8)]
    messages = RING - 1 + sum(size - 1 for _, size in groups)
    nbr = neighbours.T
    window_shape = jax.ShapeDtypeStruct((3, RING, quarter, columns, width), BF16)

    window, upper = talk(
        functools.partial(halo_kernel, shards),
        (window_shape, jax.ShapeDtypeStruct(upper_blocks.shape, BF16)),
        [pltpu.VMEM(pass_rates.shape, F32), pltpu.SemaphoreType.DMA((RING,)), pltpu.SemaphoreType.DMA] + HALO_SEMS,
        0,
        "halo",
        pltpu.with_memory_space_constraint(pass_rates, pltpu.HBM),
        pltpu.with_memory_space_constraint(upper_blocks, pltpu.HBM),
        in_specs=[pl.BlockSpec(memory_space=pltpu.HBM)] * 2,
    )
    flat = lambda w: w.reshape(3 * rows, columns, width)
    back, along, deg, deg_along = apply(True, nbr, upper, window)
    window = talk(
        functools.partial(middle_kernel, shards),
        window_shape,
        [pltpu.VMEM(window_shape.shape, BF16)] + reduce_scratch(quarter, columns, width) + GATHER_SEMS,
        1,
        "middle",
        flat(window),
        back,
        along,
        deg,
        deg_along,
    )
    back, along = apply(False, nbr, upper, window)
    out_shape = jax.ShapeDtypeStruct((sub, rows * width), F32)
    return talk(
        functools.partial(last_kernel, shards, groups),
        (out_shape, out_shape),
        [
            pltpu.VMEM((3, RING, rows, sub, width), BF16),
            pltpu.VMEM((RING, rows, sub, width), BF16),
            pltpu.VMEM((RING, sub, width), F32),
            pltpu.VMEM((sub, width), F32),
            pltpu.VMEM((messages, sub, width), F32),
        ]
        + pairs((messages,))
        + reduce_scratch(rows, sub, width),
        2,
        "last",
        flat(window),
        back,
        along,
        deg,
        deg_along,
        pass_rates,
    )


def solution(mesh):
    in_specs = (P(None, "rows"), P("rows", "cols", None, None), P("rows", "cols"))
    out_specs = (P("cols", "rows"), P("cols", "rows"))
    return jax.shard_map(per_device, mesh=mesh, in_specs=in_specs, out_specs=out_specs, check_vma=False)
```
